32 devices in a mesh: sky: 8 (over z, y), band: 4 (over x, core).
Axes of the slice: x: 2, y: 2, z: 4, core: 2. Of those that a mesh axis runs over, the one named last changes fastest.
Arguments:
- exposures: bfloat16 [8, 4, 1024, 1024], P('sky', 'band'), may hold values from -6 to 6
- inv_variance: bfloat16 [8, 4, 1024, 1024], P('sky', 'band'), may hold values from 0.25 to 4
- mask_planes: int32 [8, 4, 2, 35], P('sky', 'band'), may hold values from 0 to 1073741823, as said below
- sky_columns: int32 [8, 4, 8], replicated, may hold values from 0 to 7, as said below
- basis_rows: float32 [9, 25], replicated, may hold values from -1 to 1
- basis_cols: float32 [9, 25], replicated, may hold values from -1 to 1
- match_coeffs: float32 [8, 4, 9], P('sky', 'band'), may hold values from -2 to 2
- detect_taps: float32 [4, 31], P('band'), may hold values from 0.05 to 0.3
Outputs:
- difference: bfloat16 [8, 4, 1024, 1024], P('sky', 'band')
- detection: float32 [1024, 1024], P('band', 'sky')
The draws below stay inside these ranges and needn't reach their ends.
Inputs may be any that keep to these rules, and one draw needn't show every extreme that they name: Each row sky_columns[e, b] holds 8 consecutive sky tile columns in order, counted modulo 8; every sky tile column is covered by some exposure of every band. Bit j of mask_planes[e, b, 0, w] marks pixel column 30 w + j of that exposure as bad and bit j of mask_planes[e, b, 1, w] pixel row 30 w + j; bits past 1024 are ignored. In every draw some word has all 30 bits set.
All inputs are finite; a program needn't handle non-finite values.
Results may differ from the reference program's by a relative error of at most 0.0095.
Values may be sent and summed in bfloat16 or wider, within the bound.
No kernel may reach another device: no remote copies, remote signals or barrier semaphores. Data moves between devices by JAX's collectives and lax.ppermute only.
A program may use at most 128 MiB of HBM per device.

```python
import math
import jax
import jax.numpy as jnp
from jax import lax

IMG = 1024
TILE = 128
NB = 9
TAPS = 25
DTAPS = 31
ET = 8
SKYCOLS = 8
EXPOSURES = 8
BANDS = 4
NWORD = 35


def draw_mask_planes(key, part):
    flags = jax.random.randint(jax.random.fold_in(key, 11), (EXPOSURES, BANDS, 2, NWORD, 30), 0, 12)
    bit_values = (flags == 0).astype(jnp.int32)
    powers = jnp.left_shift(jnp.ones((30,), jnp.int32), jnp.arange(30, dtype=jnp.int32))
    words = jnp.sum(bit_values * powers, axis=-1).astype(jnp.int32)
    word_total = EXPOSURES * BANDS * 2 * NWORD
    full_place = jax.random.randint(jax.random.fold_in(key, 13), (), 0, word_total)
    places = jnp.arange(word_total, dtype=jnp.int32).reshape(EXPOSURES, BANDS, 2, NWORD)
    all_bits = jnp.full((EXPOSURES, BANDS, 2, NWORD), 1073741823, jnp.int32)
    return jnp.where(places == full_place, all_bits, words).astype(jnp.int32)


def draw_sky_columns(key, part):
    key_start, key_deep, key_pick, key_spread, key_any = jax.random.split(jax.random.fold_in(key, 7), 5)
    column_total = SKYCOLS
    exposure_ids = jnp.arange(EXPOSURES, dtype=jnp.int32)[:, None]
    start_column = jax.random.randint(key_start, (1, BANDS), 0, column_total)
    deep_column = jax.random.randint(key_deep, (1, BANDS), 0, column_total)
    covering = (start_column + exposure_ids * ET) % column_total
    clustered = (deep_column + jax.random.randint(key_spread, (EXPOSURES, BANDS), 0, ET // 2 + 1)) % column_total
    anywhere = jax.random.randint(key_any, (EXPOSURES, BANDS), 0, column_total)
    choose_deep = jax.random.randint(key_pick, (EXPOSURES, BANDS), 0, 2) == 0
    offsets = jnp.where(choose_deep, clustered, anywhere)
    cover_count = (column_total + ET - 1) // ET
    offsets = jnp.where(exposure_ids < cover_count, covering, offsets)
    return ((offsets[:, :, None] + jnp.arange(ET, dtype=jnp.int32)[None, None, :]) % column_total).astype(jnp.int32)


def block_levels(key, extent, shards, smallest, largest):
    level = 1.0
    for dim, parts in shards:
        steps = jax.random.uniform(jax.random.fold_in(jax.random.fold_in(key, 6), dim), (parts,), jnp.float32, smallest / len(shards), largest / len(shards))
        level = level * jnp.repeat(jnp.exp(steps), extent[dim] // parts).reshape((-1,) + (1,) * (len(extent) - 1 - dim))
    return level


def normal_values(stream_key, shape, spread, reach, shards=(), kind=jnp.bfloat16):
    values = spread * jax.random.normal(stream_key, shape, jnp.float32)
    if shards:
        values = values * block_levels(stream_key, shape, shards, -0.22, 0.18)
    return jnp.clip(values, -reach, reach).astype(kind)


def setup_inputs(seed: int = 0) -> dict:
    streams_of = jax.random.split(jax.random.key(seed), 9)
    return {
        "exposures": normal_values(streams_of[0], (EXPOSURES, BANDS, IMG, IMG), 1.0, 6.0, ((0, 8), (1, 4))),
        "inv_variance": jnp.clip(jnp.exp(math.log(4.0) - 2.7725887 * jax.random.uniform(streams_of[1], (EXPOSURES, BANDS, IMG, IMG), jnp.float32) ** block_levels(streams_of[1], (EXPOSURES, BANDS, IMG, IMG), ((0, 8), (1, 4)), -0.2, 0.2)), 0.25, 4.0).astype(jnp.bfloat16),
        "mask_planes": draw_mask_planes(jax.random.fold_in(streams_of[8], 71), 0),
        "sky_columns": draw_sky_columns(jax.random.fold_in(streams_of[8], 71), 0),
        "basis_rows": normal_values(streams_of[4], (NB, TAPS), 0.2, 1.0, (), jnp.float32),
        "basis_cols": normal_values(streams_of[5], (NB, TAPS), 0.2, 1.0, (), jnp.float32),
        "match_coeffs": normal_values(streams_of[6], (EXPOSURES, BANDS, NB), 0.35, 2.0, ((0, 8), (1, 4)), jnp.float32),
        "detect_taps": jnp.clip(0.05 + 0.25 * jax.random.uniform(streams_of[7], (BANDS, DTAPS), jnp.float32) ** block_levels(streams_of[7], (BANDS, DTAPS), ((0, 4),), -0.2, 0.2), 0.05, 0.3),
    }


def rounded(values):
    return lax.optimization_barrier(values.astype(jnp.bfloat16))


def band_matrix(tap_rows, window_width):
    offsets = jnp.arange(window_width, dtype=jnp.int32)[:, None] - jnp.arange(TILE, dtype=jnp.int32)[None, :]
    selector = (offsets[:, :, None] == jnp.arange(tap_rows.shape[1], dtype=jnp.int32)[None, None, :]).astype(jnp.float32)
    return jnp.einsum("wtl,kl->kwt", selector, tap_rows.astype(jnp.float32), precision=lax.Precision.HIGHEST).astype(jnp.bfloat16)


def keep_pixels(planes, side_length):
    places = jnp.arange(side_length, dtype=jnp.int32)
    column_bits = jnp.bitwise_and(jnp.right_shift(planes[0][places // 30], places % 30), 1)
    row_bits = jnp.bitwise_and(jnp.right_shift(planes[1][places // 30], places % 30), 1)
    return jnp.logical_and(row_bits[:, None] == 0, column_bits[None, :] == 0)


def psf_match(picture, column_taps, row_taps):
    side_length = picture.shape[1]
    block_count = side_length // TILE
    margin = TAPS // 2
    width_full = TILE + 2 * margin
    padded = jnp.pad(picture, ((0, 0), (margin, margin)))
    blocks = jnp.stack([padded[:, TILE * block_index: TILE * block_index + width_full] for block_index in range(block_count)], 0)
    column_band = band_matrix(column_taps, width_full)
    column_pass = rounded(jnp.einsum("jyw,kwt->kyjt", blocks.astype(jnp.float32), column_band.astype(jnp.float32)).reshape(NB, side_length, side_length))
    row_padded = jnp.pad(column_pass, ((0, 0), (margin, margin), (0, 0)))
    row_blocks = jnp.stack([row_padded[:, TILE * block_index: TILE * block_index + width_full, :] for block_index in range(block_count)], 0)
    row_band = band_matrix(row_taps, width_full)
    summed = jnp.einsum("ikwx,kwt->itx", row_blocks.astype(jnp.float32), row_band.astype(jnp.float32))
    return summed.reshape(side_length, side_length).astype(jnp.bfloat16)


def reference(exposures, inv_variance, mask_planes, sky_columns, basis_rows, basis_cols, match_coeffs, detect_taps):
    row_taps = basis_rows.astype(jnp.bfloat16)
    count_all = EXPOSURES * BANDS

    def match_one(inputs):
        picture, variance_inv, planes, coeffs = inputs
        column_taps = (coeffs[:, None] * basis_cols).astype(jnp.bfloat16)
        matched_one = psf_match(picture, column_taps, row_taps)
        keep = keep_pixels(planes, picture.shape[0])
        weight_one = jnp.where(keep, variance_inv, jnp.zeros_like(variance_inv))
        return matched_one, weight_one

    matched, weight = lax.map(match_one, (exposures.reshape(count_all, IMG, IMG), inv_variance.reshape(count_all, IMG, IMG), mask_planes.reshape(count_all, 2, NWORD), match_coeffs.reshape(count_all, NB)))
    matched = matched.reshape(EXPOSURES, BANDS, IMG, ET, TILE).astype(jnp.float32)
    weight = weight.reshape(EXPOSURES, BANDS, IMG, ET, TILE).astype(jnp.float32)
    placer = (sky_columns[:, :, :, None] == jnp.arange(SKYCOLS, dtype=jnp.int32)[None, None, None, :]).astype(jnp.float32)
    numer = jnp.einsum("ebyct,ebcs->byst", weight * matched, placer, precision=lax.Precision.HIGHEST)
    denom = jnp.einsum("ebyct,ebcs->byst", weight, placer, precision=lax.Precision.HIGHEST)
    template = rounded(numer / jnp.maximum(denom, 1.0)).astype(jnp.float32)
    picked = jnp.einsum("byst,ebcs->ebyct", template, placer, precision=lax.Precision.HIGHEST)
    difference = (matched - picked).astype(jnp.bfloat16).reshape(EXPOSURES, BANDS, IMG, IMG)
    sky_image = template.reshape(BANDS, IMG, SKYCOLS * TILE)
    taps = detect_taps.astype(jnp.bfloat16).astype(jnp.float32)
    margin = DTAPS // 2
    smoothed = jnp.zeros_like(sky_image)
    for offset in range(DTAPS):
        smoothed = smoothed + taps[:, offset][:, None, None] * jnp.roll(sky_image, margin - offset, axis=2)
    smoothed = rounded(smoothed).astype(jnp.float32)
    padded = jnp.pad(smoothed, ((0, 0), (margin, margin), (0, 0)))
    filtered = jnp.zeros_like(smoothed)
    for offset in range(DTAPS):
        filtered = filtered + taps[:, offset][:, None, None] * padded[:, offset: offset + IMG, :]
    detection = jnp.sum(filtered * filtered, axis=0)
    return difference, detection
```

```python
import functools

import jax
import jax.numpy as jnp
from jax import lax
from jax.experimental import pallas as pl
from jax.experimental.pallas import tpu as pltpu
from jax.sharding import PartitionSpec as P

TILE = 128
NB = 9
TAPS = 25
DTAPS = 31
BITS = 30
EDGE = 16
WINDOW = TILE + 2 * EDGE
SHIFT = TILE // 2
CHUNKS = 2
F32 = jnp.float32
BF16 = jnp.bfloat16


def toeplitz(base_row, rows):
    wide = jnp.broadcast_to(base_row, (rows, base_row.shape[1]))
    return pltpu.roll(wide, 0, 1, stride=1, stride_axis=0)


def prepare_kernel(base_ref, column_ref, row_ref, across_ref, down_ref):
    for k in range(NB):
        column_ref[:, k * TILE : (k + 1) * TILE] = toeplitz(base_ref[k : k + 1, :], TILE).T.astype(BF16)
        row_ref[:, k * WINDOW : (k + 1) * WINDOW] = toeplitz(base_ref[NB + k : NB + k + 1, :], TILE)[
            :, :WINDOW
        ].astype(BF16)
    across_ref[...] = toeplitz(base_ref[2 * NB : 2 * NB + 1, :], TILE).T.astype(BF16)
    down_ref[...] = toeplitz(base_ref[2 * NB + 1 : 2 * NB + 2, :], TILE)[:, :WINDOW].astype(BF16)


def place_left(taps, offset):
    return jnp.pad(taps, ((0, 0), (offset, 2 * TILE - offset - taps.shape[1])))


def prepare(match_coeffs, basis_cols, basis_rows, detect_taps):
    column_taps = (match_coeffs[:, None] * basis_cols).astype(BF16).astype(F32)
    row_taps = basis_rows.astype(BF16).astype(F32)
    taps = detect_taps.astype(BF16).astype(F32)
    base = jnp.concatenate(
        [
            place_left(column_taps, SHIFT - TAPS // 2),
            place_left(row_taps, EDGE - TAPS // 2),
            place_left(taps, SHIFT - DTAPS // 2),
            place_left(taps, EDGE - DTAPS // 2),
        ],
        0,
    )
    return pl.pallas_call(
        prepare_kernel,
        out_shape=(
            jax.ShapeDtypeStruct((2 * TILE, NB * TILE), BF16),
            jax.ShapeDtypeStruct((TILE, NB * WINDOW), BF16),
            jax.ShapeDtypeStruct((2 * TILE, TILE), BF16),
            jax.ShapeDtypeStruct((TILE, WINDOW), BF16),
        ),
        name="prepare",
    )(base)


def bad_bits(words_ref, plane, first_word, count, places):
    bad = jnp.zeros(places.shape, jnp.int32)
    last = words_ref.shape[1] - 1
    for step in range(count):
        index = first_word + step
        word = words_ref[plane, jnp.minimum(index, last)]
        away = places - index * BITS
        inside = jnp.logical_and(away >= 0, away < BITS)
        bits = jnp.bitwise_and(jnp.right_shift(jnp.full(places.shape, word), jnp.clip(away, 0, BITS - 1)), 1)
        bad = jnp.where(inside, bits, bad)
    return bad


def weight_kernel(sky_count, meta_ref, words_ref, variance_ref, weight_ref):
    rows, side = variance_ref.shape
    first_row = (meta_ref[0] + pl.program_id(0)) * rows
    lanes = lax.broadcasted_iota(jnp.int32, (8, side), 1)
    column_bad = bad_bits(words_ref, 0, 0, words_ref.shape[1], lanes)[0:1, :]
    places = first_row + lax.broadcasted_iota(jnp.int32, (rows, TILE), 0)
    row_bad = bad_bits(words_ref, 1, first_row // BITS, rows // BITS + 2, places)
    if sky_count * TILE != side:
        weight_ref[...] = jnp.zeros_like(weight_ref)
    for tile in range(side // TILE):
        window = slice(tile * TILE, (tile + 1) * TILE)
        bad = row_bad + column_bad[:, window]
        kept = jnp.where(bad == 0, variance_ref[:, window].astype(F32), 0.0)
        target = lax.rem(meta_ref[1] + tile, sky_count) * TILE
        weight_ref[:, pl.ds(pl.multiple_of(target, TILE), TILE)] = kept.astype(BF16)


def weigh(inv_variance, words, half, start, half_rows, sky_count):
    side = inv_variance.shape[0]
    rows = min(256, half_rows)
    meta = jnp.stack([half * (half_rows // rows), start])
    return pl.pallas_call(
        functools.partial(weight_kernel, sky_count),
        out_shape=jax.ShapeDtypeStruct((half_rows, sky_count * TILE), BF16),
        grid_spec=pltpu.PrefetchScalarGridSpec(
            num_scalar_prefetch=2,
            grid=(half_rows // rows,),
            in_specs=[pl.BlockSpec((rows, side), lambda i, m, w: (m[0] + i, 0))],
            out_specs=pl.BlockSpec((rows, sky_count * TILE), lambda i, m, w: (i, 0)),
        ),
        cost_estimate=pl.CostEstimate(flops=half_rows * side * 8, bytes_accessed=half_rows * side * 4, transcendentals=0),
        name="weigh",
    )(meta, words, inv_variance)


def match_kernel(sky_count, meta_ref, picture_ref, column_ref, row_ref, weight_ref, matched_ref, product_ref, wide, stacked):
    side = picture_ref.shape[0]
    block = meta_ref[0] + pl.program_id(0)
    last_block = side // TILE - 1
    first = pl.multiple_of(block * TILE, TILE)
    nothing = jnp.zeros((TILE, SHIFT), BF16)

    def spread(values):
        edge = nothing[: values.shape[0]]
        return jnp.concatenate([edge, values, edge], axis=1)

    above = picture_ref[pl.ds(pl.multiple_of(jnp.maximum(first - EDGE, 0), EDGE), EDGE), :]
    below = picture_ref[pl.ds(pl.multiple_of(jnp.minimum(first + TILE, side - EDGE), EDGE), EDGE), :]
    wide[0:EDGE, :] = spread(jnp.where(block > 0, above, jnp.zeros_like(above)))
    wide[EDGE : EDGE + TILE, :] = spread(picture_ref[pl.ds(first, TILE), :])
    wide[EDGE + TILE :, :] = spread(jnp.where(block < last_block, below, jnp.zeros_like(below)))
    if sky_count * TILE != side:
        product_ref[...] = jnp.zeros_like(product_ref)
    for pair in range(side // (2 * TILE)):
        for part in range(2):
            tile = 2 * pair + part
            passed = jnp.dot(
                wide[:, tile * TILE : (tile + 2) * TILE], column_ref[...], preferred_element_type=F32
            ).astype(BF16)
            for k in range(NB):
                stacked[k * WINDOW : (k + 1) * WINDOW, part * TILE : (part + 1) * TILE] = passed[
                    :, k * TILE : (k + 1) * TILE
                ]
        summed = jnp.dot(row_ref[...], stacked[...], preferred_element_type=F32).astype(BF16)
        matched_ref[:, pair * 2 * TILE : (pair + 1) * 2 * TILE] = summed
        for part in range(2):
            target = pl.multiple_of(lax.rem(meta_ref[1] + 2 * pair + part, sky_count) * TILE, TILE)
            weight = weight_ref[:, pl.ds(target, TILE)].astype(F32)
            product = weight * summed[:, part * TILE : (part + 1) * TILE].astype(F32)
            product_ref[:, pl.ds(target, TILE)] = product.astype(BF16)


def match(picture, column_band, row_band, weight, half, chunk, start, half_rows, sky_count):
    side = picture.shape[0]
    chunk_rows = half_rows // CHUNKS
    steps = chunk_rows // TILE
    meta = jnp.stack([(half * CHUNKS + chunk) * steps, start])
    stripe = sky_count * TILE
    return pl.pallas_call(
        functools.partial(match_kernel, sky_count),
        out_shape=(
            jax.ShapeDtypeStruct((chunk_rows, side), BF16),
            jax.ShapeDtypeStruct((chunk_rows, stripe), BF16),
        ),
        grid_spec=pltpu.PrefetchScalarGridSpec(
            num_scalar_prefetch=1,
            grid=(steps,),
            in_specs=[
                pl.BlockSpec((side, side), lambda i, m: (0, 0)),
                pl.BlockSpec(column_band.shape, lambda i, m: (0, 0)),
                pl.BlockSpec(row_band.shape, lambda i, m: (0, 0)),
                pl.BlockSpec((TILE, stripe), lambda i, m: (chunk * steps + i, 0)),
            ],
            out_specs=(
                pl.BlockSpec((TILE, side), lambda i, m: (i, 0)),
                pl.BlockSpec((TILE, stripe), lambda i, m: (i, 0)),
            ),
            scratch_shapes=[
                pltpu.VMEM((WINDOW, side + TILE), BF16),
                pltpu.VMEM((NB * WINDOW, 2 * TILE), BF16),
            ],
        ),
        cost_estimate=pl.CostEstimate(
            flops=2 * chunk_rows * side * NB * (2 * TILE + WINDOW), bytes_accessed=chunk_rows * side * 8, transcendentals=0
        ),
        name="match",
    )(meta, picture, column_band, row_band, weight)


def difference_kernel(sky_count, meta_ref, matched_ref, template_ref, out_ref):
    for tile in range(matched_ref.shape[1] // TILE):
        window = slice(tile * TILE, (tile + 1) * TILE)
        source = pl.multiple_of(lax.rem(meta_ref[0] + tile, sky_count) * TILE, TILE)
        picked = template_ref[:, pl.ds(source, TILE)].astype(F32)
        out_ref[:, window] = (matched_ref[:, window].astype(F32) - picked).astype(BF16)


def subtract(matched, template, start, sky_count):
    side = matched.shape[1]
    rows = min(256, side)
    stripe = sky_count * TILE
    return pl.pallas_call(
        functools.partial(difference_kernel, sky_count),
        out_shape=jax.ShapeDtypeStruct((side, side), BF16),
        grid_spec=pltpu.PrefetchScalarGridSpec(
            num_scalar_prefetch=1,
            grid=(side // rows,),
            in_specs=[
                pl.BlockSpec((rows, side), lambda i, m: (i, 0)),
                pl.BlockSpec((rows, stripe), lambda i, m: (i, 0)),
            ],
            out_specs=pl.BlockSpec((rows, side), lambda i, m: (i, 0)),
        ),
        cost_estimate=pl.CostEstimate(flops=side * side, bytes_accessed=side * side * 6, transcendentals=0),
        name="subtract",
    )(start[None], matched, template)


def detect_kernel(sky_count, band_count, meta_ref, left_ref, own_ref, right_ref, across_ref, down_ref, *refs):
    powers, smoothed = refs[:band_count], refs[band_count]
    side = own_ref.shape[0]
    rows = side // band_count
    smoothed[0:EDGE, :] = jnp.zeros((EDGE, TILE), BF16)
    smoothed[EDGE + side :, :] = jnp.zeros((EDGE, TILE), BF16)
    window = jnp.concatenate([left_ref[:, SHIFT:], own_ref[...], right_ref[:, :SHIFT]], axis=1)
    smoothed[EDGE : EDGE + side, :] = jnp.dot(window, across_ref[...], preferred_element_type=F32).astype(BF16)
    for step in range(band_count):
        first = lax.rem(meta_ref[1] + step, band_count) * rows
        for inner in range(rows // TILE):
            source = pl.multiple_of(first + inner * TILE, TILE)
            filtered = jnp.dot(down_ref[...], smoothed[pl.ds(source, WINDOW), :], preferred_element_type=F32)
            powers[step][inner * TILE : (inner + 1) * TILE, :] = filtered * filtered


def detect(template, across_band, down_band, own_sky, own_band, sky_count, band_count):
    side = template.shape[0]
    meta = jnp.stack([own_sky, own_band])
    columns = [
        pl.BlockSpec((side, TILE), lambda i, m, d=d: (0, lax.rem(m[0] + d, sky_count)))
        for d in (sky_count - 1, 0, 1)
    ]
    return pl.pallas_call(
        functools.partial(detect_kernel, sky_count, band_count),
        out_shape=[jax.ShapeDtypeStruct((side // band_count, TILE), F32)] * band_count,
        grid_spec=pltpu.PrefetchScalarGridSpec(
            num_scalar_prefetch=1,
            grid=(1,),
            in_specs=columns
            + [
                pl.BlockSpec(across_band.shape, lambda i, m: (0, 0)),
                pl.BlockSpec(down_band.shape, lambda i, m: (0, 0)),
            ],
            out_specs=[pl.BlockSpec((side // band_count, TILE), lambda i, m: (0, 0))] * band_count,
            scratch_shapes=[pltpu.VMEM((side + 2 * EDGE, TILE), BF16)],
        ),
        cost_estimate=pl.CostEstimate(flops=side * TILE * 800, bytes_accessed=side * TILE * 16, transcendentals=0),
        name="detect",
    )(meta, template, template, template, across_band, down_band)


def body(exposures, inv_variance, mask_planes, sky_columns, basis_rows, basis_cols, match_coeffs, detect_taps):
    picture = exposures[0, 0]
    side = picture.shape[0]
    sky_count = lax.axis_size("sky")
    band_count = lax.axis_size("band")
    own_sky = lax.axis_index("sky")
    own_band = lax.axis_index("band")
    pair = 2 if sky_count % 2 == 0 else 1
    line = sky_count // pair
    low = lax.rem(own_sky, pair)
    high = own_sky // pair
    half_rows = side // pair
    chunk_rows = half_rows // CHUNKS
    part_rows = chunk_rows // line
    stripe = sky_count * TILE
    start = sky_columns[own_sky, own_band, 0]
    swap = [(i, i ^ 1) for i in range(sky_count)]

    def shift_line(step):
        return [(i, (i // pair + step) % line * pair + i % pair) for i in range(sky_count)]

    def part_of(block, step):
        return lax.dynamic_slice_in_dim(block, lax.rem(high + step, line) * part_rows, part_rows, 0)

    def reduce_line(mine, theirs):
        def total(step):
            block = part_of(mine, step).astype(F32)
            return block if theirs is None else block + part_of(theirs, step).astype(F32)

        arrived = [lax.ppermute(total(step).astype(BF16), "sky", shift_line(step)) for step in range(1, line)]
        result = total(0)
        for block in arrived:
            result = result + block.astype(F32)
        return result

    def exchange(block):
        return lax.ppermute(block, "sky", swap)

    def chunk_of(block, chunk):
        return None if block is None else block[chunk * chunk_rows : (chunk + 1) * chunk_rows]

    words = mask_planes[0, 0]
    other = pair - 1 - low
    weight_other = weigh(inv_variance[0, 0], words, other, start, half_rows, sky_count)
    weight_in = [exchange(chunk_of(weight_other, c)) if pair == 2 else None for c in range(CHUNKS)]
    weight_own = weight_other if pair == 1 else weigh(inv_variance[0, 0], words, low, start, half_rows, sky_count)
    column_band, row_band, across_band, down_band = prepare(
        match_coeffs[0, 0], basis_cols, basis_rows, detect_taps
    )

    def matching(weight, half, chunk):
        return match(picture, column_band, row_band, weight, half, chunk, start, half_rows, sky_count)

    away, product_in = [None] * CHUNKS, [None] * CHUNKS
    if pair == 2:
        for c in range(CHUNKS):
            away[c], product = matching(weight_other, other, c)
            product_in[c] = exchange(product)
    home, product_own = zip(*[matching(weight_own, low, c) for c in range(CHUNKS)])

    template = jnp.zeros((side, stripe), BF16)
    matched = jnp.zeros((side, side), BF16)
    for c in range(CHUNKS):
        denom = reduce_line(chunk_of(weight_own, c), weight_in[c])
        numer = reduce_line(product_own[c], product_in[c])
        block = (numer / jnp.maximum(denom, 1.0)).astype(BF16)
        near = [block] + [lax.ppermute(block, "sky", shift_line(step)) for step in range(1, line)]
        for step, piece in enumerate(near):
            place = c * chunk_rows + lax.rem(high + line - step, line) * part_rows
            template = lax.dynamic_update_slice(template, piece, (low * half_rows + place, 0))
            if pair == 2:
                template = lax.dynamic_update_slice(template, exchange(piece), (other * half_rows + place, 0))
        matched = lax.dynamic_update_slice(matched, home[c], (low * half_rows + c * chunk_rows, 0))
        if pair == 2:
            matched = lax.dynamic_update_slice(matched, away[c], (other * half_rows + c * chunk_rows, 0))

    powers = detect(template, across_band, down_band, own_sky, own_band, sky_count, band_count)
    detection = powers[0]
    for step in range(1, band_count):
        ring = [(i, (i + step) % band_count) for i in range(band_count)]
        detection = detection + lax.ppermute(powers[step], "band", ring)
    difference = subtract(matched, template, start, sky_count)
    return (difference[None, None], detection)


def solution(mesh):
    in_specs = (
        P("sky", "band", None, None),
        P("sky", "band", None, None),
        P("sky", "band", None, None),
        P(),
        P(),
        P(),
        P("sky", "band", None),
        P("band", None),
    )
    out_specs = (P("sky", "band", None, None), P("band", "sky"))
    return jax.shard_map(body, mesh=mesh, in_specs=in_specs, out_specs=out_specs, check_vma=False)
```

```python
import functools

import jax
import jax.numpy as jnp
from jax import lax
from jax.experimental import pallas as pl
from jax.experimental.pallas import tpu as pltpu
from jax.sharding import PartitionSpec as P

TILE = 128
NB = 9
TAPS = 25
DTAPS = 31
BITS = 30
EDGE = 16
WINDOW = TILE + 2 * EDGE
SHIFT = TILE // 2
CHUNKS = 2
START, OWN, OTHER, LINE, SKY, BAND = range(6)
F32 = jnp.float32
BF16 = jnp.bfloat16


def toeplitz(base_row, rows):
    wide = jnp.broadcast_to(base_row, (rows, base_row.shape[1]))
    return pltpu.roll(wide, 0, 1, stride=1, stride_axis=0)


def prepare_kernel(base_ref, column_ref, row_ref, across_ref, down_ref):
    for k in range(NB):
        column_ref[:, k * TILE : (k + 1) * TILE] = toeplitz(base_ref[k : k + 1, :], TILE).T.astype(BF16)
        row_ref[:, k * WINDOW : (k + 1) * WINDOW] = toeplitz(base_ref[NB + k : NB + k + 1, :], TILE)[
            :, :WINDOW
        ].astype(BF16)
    across_ref[...] = toeplitz(base_ref[2 * NB : 2 * NB + 1, :], TILE).T.astype(BF16)
    down_ref[...] = toeplitz(base_ref[2 * NB + 1 : 2 * NB + 2, :], TILE)[:, :WINDOW].astype(BF16)


def place_left(taps, offset):
    return jnp.pad(taps, ((0, 0), (offset, 2 * TILE - offset - taps.shape[1])))


def prepare(match_coeffs, basis_cols, basis_rows, detect_taps):
    column_taps = (match_coeffs[:, None] * basis_cols).astype(BF16).astype(F32)
    row_taps = basis_rows.astype(BF16).astype(F32)
    taps = detect_taps.astype(BF16).astype(F32)
    base = jnp.concatenate(
        [
            place_left(column_taps, SHIFT - TAPS // 2),
            place_left(row_taps, EDGE - TAPS // 2),
            place_left(taps, SHIFT - DTAPS // 2),
            place_left(taps, EDGE - DTAPS // 2),
        ],
        0,
    )
    return pl.pallas_call(
        prepare_kernel,
        out_shape=(
            jax.ShapeDtypeStruct((2 * TILE, NB * TILE), BF16),
            jax.ShapeDtypeStruct((TILE, NB * WINDOW), BF16),
            jax.ShapeDtypeStruct((2 * TILE, TILE), BF16),
            jax.ShapeDtypeStruct((TILE, WINDOW), BF16),
        ),
        name="prepare",
    )(base)


def bad_bits(words_ref, plane, first_word, count, places):
    last = words_ref.shape[1] - 1
    word = jnp.full(places.shape, words_ref[plane, jnp.minimum(first_word, last)])
    begin = jnp.full(places.shape, first_word * BITS)
    for step in range(1, count):
        index = first_word + step
        reached = places >= index * BITS
        word = jnp.where(reached, words_ref[plane, jnp.minimum(index, last)], word)
        begin = jnp.where(reached, index * BITS, begin)
    return jnp.bitwise_and(jnp.right_shift(word, places - begin), 1)


def weight_kernel(sky_count, half_slot, half_blocks, meta_ref, words_ref, variance_ref, weight_ref):
    rows, side = variance_ref.shape
    first_row = (meta_ref[half_slot] * half_blocks + pl.program_id(0)) * rows
    lanes = lax.broadcasted_iota(jnp.int32, (8, side), 1)
    column_bad = bad_bits(words_ref, 0, 0, words_ref.shape[1], lanes)[0:1, :]
    places = first_row + lax.broadcasted_iota(jnp.int32, (rows, TILE), 0)
    row_bad = bad_bits(words_ref, 1, first_row // BITS, rows // BITS + 2, places)
    if sky_count * TILE != side:
        weight_ref[...] = jnp.zeros_like(weight_ref)
    for tile in range(side // TILE):
        window = slice(tile * TILE, (tile + 1) * TILE)
        bad = row_bad + column_bad[:, window]
        kept = jnp.where(bad == 0, variance_ref[:, window].astype(F32), 0.0)
        target = lax.rem(meta_ref[START] + tile, sky_count) * TILE
        weight_ref[:, pl.ds(pl.multiple_of(target, TILE), TILE)] = kept.astype(BF16)


def weigh(inv_variance, words, meta, half_slot, half_rows, sky_count):
    side = inv_variance.shape[0]
    rows = min(256, half_rows)
    blocks = half_rows // rows
    return pl.pallas_call(
        functools.partial(weight_kernel, sky_count, half_slot, blocks),
        out_shape=jax.ShapeDtypeStruct((half_rows, sky_count * TILE), BF16),
        grid_spec=pltpu.PrefetchScalarGridSpec(
            num_scalar_prefetch=2,
            grid=(blocks,),
            in_specs=[pl.BlockSpec((rows, side), lambda i, m, w: (m[half_slot] * blocks + i, 0))],
            out_specs=pl.BlockSpec((rows, sky_count * TILE), lambda i, m, w: (i, 0)),
        ),
        cost_estimate=pl.CostEstimate(flops=half_rows * side * 8, bytes_accessed=half_rows * side * 4, transcendentals=0),
        name="weigh",
    )(meta, words, inv_variance)


def match_kernel(sky_count, half_slot, half_blocks, offset, meta_ref, picture_ref, column_ref, row_ref, weight_ref, matched_ref, product_ref, wide, stacked):
    side = picture_ref.shape[0]
    block = meta_ref[half_slot] * half_blocks + offset + pl.program_id(0)
    last_block = side // TILE - 1
    first = pl.multiple_of(block * TILE, TILE)
    nothing = jnp.zeros((TILE, SHIFT), BF16)

    def spread(values):
        edge = nothing[: values.shape[0]]
        return jnp.concatenate([edge, values, edge], axis=1)

    above = picture_ref[pl.ds(pl.multiple_of(jnp.maximum(first - EDGE, 0), EDGE), EDGE), :]
    below = picture_ref[pl.ds(pl.multiple_of(jnp.minimum(first + TILE, side - EDGE), EDGE), EDGE), :]
    wide[0:EDGE, :] = spread(jnp.where(block > 0, above, jnp.zeros_like(above)))
    wide[EDGE : EDGE + TILE, :] = spread(picture_ref[pl.ds(first, TILE), :])
    wide[EDGE + TILE :, :] = spread(jnp.where(block < last_block, below, jnp.zeros_like(below)))
    if sky_count * TILE != side:
        product_ref[...] = jnp.zeros_like(product_ref)
    for pair in range(side // (2 * TILE)):
        for part in range(2):
            tile = 2 * pair + part
            passed = jnp.dot(
                wide[:, tile * TILE : (tile + 2) * TILE], column_ref[...], preferred_element_type=F32
            ).astype(BF16)
            for k in range(NB):
                stacked[k * WINDOW : (k + 1) * WINDOW, part * TILE : (part + 1) * TILE] = passed[
                    :, k * TILE : (k + 1) * TILE
                ]
        summed = jnp.dot(row_ref[...], stacked[...], preferred_element_type=F32).astype(BF16)
        matched_ref[:, pair * 2 * TILE : (pair + 1) * 2 * TILE] = summed
        for part in range(2):
            target = pl.multiple_of(lax.rem(meta_ref[START] + 2 * pair + part, sky_count) * TILE, TILE)
            weight = weight_ref[:, pl.ds(target, TILE)].astype(F32)
            product = weight * summed[:, part * TILE : (part + 1) * TILE].astype(F32)
            product_ref[:, pl.ds(target, TILE)] = product.astype(BF16)


def match(picture, column_band, row_band, weight, meta, half_slot, chunk, half_rows, sky_count):
    side = picture.shape[0]
    chunk_rows = half_rows // CHUNKS
    steps = chunk_rows // TILE
    stripe = sky_count * TILE
    return pl.pallas_call(
        functools.partial(match_kernel, sky_count, half_slot, CHUNKS * steps, chunk * steps),
        out_shape=(
            jax.ShapeDtypeStruct((chunk_rows, side), BF16),
            jax.ShapeDtypeStruct((chunk_rows, stripe), BF16),
        ),
        grid_spec=pltpu.PrefetchScalarGridSpec(
            num_scalar_prefetch=1,
            grid=(steps,),
            in_specs=[
                pl.BlockSpec((side, side), lambda i, m: (0, 0)),
                pl.BlockSpec(column_band.shape, lambda i, m: (0, 0)),
                pl.BlockSpec(row_band.shape, lambda i, m: (0, 0)),
                pl.BlockSpec((TILE, stripe), lambda i, m: (chunk * steps + i, 0)),
            ],
            out_specs=(
                pl.BlockSpec((TILE, side), lambda i, m: (i, 0)),
                pl.BlockSpec((TILE, stripe), lambda i, m: (i, 0)),
            ),
            scratch_shapes=[
                pltpu.VMEM((WINDOW, side + TILE), BF16),
                pltpu.VMEM((NB * WINDOW, 2 * TILE), BF16),
            ],
        ),
        cost_estimate=pl.CostEstimate(
            flops=2 * chunk_rows * side * NB * (2 * TILE + WINDOW), bytes_accessed=chunk_rows * side * 8, transcendentals=0
        ),
        name="match",
    )(meta, picture, column_band, row_band, weight)


def row_of(place, line, chunk_rows):
    row = 0
    for bit in range(line.bit_length() - 1):
        row = row + lax.rem(place >> bit, 2) * (chunk_rows >> (bit + 1))
    return row


def piece_rows(meta_ref, step, line, chunk_rows, part_rows):
    row = row_of(lax.rem(meta_ref[LINE] + line - step, line), line, chunk_rows)
    return pl.ds(pl.multiple_of(row, part_rows), part_rows)


def difference_kernel(sky_count, pair, line, chunk, meta_ref, *refs):
    matched = refs[:pair]
    pieces = refs[pair : pair + pair * line]
    out_ref = refs[-1]
    part_rows = pieces[0].shape[0]
    chunk_rows, side = matched[0].shape
    for group in range(pair):
        half = meta_ref[OWN + group]
        for step in range(line):
            rows = piece_rows(meta_ref, step, line, chunk_rows, part_rows)
            piece = pieces[group * line + step]
            for tile in range(side // TILE):
                window = slice(tile * TILE, (tile + 1) * TILE)
                source = pl.multiple_of(lax.rem(meta_ref[START] + tile, sky_count) * TILE, TILE)
                picked = piece[:, pl.ds(source, TILE)].astype(F32)
                out_ref[half, 0, rows, window] = (matched[group][rows, window].astype(F32) - picked).astype(BF16)


def subtract(matched, pieces, meta, chunk, before, sky_count):
    chunk_rows, side = matched[0].shape
    pair = len(matched)
    line = len(pieces) // pair
    operands = [*matched, *pieces]
    specs = [pl.BlockSpec(array.shape, lambda i, m: (0, 0)) for array in operands]
    aliases = {}
    if before is not None:
        operands.append(before)
        specs.append(pl.BlockSpec(memory_space=pl.ANY))
        aliases = {len(operands): 0}
    return pl.pallas_call(
        functools.partial(difference_kernel, sky_count, pair, line, chunk),
        out_shape=jax.ShapeDtypeStruct((pair, CHUNKS, chunk_rows, side), BF16),
        grid_spec=pltpu.PrefetchScalarGridSpec(
            num_scalar_prefetch=1,
            grid=(1,),
            in_specs=specs,
            out_specs=pl.BlockSpec((pair, 1, chunk_rows, side), lambda i, m: (0, chunk, 0, 0)),
        ),
        input_output_aliases=aliases,
        cost_estimate=pl.CostEstimate(
            flops=pair * chunk_rows * side, bytes_accessed=pair * chunk_rows * side * 6, transcendentals=0
        ),
        name="subtract",
    )(meta, *operands)


def smooth_kernel(sky_count, pair, line, meta_ref, across_ref, *refs):
    pieces, out_ref = refs[:-1], refs[-1]
    part_rows = pieces[0].shape[0]
    chunk_rows = out_ref.shape[1]

    def column(piece, away):
        source = lax.rem(meta_ref[SKY] + away, sky_count) * TILE
        return piece[:, pl.ds(pl.multiple_of(source, TILE), TILE)]

    for group in range(pair):
        half = meta_ref[OWN + group]
        for step in range(line):
            rows = piece_rows(meta_ref, step, line, chunk_rows, part_rows)
            piece = pieces[group * line + step]
            window = jnp.concatenate(
                [column(piece, sky_count - 1)[:, SHIFT:], column(piece, 0), column(piece, 1)[:, :SHIFT]], axis=1
            )
            out_ref[half, rows, :] = jnp.dot(window, across_ref[...], preferred_element_type=F32).astype(BF16)


def smooth(pieces, across_band, meta, pair, chunk_rows, sky_count):
    line = len(pieces) // pair
    operands = [across_band, *pieces]
    return pl.pallas_call(
        functools.partial(smooth_kernel, sky_count, pair, line),
        out_shape=jax.ShapeDtypeStruct((pair, chunk_rows, TILE), BF16),
        grid_spec=pltpu.PrefetchScalarGridSpec(
            num_scalar_prefetch=1,
            grid=(1,),
            in_specs=[pl.BlockSpec(array.shape, lambda i, m: (0, 0)) for array in operands],
            out_specs=pl.BlockSpec((pair, chunk_rows, TILE), lambda i, m: (0, 0, 0)),
        ),
        cost_estimate=pl.CostEstimate(
            flops=pair * chunk_rows * TILE * 512, bytes_accessed=pair * chunk_rows * sky_count * TILE * 2, transcendentals=0
        ),
        name="smooth",
    )(meta, *operands)


def power_kernel(band_count, meta_ref, down_ref, *refs):
    sources, powers, smoothed = refs[:CHUNKS], refs[CHUNKS : CHUNKS + band_count], refs[-1]
    pair, chunk_rows = sources[0].shape[:2]
    side = pair * CHUNKS * chunk_rows
    rows = side // band_count
    smoothed[0:EDGE, :] = jnp.zeros((EDGE, TILE), BF16)
    smoothed[EDGE + side :, :] = jnp.zeros((EDGE, TILE), BF16)
    for half in range(pair):
        for chunk in range(CHUNKS):
            first = EDGE + (half * CHUNKS + chunk) * chunk_rows
            smoothed[first : first + chunk_rows, :] = sources[chunk][half]
    for step in range(band_count):
        first = lax.rem(meta_ref[BAND] + step, band_count) * rows
        for inner in range(rows // TILE):
            source = pl.multiple_of(first + inner * TILE, TILE)
            filtered = jnp.dot(down_ref[...], smoothed[pl.ds(source, WINDOW), :], preferred_element_type=F32)
            powers[step][inner * TILE : (inner + 1) * TILE, :] = filtered * filtered


def power(sources, down_band, meta, band_count):
    side = CHUNKS * sources[0].shape[0] * sources[0].shape[1]
    return pl.pallas_call(
        functools.partial(power_kernel, band_count),
        out_shape=[jax.ShapeDtypeStruct((side // band_count, TILE), F32)] * band_count,
        grid_spec=pltpu.PrefetchScalarGridSpec(
            num_scalar_prefetch=1,
            grid=(1,),
            in_specs=[pl.BlockSpec(down_band.shape, lambda i, m: (0, 0))]
            + [pl.BlockSpec(array.shape, lambda i, m: (0, 0, 0)) for array in sources],
            out_specs=[pl.BlockSpec((side // band_count, TILE), lambda i, m: (0, 0))] * band_count,
            scratch_shapes=[pltpu.VMEM((side + 2 * EDGE, TILE), BF16)],
        ),
        cost_estimate=pl.CostEstimate(flops=side * TILE * 320, bytes_accessed=side * TILE * 6, transcendentals=0),
        name="power",
    )(meta, down_band, *sources)


def body(exposures, inv_variance, mask_planes, sky_columns, basis_rows, basis_cols, match_coeffs, detect_taps):
    picture = exposures[0, 0]
    side = picture.shape[0]
    sky_count = lax.axis_size("sky")
    band_count = lax.axis_size("band")
    own_sky = lax.axis_index("sky")
    own_band = lax.axis_index("band")
    pair = 2
    line = sky_count // pair
    low = lax.rem(own_sky, pair)
    high = own_sky // pair
    half_rows = side // pair
    chunk_rows = half_rows // CHUNKS
    slots = jnp.arange(8, dtype=jnp.int32)
    meta = jnp.zeros((8,), jnp.int32)
    scalars = {START: sky_columns[own_sky, own_band, 0], OWN: low, OTHER: 1 - low, LINE: high, SKY: own_sky, BAND: own_band}
    for slot, value in scalars.items():
        meta = jnp.where(slots == slot, value, meta)

    def exchange(block, bit):
        return lax.ppermute(block, "sky", [(i, i ^ (1 << bit)) for i in range(sky_count)])

    def reduce_line(label, terms):
        rows = chunk_rows
        bit = 1
        while 1 << bit < sky_count:
            rows = rows // 2
            mine = lax.rem(own_sky >> bit, 2)
            leaving = sum(lax.dynamic_slice_in_dim(t, (1 - mine) * rows, rows, -2).astype(F32) for t in terms)
            with jax.named_scope(f"{label}_{bit}"):
                arrived = exchange(leaving.astype(BF16), bit)
            terms = [lax.dynamic_slice_in_dim(t, mine * rows, rows, -2) for t in terms] + [arrived]
            bit += 1
        return sum(t.astype(F32) for t in terms)

    words = mask_planes[0, 0]
    variance = inv_variance[0, 0]
    with jax.named_scope("weigh_other"):
        weight_other = weigh(variance, words, meta, OTHER, half_rows, sky_count)
    with jax.named_scope("send_weight_0"):
        weight_in = exchange(weight_other, 0)
    with jax.named_scope("prepare"):
        column_band, row_band, across_band, down_band = prepare(
            match_coeffs[0, 0], basis_cols, basis_rows, detect_taps
        )

    def matching(weight, half_slot, chunk):
        return match(picture, column_band, row_band, weight, meta, half_slot, chunk, half_rows, sky_count)

    away, product_in, home, product_own = ([None] * CHUNKS for _ in range(4))
    for c in range(CHUNKS):
        with jax.named_scope(f"match_other_{c}"):
            away[c], product = matching(weight_other, OTHER, c)
        with jax.named_scope(f"send_product_{c}_0"):
            product_in[c] = exchange(product, 0)
    with jax.named_scope("weigh_own"):
        weight_own = weigh(variance, words, meta, OWN, half_rows, sky_count)
    for c in range(CHUNKS):
        with jax.named_scope(f"match_own_{c}"):
            home[c], product_own[c] = matching(weight_own, OWN, c)

    by_chunk = (CHUNKS, chunk_rows, sky_count * TILE)
    denom = reduce_line("send_weight", [weight_own.reshape(by_chunk), weight_in.reshape(by_chunk)])
    shifts = [[(i, (i // pair + step) % line * pair + i % pair) for i in range(sky_count)] for step in range(line)]
    smoothed = [None] * CHUNKS
    difference = None
    for c in range(CHUNKS):
        numer = reduce_line(f"send_product_{c}", [product_own[c], product_in[c]])
        if c:
            numer, _ = lax.optimization_barrier((numer, block))
        block = (numer / jnp.maximum(denom[c], 1.0)).astype(BF16)
        near, far = [block], []
        with jax.named_scope(f"spread_{c}_0"):
            far.append(exchange(block, 0))
        for step in range(1, line):
            with jax.named_scope(f"gather_{c}_{step}"):
                near.append(lax.ppermute(block, "sky", shifts[step]))
        for step in range(1, line):
            with jax.named_scope(f"spread_{c}_{step}"):
                far.append(exchange(near[step], 0))
        pieces = near + far
        with jax.named_scope(f"smooth_{c}"):
            smoothed[c] = smooth(pieces, across_band, meta, pair, chunk_rows, sky_count)
        with jax.named_scope(f"subtract_{c}"):
            difference = subtract([home[c], away[c]], pieces, meta, c, difference, sky_count)

    with jax.named_scope("power"):
        powers = power(smoothed, down_band, meta, band_count)
    detection = powers[0]
    for step in range(1, band_count):
        with jax.named_scope(f"bands_{step}"):
            ring = [(i, (i + step) % band_count) for i in range(band_count)]
            detection = detection + lax.ppermute(powers[step], "band", ring)
    return (difference.reshape(1, 1, side, side), detection)


def solution(mesh):
    in_specs = (
        P("sky", "band", None, None),
        P("sky", "band", None, None),
        P("sky", "band", None, None),
        P(),
        P(),
        P(),
        P("sky", "band", None),
        P("band", None),
    )
    out_specs = (P("sky", "band", None, None), P("band", "sky"))
    return jax.shard_map(body, mesh=mesh, in_specs=in_specs, out_specs=out_specs, check_vma=False)
```

```python
import functools

import jax
import jax.numpy as jnp
from jax import lax
from jax.experimental import pallas as pl
from jax.experimental.pallas import tpu as pltpu
from jax.sharding import PartitionSpec as P


TILE = 128
NB = 9
TAPS = 25
DTAPS = 31
BITS = 30
EDGE = 16
WINDOW = TILE + 2 * EDGE
SHIFT = TILE // 2
CHUNKS = 2
START, OWN, OTHER, LINE, SKY, BAND = range(6)
F32 = jnp.float32
BF16 = jnp.bfloat16


def toeplitz(base_row, rows):
    wide = jnp.broadcast_to(base_row, (rows, base_row.shape[1]))
    return pltpu.roll(wide, 0, 1, stride=1, stride_axis=0)


def prepare_kernel(base_ref, column_ref, row_ref, across_ref, down_ref):
    for k in range(NB):
        column_ref[:, k * TILE : (k + 1) * TILE] = toeplitz(base_ref[k : k + 1, :], TILE).T.astype(BF16)
        row_ref[:, k * WINDOW : (k + 1) * WINDOW] = toeplitz(base_ref[NB + k : NB + k + 1, :], TILE)[
            :, :WINDOW
        ].astype(BF16)
    across_ref[...] = toeplitz(base_ref[2 * NB : 2 * NB + 1, :], TILE).T.astype(BF16)
    down_ref[...] = toeplitz(base_ref[2 * NB + 1 : 2 * NB + 2, :], TILE)[:, :WINDOW].astype(BF16)


def place_left(taps, offset):
    return jnp.pad(taps, ((0, 0), (offset, 2 * TILE - offset - taps.shape[1])))


def prepare(match_coeffs, basis_cols, basis_rows, detect_taps):
    column_taps = (match_coeffs[:, None] * basis_cols).astype(BF16).astype(F32)
    row_taps = basis_rows.astype(BF16).astype(F32)
    taps = detect_taps.astype(BF16).astype(F32)
    base = jnp.concatenate(
        [
            place_left(column_taps, SHIFT - TAPS // 2),
            place_left(row_taps, EDGE - TAPS // 2),
            place_left(taps, SHIFT - DTAPS // 2),
            place_left(taps, EDGE - DTAPS // 2),
        ],
        0,
    )
    return pl.pallas_call(
        prepare_kernel,
        out_shape=(
            jax.ShapeDtypeStruct((2 * TILE, NB * TILE), BF16),
            jax.ShapeDtypeStruct((TILE, NB * WINDOW), BF16),
            jax.ShapeDtypeStruct((2 * TILE, TILE), BF16),
            jax.ShapeDtypeStruct((TILE, WINDOW), BF16),
        ),
        compiler_params=pltpu.CompilerParams(vmem_limit_bytes=16 << 20),
        name="prepare",
    )(base)


def bad_bits(words_ref, plane, first_word, count, places):
    last = words_ref.shape[1] - 1
    word = jnp.full(places.shape, words_ref[plane, jnp.minimum(first_word, last)])
    begin = jnp.full(places.shape, first_word * BITS)
    for step in range(1, count):
        index = first_word + step
        reached = places >= index * BITS
        word = jnp.where(reached, words_ref[plane, jnp.minimum(index, last)], word)
        begin = jnp.where(reached, index * BITS, begin)
    return jnp.bitwise_and(jnp.right_shift(word, places - begin), 1)


def weight_kernel(sky_count, half_slot, half_blocks, meta_ref, words_ref, variance_ref, weight_ref):
    rows, side = variance_ref.shape
    first_row = (meta_ref[half_slot] * half_blocks + pl.program_id(0)) * rows
    lanes = lax.broadcasted_iota(jnp.int32, (8, side), 1)
    column_bad = bad_bits(words_ref, 0, 0, words_ref.shape[1], lanes)[0:1, :]
    places = first_row + lax.broadcasted_iota(jnp.int32, (rows, TILE), 0)
    row_bad = bad_bits(words_ref, 1, first_row // BITS, rows // BITS + 2, places)
    if sky_count * TILE != side:
        weight_ref[...] = jnp.zeros_like(weight_ref)
    for tile in range(side // TILE):
        window = slice(tile * TILE, (tile + 1) * TILE)
        bad = row_bad + column_bad[:, window]
        kept = jnp.where(bad == 0, variance_ref[:, window].astype(F32), 0.0)
        target = lax.rem(meta_ref[START] + tile, sky_count) * TILE
        weight_ref[:, pl.ds(pl.multiple_of(target, TILE), TILE)] = kept.astype(BF16)


def weigh(inv_variance, words, meta, half_slot, half_rows, sky_count):
    side = inv_variance.shape[0]
    rows = min(256, half_rows)
    blocks = half_rows // rows
    return pl.pallas_call(
        functools.partial(weight_kernel, sky_count, half_slot, blocks),
        out_shape=jax.ShapeDtypeStruct((half_rows, sky_count * TILE), BF16),
        grid_spec=pltpu.PrefetchScalarGridSpec(
            num_scalar_prefetch=2,
            grid=(blocks,),
            in_specs=[pl.BlockSpec((rows, side), lambda i, m, w: (m[half_slot] * blocks + i, 0))],
            out_specs=pl.BlockSpec((rows, sky_count * TILE), lambda i, m, w: (i, 0)),
        ),
        cost_estimate=pl.CostEstimate(flops=half_rows * side * 8, bytes_accessed=half_rows * side * 4, transcendentals=0),
        compiler_params=pltpu.CompilerParams(vmem_limit_bytes=20 << 20),
        name="weigh",
    )(meta, words, inv_variance)


def match_kernel(sky_count, half_slot, half_blocks, offset, meta_ref, picture_ref, column_ref, row_ref, weight_ref, matched_ref, product_ref, windows, stacked):
    side = picture_ref.shape[0]
    block = meta_ref[half_slot] * half_blocks + offset + pl.program_id(0)
    last_block = side // TILE - 1
    first = pl.multiple_of(block * TILE, TILE)
    nothing = jnp.zeros((TILE, SHIFT), BF16)

    def spread(values):
        edge = nothing[: values.shape[0]]
        return jnp.concatenate([edge, values, edge], axis=1)

    above = picture_ref[pl.ds(pl.multiple_of(jnp.maximum(first - EDGE, 0), EDGE), EDGE), :]
    below = picture_ref[pl.ds(pl.multiple_of(jnp.minimum(first + TILE, side - EDGE), EDGE), EDGE), :]
    tiles = side // TILE
    parts = (
        (0, spread(jnp.where(block > 0, above, jnp.zeros_like(above)))),
        (EDGE, spread(picture_ref[pl.ds(first, TILE), :])),
        (EDGE + TILE, spread(jnp.where(block < last_block, below, jnp.zeros_like(below)))),
    )
    for tile in range(tiles):
        for row, part in parts:
            row = tile * WINDOW + row
            windows[row : row + part.shape[0], :] = part[:, tile * TILE : (tile + 2) * TILE]
    for group in range(0, NB, 2):
        bands = range(group, min(group + 2, NB))
        passed = jnp.dot(
            windows[...], column_ref[:, group * TILE : (bands[-1] + 1) * TILE], preferred_element_type=F32
        ).astype(BF16)
        for k in bands:
            for tile in range(tiles):
                stacked[k * WINDOW : (k + 1) * WINDOW, tile * TILE : (tile + 1) * TILE] = passed[
                    tile * WINDOW : (tile + 1) * WINDOW, (k - group) * TILE : (k - group + 1) * TILE
                ]
    if sky_count != tiles:
        product_ref[...] = jnp.zeros_like(product_ref)
    for pair in range(tiles // 2):
        both = slice(pair * 2 * TILE, (pair + 1) * 2 * TILE)
        summed = jnp.dot(row_ref[...], stacked[:, both], preferred_element_type=F32).astype(BF16)
        matched_ref[:, both] = summed
        for part in range(2):
            target = pl.multiple_of(lax.rem(meta_ref[START] + 2 * pair + part, sky_count) * TILE, TILE)
            weight = weight_ref[:, pl.ds(target, TILE)].astype(F32)
            product = weight * summed[:, part * TILE : (part + 1) * TILE].astype(F32)
            product_ref[:, pl.ds(target, TILE)] = product.astype(BF16)


def match(picture, column_band, row_band, weight, meta, half_slot, chunk, half_rows, sky_count):
    side = picture.shape[0]
    chunk_rows = half_rows // CHUNKS
    steps = chunk_rows // TILE
    stripe = sky_count * TILE
    return pl.pallas_call(
        functools.partial(match_kernel, sky_count, half_slot, CHUNKS * steps, chunk * steps),
        out_shape=(
            jax.ShapeDtypeStruct((chunk_rows, side), BF16),
            jax.ShapeDtypeStruct((chunk_rows, stripe), BF16),
        ),
        grid_spec=pltpu.PrefetchScalarGridSpec(
            num_scalar_prefetch=1,
            grid=(steps,),
            in_specs=[
                pl.BlockSpec((side, side), lambda i, m: (0, 0)),
                pl.BlockSpec(column_band.shape, lambda i, m: (0, 0)),
                pl.BlockSpec(row_band.shape, lambda i, m: (0, 0)),
                pl.BlockSpec((TILE, stripe), lambda i, m: (chunk * steps + i, 0)),
            ],
            out_specs=(
                pl.BlockSpec((TILE, side), lambda i, m: (i, 0)),
                pl.BlockSpec((TILE, stripe), lambda i, m: (i, 0)),
            ),
            scratch_shapes=[
                pltpu.VMEM((side // TILE * WINDOW, 2 * TILE), BF16),
                pltpu.VMEM((NB * WINDOW, side), BF16),
            ],
        ),
        cost_estimate=pl.CostEstimate(
            flops=2 * chunk_rows * side * NB * (2 * TILE + WINDOW), bytes_accessed=chunk_rows * side * 8, transcendentals=0
        ),
        compiler_params=pltpu.CompilerParams(vmem_limit_bytes=28 << 20),
        name="match",
    )(meta, picture, column_band, row_band, weight)


def row_of(place, line, chunk_rows):
    row = 0
    for bit in range(line.bit_length() - 1):
        row = row + lax.rem(place >> bit, 2) * (chunk_rows >> (bit + 1))
    return row


def piece_rows(meta_ref, step, line, chunk_rows, part_rows):
    row = row_of(lax.rem(meta_ref[LINE] + line - step, line), line, chunk_rows)
    return pl.ds(pl.multiple_of(row, part_rows), part_rows)


def difference_kernel(sky_count, pair, line, meta_ref, *refs):
    matched = refs[:pair]
    pieces = refs[pair : pair + pair * line]
    out_ref = refs[-1]
    part_rows = pieces[0].shape[0]
    chunk_rows, side = matched[0].shape
    for group in range(pair):
        half = meta_ref[OWN + group]
        for step in range(line):
            rows = piece_rows(meta_ref, step, line, chunk_rows, part_rows)
            piece = pieces[group * line + step]
            for tile in range(side // TILE):
                window = slice(tile * TILE, (tile + 1) * TILE)
                source = pl.multiple_of(lax.rem(meta_ref[START] + tile, sky_count) * TILE, TILE)
                picked = piece[:, pl.ds(source, TILE)].astype(F32)
                out_ref[half, 0, rows, window] = (matched[group][rows, window].astype(F32) - picked).astype(BF16)


def subtract(matched, pieces, meta, chunk, before, sky_count):
    chunk_rows, side = matched[0].shape
    pair = len(matched)
    line = len(pieces) // pair
    operands = [*matched, *pieces]
    specs = [pl.BlockSpec(array.shape, lambda i, m: (0, 0)) for array in operands]
    aliases = {}
    if before is not None:
        operands.append(before)
        specs.append(pl.BlockSpec(memory_space=pl.ANY))
        aliases = {len(operands): 0}
    return pl.pallas_call(
        functools.partial(difference_kernel, sky_count, pair, line),
        out_shape=jax.ShapeDtypeStruct((pair, CHUNKS, chunk_rows, side), BF16),
        grid_spec=pltpu.PrefetchScalarGridSpec(
            num_scalar_prefetch=1,
            grid=(1,),
            in_specs=specs,
            out_specs=pl.BlockSpec((pair, 1, chunk_rows, side), lambda i, m: (0, chunk, 0, 0)),
        ),
        input_output_aliases=aliases,
        cost_estimate=pl.CostEstimate(
            flops=pair * chunk_rows * side, bytes_accessed=pair * chunk_rows * side * 6, transcendentals=0
        ),
        compiler_params=pltpu.CompilerParams(vmem_limit_bytes=24 << 20),
        name="subtract",
    )(meta, *operands)


def smooth_kernel(sky_count, pair, line, meta_ref, across_ref, *refs):
    pieces, out_ref = refs[:-1], refs[-1]
    part_rows = pieces[0].shape[0]
    chunk_rows = out_ref.shape[1]

    def column(piece, away):
        source = lax.rem(meta_ref[SKY] + away, sky_count) * TILE
        return piece[:, pl.ds(pl.multiple_of(source, TILE), TILE)]

    for group in range(pair):
        half = meta_ref[OWN + group]
        for step in range(line):
            rows = piece_rows(meta_ref, step, line, chunk_rows, part_rows)
            piece = pieces[group * line + step]
            window = jnp.concatenate(
                [column(piece, sky_count - 1)[:, SHIFT:], column(piece, 0), column(piece, 1)[:, :SHIFT]], axis=1
            )
            out_ref[half, rows, :] = jnp.dot(window, across_ref[...], preferred_element_type=F32).astype(BF16)


def smooth(pieces, across_band, meta, pair, chunk_rows, sky_count):
    line = len(pieces) // pair
    operands = [across_band, *pieces]
    return pl.pallas_call(
        functools.partial(smooth_kernel, sky_count, pair, line),
        out_shape=jax.ShapeDtypeStruct((pair, chunk_rows, TILE), BF16),
        grid_spec=pltpu.PrefetchScalarGridSpec(
            num_scalar_prefetch=1,
            grid=(1,),
            in_specs=[pl.BlockSpec(array.shape, lambda i, m: (0, 0)) for array in operands],
            out_specs=pl.BlockSpec((pair, chunk_rows, TILE), lambda i, m: (0, 0, 0)),
        ),
        cost_estimate=pl.CostEstimate(
            flops=pair * chunk_rows * TILE * 512, bytes_accessed=pair * chunk_rows * sky_count * TILE * 2, transcendentals=0
        ),
        compiler_params=pltpu.CompilerParams(vmem_limit_bytes=20 << 20),
        name="smooth",
    )(meta, *operands)


def power_kernel(band_count, meta_ref, down_ref, *refs):
    sources, powers, smoothed = refs[:CHUNKS], refs[CHUNKS : CHUNKS + band_count], refs[-1]
    pair, chunk_rows = sources[0].shape[:2]
    side = pair * CHUNKS * chunk_rows
    rows = side // band_count
    smoothed[0:EDGE, :] = jnp.zeros((EDGE, TILE), BF16)
    smoothed[EDGE + side :, :] = jnp.zeros((EDGE, TILE), BF16)
    for half in range(pair):
        for chunk in range(CHUNKS):
            first = EDGE + (half * CHUNKS + chunk) * chunk_rows
            smoothed[first : first + chunk_rows, :] = sources[chunk][half]
    for step in range(band_count):
        first = lax.rem(meta_ref[BAND] + step, band_count) * rows
        for inner in range(rows // TILE):
            source = pl.multiple_of(first + inner * TILE, TILE)
            filtered = jnp.dot(down_ref[...], smoothed[pl.ds(source, WINDOW), :], preferred_element_type=F32)
            powers[step][inner * TILE : (inner + 1) * TILE, :] = filtered * filtered


def power(sources, down_band, meta, band_count):
    side = CHUNKS * sources[0].shape[0] * sources[0].shape[1]
    return pl.pallas_call(
        functools.partial(power_kernel, band_count),
        out_shape=[jax.ShapeDtypeStruct((side // band_count, TILE), F32)] * band_count,
        grid_spec=pltpu.PrefetchScalarGridSpec(
            num_scalar_prefetch=1,
            grid=(1,),
            in_specs=[pl.BlockSpec(down_band.shape, lambda i, m: (0, 0))]
            + [pl.BlockSpec(array.shape, lambda i, m: (0, 0, 0)) for array in sources],
            out_specs=[pl.BlockSpec((side // band_count, TILE), lambda i, m: (0, 0))] * band_count,
            scratch_shapes=[pltpu.VMEM((side + 2 * EDGE, TILE), BF16)],
        ),
        cost_estimate=pl.CostEstimate(flops=side * TILE * 320, bytes_accessed=side * TILE * 6, transcendentals=0),
        compiler_params=pltpu.CompilerParams(vmem_limit_bytes=16 << 20),
        name="power",
    )(meta, down_band, *sources)


def body(exposures, inv_variance, mask_planes, sky_columns, basis_rows, basis_cols, match_coeffs, detect_taps):
    picture = exposures[0, 0]
    side = picture.shape[0]
    sky_count = lax.axis_size("sky")
    band_count = lax.axis_size("band")
    own_sky = lax.axis_index("sky")
    own_band = lax.axis_index("band")
    pair = 2
    line = sky_count // pair
    low = lax.rem(own_sky, pair)
    high = own_sky // pair
    half_rows = side // pair
    chunk_rows = half_rows // CHUNKS
    slots = jnp.arange(8, dtype=jnp.int32)
    meta = jnp.zeros((8,), jnp.int32)
    scalars = {START: sky_columns[own_sky, own_band, 0], OWN: low, OTHER: 1 - low, LINE: high, SKY: own_sky, BAND: own_band}
    for slot, value in scalars.items():
        meta = jnp.where(slots == slot, value, meta)

    def exchange(block, bit):
        return lax.ppermute(block, "sky", [(i, i ^ (1 << bit)) for i in range(sky_count)])

    def reduce_line(terms):
        rows = chunk_rows
        bit = 1
        while 1 << bit < sky_count:
            rows = rows // 2
            mine = lax.rem(own_sky >> bit, 2)
            leaving = sum(lax.dynamic_slice_in_dim(t, (1 - mine) * rows, rows, -2).astype(F32) for t in terms)
            arrived = exchange(leaving.astype(BF16), bit)
            terms = [lax.dynamic_slice_in_dim(t, mine * rows, rows, -2) for t in terms] + [arrived]
            bit += 1
        return sum(t.astype(F32) for t in terms)

    words = mask_planes[0, 0]
    variance = inv_variance[0, 0]
    weight_other = weigh(variance, words, meta, OTHER, half_rows, sky_count)
    weight_in = exchange(weight_other, 0)
    column_band, row_band, across_band, down_band = prepare(
        match_coeffs[0, 0], basis_cols, basis_rows, detect_taps
    )

    def matching(weight, half_slot, chunk):
        return match(picture, column_band, row_band, weight, meta, half_slot, chunk, half_rows, sky_count)

    away, product_in, home, product_own = ([None] * CHUNKS for _ in range(4))
    for c in range(CHUNKS):
        away[c], product = matching(weight_other, OTHER, c)
        product_in[c] = exchange(product, 0)
    weight_own = weigh(variance, words, meta, OWN, half_rows, sky_count)
    for c in range(CHUNKS):
        home[c], product_own[c] = matching(weight_own, OWN, c)

    by_chunk = (CHUNKS, chunk_rows, sky_count * TILE)
    denom = reduce_line([weight_own.reshape(by_chunk), weight_in.reshape(by_chunk)])
    shifts = [[(i, (i // pair + step) % line * pair + i % pair) for i in range(sky_count)] for step in range(line)]
    smoothed = [None] * CHUNKS
    difference = None
    for c in range(CHUNKS):
        numer = reduce_line([product_own[c], product_in[c]])
        if c:
            numer, _ = lax.optimization_barrier((numer, block))
        block = (numer / jnp.maximum(denom[c], 1.0)).astype(BF16)
        near, far = [block], []
        far.append(exchange(block, 0))
        for step in range(1, line):
            near.append(lax.ppermute(block, "sky", shifts[step]))
        for step in range(1, line):
            far.append(exchange(near[step], 0))
        pieces = near + far
        smoothed[c] = smooth(pieces, across_band, meta, pair, chunk_rows, sky_count)
        difference = subtract([home[c], away[c]], pieces, meta, c, difference, sky_count)

    powers = power(smoothed, down_band, meta, band_count)
    detection = powers[0]
    for step in range(1, band_count):
        ring = [(i, (i + step) % band_count) for i in range(band_count)]
        detection = detection + lax.ppermute(powers[step], "band", ring)
    return (difference.reshape(1, 1, side, side), detection)


def solution(mesh):
    in_specs = (
        P("sky", "band", None, None),
        P("sky", "band", None, None),
        P("sky", "band", None, None),
        P(),
        P(),
        P(),
        P("sky", "band", None),
        P("band", None),
    )
    out_specs = (P("sky", "band", None, None), P("band", "sky"))

    return jax.shard_map(body, mesh=mesh, in_specs=in_specs, out_specs=out_specs, check_vma=False)
```

```python
import functools

import jax
import jax.numpy as jnp
from jax import lax
from jax.experimental import pallas as pl
from jax.experimental.pallas import tpu as pltpu
from jax.sharding import PartitionSpec as P


TILE = 128
NB = 9
TAPS = 25
DTAPS = 31
BITS = 30
EDGE = 16
WINDOW = TILE + 2 * EDGE
SHIFT = TILE // 2
CHUNKS = 2
START, OWN, OTHER, LINE, SKY, BAND = range(6)
F32 = jnp.float32
BF16 = jnp.bfloat16


def toeplitz(base_row, rows):
    wide = jnp.broadcast_to(base_row, (rows, base_row.shape[1]))
    return pltpu.roll(wide, 0, 1, stride=1, stride_axis=0)


def prepare_kernel(base_ref, column_ref, row_ref, across_ref, down_ref):
    for k in range(NB):
        column_ref[:, k * TILE : (k + 1) * TILE] = toeplitz(base_ref[k : k + 1, :], TILE).T.astype(BF16)
        row_ref[:, k * WINDOW : (k + 1) * WINDOW] = toeplitz(base_ref[NB + k : NB + k + 1, :], TILE)[
            :, :WINDOW
        ].astype(BF16)
    across_ref[...] = toeplitz(base_ref[2 * NB : 2 * NB + 1, :], TILE).T.astype(BF16)
    down_ref[...] = toeplitz(base_ref[2 * NB + 1 : 2 * NB + 2, :], TILE)[:, :WINDOW].astype(BF16)


def place_left(taps, offset):
    return jnp.pad(taps, ((0, 0), (offset, 2 * TILE - offset - taps.shape[1])))


def prepare(match_coeffs, basis_cols, basis_rows, detect_taps):
    column_taps = (match_coeffs[:, None] * basis_cols).astype(BF16).astype(F32)
    row_taps = basis_rows.astype(BF16).astype(F32)
    taps = detect_taps.astype(BF16).astype(F32)
    base = jnp.concatenate(
        [
            place_left(column_taps, SHIFT - TAPS // 2),
            place_left(row_taps, EDGE - TAPS // 2),
            place_left(taps, SHIFT - DTAPS // 2),
            place_left(taps, EDGE - DTAPS // 2),
        ],
        0,
    )
    return pl.pallas_call(
        prepare_kernel,
        out_shape=(
            jax.ShapeDtypeStruct((2 * TILE, NB * TILE), BF16),
            jax.ShapeDtypeStruct((TILE, NB * WINDOW), BF16),
            jax.ShapeDtypeStruct((2 * TILE, TILE), BF16),
            jax.ShapeDtypeStruct((TILE, WINDOW), BF16),
        ),
        compiler_params=pltpu.CompilerParams(vmem_limit_bytes=16 << 20),
        name="prepare",
    )(base)


def bad_bits(words_ref, plane, first_word, count, places):
    last = words_ref.shape[1] - 1
    word = jnp.full(places.shape, words_ref[plane, jnp.minimum(first_word, last)])
    begin = jnp.full(places.shape, first_word * BITS)
    for step in range(1, count):
        index = first_word + step
        reached = places >= index * BITS
        word = jnp.where(reached, words_ref[plane, jnp.minimum(index, last)], word)
        begin = jnp.where(reached, index * BITS, begin)
    return jnp.bitwise_and(jnp.right_shift(word, places - begin), 1)


def weight_kernel(sky_count, halves, chunk, meta_ref, words_ref, variance_ref, weight_ref):
    rows, side = variance_ref.shape
    half = meta_ref[halves[0]]
    for index in range(1, len(halves)):
        half = jnp.where(pl.program_id(0) == index, meta_ref[halves[index]], half)
    first_row = (half * CHUNKS + chunk) * rows
    lanes = lax.broadcasted_iota(jnp.int32, (8, side), 1)
    column_bad = bad_bits(words_ref, 0, 0, words_ref.shape[1], lanes)[0:1, :]
    places = first_row + lax.broadcasted_iota(jnp.int32, (rows, TILE), 0)
    row_bad = bad_bits(words_ref, 1, first_row // BITS, rows // BITS + 2, places)
    if sky_count * TILE != side:
        weight_ref[...] = jnp.zeros_like(weight_ref)
    for tile in range(side // TILE):
        window = slice(tile * TILE, (tile + 1) * TILE)
        bad = row_bad + column_bad[:, window]
        kept = jnp.where(bad == 0, variance_ref[:, window].astype(F32), 0.0)
        target = lax.rem(meta_ref[START] + tile, sky_count) * TILE
        weight_ref[0, :, pl.ds(pl.multiple_of(target, TILE), TILE)] = kept.astype(BF16)


def weigh(inv_variance, words, meta, halves, chunk, rows, sky_count):
    side = inv_variance.shape[0]
    stripe = sky_count * TILE

    def source(i, m, w):
        half = m[halves[0]]
        for index in range(1, len(halves)):
            half = jnp.where(i == index, m[halves[index]], half)
        return (half * CHUNKS + chunk, 0)

    return pl.pallas_call(
        functools.partial(weight_kernel, sky_count, halves, chunk),
        out_shape=jax.ShapeDtypeStruct((len(halves), rows, stripe), BF16),
        grid_spec=pltpu.PrefetchScalarGridSpec(
            num_scalar_prefetch=2,
            grid=(len(halves),),
            in_specs=[pl.BlockSpec((rows, side), source)],
            out_specs=pl.BlockSpec((1, rows, stripe), lambda i, m, w: (i, 0, 0)),
        ),
        cost_estimate=pl.CostEstimate(
            flops=len(halves) * rows * side * 8, bytes_accessed=len(halves) * rows * side * 4, transcendentals=0
        ),
        compiler_params=pltpu.CompilerParams(vmem_limit_bytes=20 << 20),
        name="weigh",
    )(meta, words, inv_variance)


def match_kernel(sky_count, half_slot, half_blocks, offset, meta_ref, picture_ref, column_ref, row_ref, weight_ref, matched_ref, product_ref, windows, stacked):
    side = picture_ref.shape[0]
    block = meta_ref[half_slot] * half_blocks + offset + pl.program_id(0)
    last_block = side // TILE - 1
    first = pl.multiple_of(block * TILE, TILE)
    nothing = jnp.zeros((TILE, SHIFT), BF16)

    def spread(values):
        edge = nothing[: values.shape[0]]
        return jnp.concatenate([edge, values, edge], axis=1)

    above = picture_ref[pl.ds(pl.multiple_of(jnp.maximum(first - EDGE, 0), EDGE), EDGE), :]
    below = picture_ref[pl.ds(pl.multiple_of(jnp.minimum(first + TILE, side - EDGE), EDGE), EDGE), :]
    tiles = side // TILE
    parts = (
        (0, spread(jnp.where(block > 0, above, jnp.zeros_like(above)))),
        (EDGE, spread(picture_ref[pl.ds(first, TILE), :])),
        (EDGE + TILE, spread(jnp.where(block < last_block, below, jnp.zeros_like(below)))),
    )
    for tile in range(tiles):
        for row, part in parts:
            row = tile * WINDOW + row
            windows[row : row + part.shape[0], :] = part[:, tile * TILE : (tile + 2) * TILE]
    for group in range(0, NB, 2):
        bands = range(group, min(group + 2, NB))
        passed = jnp.dot(
            windows[...], column_ref[:, group * TILE : (bands[-1] + 1) * TILE], preferred_element_type=F32
        ).astype(BF16)
        for k in bands:
            for tile in range(tiles):
                stacked[k * WINDOW : (k + 1) * WINDOW, tile * TILE : (tile + 1) * TILE] = passed[
                    tile * WINDOW : (tile + 1) * WINDOW, (k - group) * TILE : (k - group + 1) * TILE
                ]
    if sky_count != tiles:
        product_ref[...] = jnp.zeros_like(product_ref)
    for pair in range(tiles // 2):
        both = slice(pair * 2 * TILE, (pair + 1) * 2 * TILE)
        summed = jnp.dot(row_ref[...], stacked[:, both], preferred_element_type=F32).astype(BF16)
        matched_ref[:, both] = summed
        for part in range(2):
            target = pl.multiple_of(lax.rem(meta_ref[START] + 2 * pair + part, sky_count) * TILE, TILE)
            weight = weight_ref[:, pl.ds(target, TILE)].astype(F32)
            product = weight * summed[:, part * TILE : (part + 1) * TILE].astype(F32)
            product_ref[:, pl.ds(target, TILE)] = product.astype(BF16)


def match(picture, column_band, row_band, weight, which, meta, half_slot, chunk, half_rows, sky_count):
    side = picture.shape[0]
    chunk_rows = half_rows // CHUNKS
    steps = chunk_rows // TILE
    stripe = sky_count * TILE
    return pl.pallas_call(
        functools.partial(match_kernel, sky_count, half_slot, CHUNKS * steps, chunk * steps),
        out_shape=(
            jax.ShapeDtypeStruct((chunk_rows, side), BF16),
            jax.ShapeDtypeStruct((chunk_rows, stripe), BF16),
        ),
        grid_spec=pltpu.PrefetchScalarGridSpec(
            num_scalar_prefetch=1,
            grid=(steps,),
            in_specs=[
                pl.BlockSpec((side, side), lambda i, m: (0, 0)),
                pl.BlockSpec(column_band.shape, lambda i, m: (0, 0)),
                pl.BlockSpec(row_band.shape, lambda i, m: (0, 0)),
                pl.BlockSpec((None, TILE, stripe), lambda i, m: (which, i, 0)),
            ],
            out_specs=(
                pl.BlockSpec((TILE, side), lambda i, m: (i, 0)),
                pl.BlockSpec((TILE, stripe), lambda i, m: (i, 0)),
            ),
            scratch_shapes=[
                pltpu.VMEM((side // TILE * WINDOW, 2 * TILE), BF16),
                pltpu.VMEM((NB * WINDOW, side), BF16),
            ],
        ),
        cost_estimate=pl.CostEstimate(
            flops=2 * chunk_rows * side * NB * (2 * TILE + WINDOW), bytes_accessed=chunk_rows * side * 8, transcendentals=0
        ),
        compiler_params=pltpu.CompilerParams(vmem_limit_bytes=28 << 20),
        name="match",
    )(meta, picture, column_band, row_band, weight)


def row_of(place, line, chunk_rows):
    row = 0
    for bit in range(line.bit_length() - 1):
        row = row + lax.rem(place >> bit, 2) * (chunk_rows >> (bit + 1))
    return row


def piece_rows(meta_ref, step, line, chunk_rows, part_rows):
    row = row_of(lax.rem(meta_ref[LINE] + line - step, line), line, chunk_rows)
    return pl.ds(pl.multiple_of(row, part_rows), part_rows)


def difference_kernel(sky_count, pair, line, meta_ref, *refs):
    matched = refs[:pair]
    pieces = refs[pair : pair + pair * line]
    out_ref = refs[-1]
    part_rows = pieces[0].shape[0]
    chunk_rows, side = matched[0].shape
    for group in range(pair):
        half = meta_ref[OWN + group]
        for step in range(line):
            rows = piece_rows(meta_ref, step, line, chunk_rows, part_rows)
            piece = pieces[group * line + step]
            for tile in range(side // TILE):
                window = slice(tile * TILE, (tile + 1) * TILE)
                source = pl.multiple_of(lax.rem(meta_ref[START] + tile, sky_count) * TILE, TILE)
                picked = piece[:, pl.ds(source, TILE)].astype(F32)
                out_ref[half, 0, rows, window] = (matched[group][rows, window].astype(F32) - picked).astype(BF16)


def subtract(matched, pieces, meta, chunk, before, sky_count):
    chunk_rows, side = matched[0].shape
    pair = len(matched)
    line = len(pieces) // pair
    operands = [*matched, *pieces]
    specs = [pl.BlockSpec(array.shape, lambda i, m: (0, 0)) for array in operands]
    aliases = {}
    if before is not None:
        operands.append(before)
        specs.append(pl.BlockSpec(memory_space=pl.ANY))
        aliases = {len(operands): 0}
    return pl.pallas_call(
        functools.partial(difference_kernel, sky_count, pair, line),
        out_shape=jax.ShapeDtypeStruct((pair, CHUNKS, chunk_rows, side), BF16),
        grid_spec=pltpu.PrefetchScalarGridSpec(
            num_scalar_prefetch=1,
            grid=(1,),
            in_specs=specs,
            out_specs=pl.BlockSpec((pair, 1, chunk_rows, side), lambda i, m: (0, chunk, 0, 0)),
        ),
        input_output_aliases=aliases,
        cost_estimate=pl.CostEstimate(
            flops=pair * chunk_rows * side, bytes_accessed=pair * chunk_rows * side * 6, transcendentals=0
        ),
        compiler_params=pltpu.CompilerParams(vmem_limit_bytes=24 << 20),
        name="subtract",
    )(meta, *operands)


def smooth_kernel(sky_count, pair, line, meta_ref, across_ref, *refs):
    pieces, out_ref = refs[:-1], refs[-1]
    part_rows = pieces[0].shape[0]
    chunk_rows = out_ref.shape[1]

    def column(piece, away):
        source = lax.rem(meta_ref[SKY] + away, sky_count) * TILE
        return piece[:, pl.ds(pl.multiple_of(source, TILE), TILE)]

    for group in range(pair):
        half = meta_ref[OWN + group]
        for step in range(line):
            rows = piece_rows(meta_ref, step, line, chunk_rows, part_rows)
            piece = pieces[group * line + step]
            window = jnp.concatenate(
                [column(piece, sky_count - 1)[:, SHIFT:], column(piece, 0), column(piece, 1)[:, :SHIFT]], axis=1
            )
            out_ref[half, rows, :] = jnp.dot(window, across_ref[...], preferred_element_type=F32).astype(BF16)


def smooth(pieces, across_band, meta, pair, chunk_rows, sky_count):
    line = len(pieces) // pair
    operands = [across_band, *pieces]
    return pl.pallas_call(
        functools.partial(smooth_kernel, sky_count, pair, line),
        out_shape=jax.ShapeDtypeStruct((pair, chunk_rows, TILE), BF16),
        grid_spec=pltpu.PrefetchScalarGridSpec(
            num_scalar_prefetch=1,
            grid=(1,),
            in_specs=[pl.BlockSpec(array.shape, lambda i, m: (0, 0)) for array in operands],
            out_specs=pl.BlockSpec((pair, chunk_rows, TILE), lambda i, m: (0, 0, 0)),
        ),
        cost_estimate=pl.CostEstimate(
            flops=pair * chunk_rows * TILE * 512, bytes_accessed=pair * chunk_rows * sky_count * TILE * 2, transcendentals=0
        ),
        compiler_params=pltpu.CompilerParams(vmem_limit_bytes=20 << 20),
        name="smooth",
    )(meta, *operands)


def power_kernel(band_count, meta_ref, down_ref, *refs):
    sources, powers, smoothed = refs[:CHUNKS], refs[CHUNKS : CHUNKS + band_count], refs[-1]
    pair, chunk_rows = sources[0].shape[:2]
    side = pair * CHUNKS * chunk_rows
    rows = side // band_count
    smoothed[0:EDGE, :] = jnp.zeros((EDGE, TILE), BF16)
    smoothed[EDGE + side :, :] = jnp.zeros((EDGE, TILE), BF16)
    for half in range(pair):
        for chunk in range(CHUNKS):
            first = EDGE + (half * CHUNKS + chunk) * chunk_rows
            smoothed[first : first + chunk_rows, :] = sources[chunk][half]
    for step in range(band_count):
        first = lax.rem(meta_ref[BAND] + step, band_count) * rows
        for inner in range(rows // TILE):
            source = pl.multiple_of(first + inner * TILE, TILE)
            filtered = jnp.dot(down_ref[...], smoothed[pl.ds(source, WINDOW), :], preferred_element_type=F32)
            powers[step][inner * TILE : (inner + 1) * TILE, :] = filtered * filtered


def power(sources, down_band, meta, band_count):
    side = CHUNKS * sources[0].shape[0] * sources[0].shape[1]
    return pl.pallas_call(
        functools.partial(power_kernel, band_count),
        out_shape=[jax.ShapeDtypeStruct((side // band_count, TILE), F32)] * band_count,
        grid_spec=pltpu.PrefetchScalarGridSpec(
            num_scalar_prefetch=1,
            grid=(1,),
            in_specs=[pl.BlockSpec(down_band.shape, lambda i, m: (0, 0))]
            + [pl.BlockSpec(array.shape, lambda i, m: (0, 0, 0)) for array in sources],
            out_specs=[pl.BlockSpec((side // band_count, TILE), lambda i, m: (0, 0))] * band_count,
            scratch_shapes=[pltpu.VMEM((side + 2 * EDGE, TILE), BF16)],
        ),
        cost_estimate=pl.CostEstimate(flops=side * TILE * 320, bytes_accessed=side * TILE * 6, transcendentals=0),
        compiler_params=pltpu.CompilerParams(vmem_limit_bytes=16 << 20),
        name="power",
    )(meta, down_band, *sources)


def body(exposures, inv_variance, mask_planes, sky_columns, basis_rows, basis_cols, match_coeffs, detect_taps):
    picture = exposures[0, 0]
    side = picture.shape[0]
    sky_count = lax.axis_size("sky")
    band_count = lax.axis_size("band")
    own_sky = lax.axis_index("sky")
    own_band = lax.axis_index("band")
    pair = 2
    line = sky_count // pair
    low = lax.rem(own_sky, pair)
    high = own_sky // pair
    half_rows = side // pair
    chunk_rows = half_rows // CHUNKS
    slots = jnp.arange(8, dtype=jnp.int32)
    meta = jnp.zeros((8,), jnp.int32)
    scalars = {START: sky_columns[own_sky, own_band, 0], OWN: low, OTHER: 1 - low, LINE: high, SKY: own_sky, BAND: own_band}
    for slot, value in scalars.items():
        meta = jnp.where(slots == slot, value, meta)

    def exchange(block, bit):
        return lax.ppermute(block, "sky", [(i, i ^ (1 << bit)) for i in range(sky_count)])

    def reduce_line(terms):
        rows = chunk_rows
        bit = 1
        while 1 << bit < sky_count:
            rows = rows // 2
            mine = lax.rem(own_sky >> bit, 2)
            leaving = sum(lax.dynamic_slice_in_dim(t, (1 - mine) * rows, rows, -2).astype(F32) for t in terms)
            arrived = exchange(leaving.astype(BF16), bit)
            terms = [lax.dynamic_slice_in_dim(t, mine * rows, rows, -2) for t in terms] + [arrived]
            bit += 1
        return terms

    def total(terms):
        return sum(t.astype(F32) for t in terms)

    words = mask_planes[0, 0]
    variance = inv_variance[0, 0]

    def weighing(halves, chunk):
        return weigh(variance, words, meta, halves, chunk, chunk_rows, sky_count)

    def matching(weight, which, half_slot, chunk):
        return match(
            picture, column_band, row_band, weight, which, meta, half_slot, chunk, half_rows, sky_count
        )

    weight_other = weighing((OTHER,), 0)
    weight_in = exchange(weight_other[0], 0)
    weight_both = weighing((OTHER, OWN), 1)
    both_terms = reduce_line([weight_both])
    column_band, row_band, across_band, down_band = prepare(
        match_coeffs[0, 0], basis_cols, basis_rows, detect_taps
    )
    weight_own = weighing((OWN,), 0)

    away, product_in, home, product_own = ([None] * CHUNKS for _ in range(4))
    for c in range(CHUNKS):
        away[c], product = matching(weight_both if c else weight_other, 0, OTHER, c)
        product_in[c] = exchange(product, 0)
    for c in range(CHUNKS):
        home[c], product_own[c] = matching(weight_both if c else weight_own, c, OWN, c)
    both_in = exchange(total([t[0] for t in both_terms]).astype(BF16), 0)
    denoms = [
        total(reduce_line([weight_own[0], weight_in])),
        total([t[1] for t in both_terms] + [both_in]),
    ]

    shifts = [[(i, (i // pair + step) % line * pair + i % pair) for i in range(sky_count)] for step in range(line)]
    smoothed = [None] * CHUNKS
    difference = None
    for c in range(CHUNKS):
        numer = total(reduce_line([product_own[c], product_in[c]]))
        if c:
            numer, _ = lax.optimization_barrier((numer, block))
        block = (numer / jnp.maximum(denoms[c], 1.0)).astype(BF16)
        near, far = [block], []
        far.append(exchange(block, 0))
        for step in range(1, line):
            near.append(lax.ppermute(block, "sky", shifts[step]))
        for step in range(1, line):
            far.append(exchange(near[step], 0))
        pieces = near + far
        smoothed[c] = smooth(pieces, across_band, meta, pair, chunk_rows, sky_count)
        difference = subtract([home[c], away[c]], pieces, meta, c, difference, sky_count)

    powers = power(smoothed, down_band, meta, band_count)
    detection = powers[0]
    for step in range(1, band_count):
        ring = [(i, (i + step) % band_count) for i in range(band_count)]
        detection = detection + lax.ppermute(powers[step], "band", ring)
    return (difference.reshape(1, 1, side, side), detection)


def solution(mesh):
    in_specs = (
        P("sky", "band", None, None),
        P("sky", "band", None, None),
        P("sky", "band", None, None),
        P(),
        P(),
        P(),
        P("sky", "band", None),
        P("band", None),
    )
    out_specs = (P("sky", "band", None, None), P("band", "sky"))

    return jax.shard_map(body, mesh=mesh, in_specs=in_specs, out_specs=out_specs, check_vma=False)
```

```python
import functools

import jax
import jax.numpy as jnp
from jax import lax
from jax.experimental import pallas as pl
from jax.experimental.pallas import tpu as pltpu
from jax.sharding import PartitionSpec as P


TILE = 128
NB = 9
TAPS = 25
DTAPS = 31
BITS = 30
EDGE = 16
WINDOW = TILE + 2 * EDGE
SHIFT = TILE // 2
CHUNKS = 2
OWN, OTHER = 0, 1
EARLY_GRANT = 60 << 20
F32 = jnp.float32
BF16 = jnp.bfloat16


def start_column(sky_ref):
    return sky_ref[lax.axis_index("sky"), lax.axis_index("band"), 0]


def half_of(which):
    low = lax.rem(lax.axis_index("sky"), 2)
    return low if which == OWN else 1 - low


def toeplitz(base_row, rows):
    wide = jnp.broadcast_to(base_row, (rows, base_row.shape[1]))
    return pltpu.roll(wide, 0, 1, stride=1, stride_axis=0)


def prepare_kernel(base_ref, column_ref, row_ref, across_ref, down_ref):
    for k in range(NB):
        column_ref[:, k * TILE : (k + 1) * TILE] = toeplitz(base_ref[k : k + 1, :], TILE).T.astype(BF16)
        row_ref[:, k * WINDOW : (k + 1) * WINDOW] = toeplitz(base_ref[NB + k : NB + k + 1, :], TILE)[
            :, :WINDOW
        ].astype(BF16)
    across_ref[...] = toeplitz(base_ref[2 * NB : 2 * NB + 1, :], TILE).T.astype(BF16)
    down_ref[...] = toeplitz(base_ref[2 * NB + 1 : 2 * NB + 2, :], TILE)[:, :WINDOW].astype(BF16)


def place_left(taps, offset):
    return jnp.pad(taps, ((0, 0), (offset, 2 * TILE - offset - taps.shape[1])))


def prepare(match_coeffs, basis_cols, basis_rows, detect_taps):
    column_taps = (match_coeffs[:, None] * basis_cols).astype(BF16).astype(F32)
    row_taps = basis_rows.astype(BF16).astype(F32)
    taps = detect_taps.astype(BF16).astype(F32)
    base = jnp.concatenate(
        [
            place_left(column_taps, SHIFT - TAPS // 2),
            place_left(row_taps, EDGE - TAPS // 2),
            place_left(taps, SHIFT - DTAPS // 2),
            place_left(taps, EDGE - DTAPS // 2),
        ],
        0,
    )
    return pl.pallas_call(
        prepare_kernel,
        out_shape=(
            jax.ShapeDtypeStruct((2 * TILE, NB * TILE), BF16),
            jax.ShapeDtypeStruct((TILE, NB * WINDOW), BF16),
            jax.ShapeDtypeStruct((2 * TILE, TILE), BF16),
            jax.ShapeDtypeStruct((TILE, WINDOW), BF16),
        ),
        compiler_params=pltpu.CompilerParams(vmem_limit_bytes=16 << 20),
        name="prepare",
    )(base)


def bad_bits(words_ref, plane, first_word, count, places):
    last = words_ref.shape[1] - 1
    word = jnp.full(places.shape, words_ref[plane, jnp.minimum(first_word, last)])
    begin = jnp.full(places.shape, first_word * BITS)
    for step in range(1, count):
        index = first_word + step
        reached = places >= index * BITS
        word = jnp.where(reached, words_ref[plane, jnp.minimum(index, last)], word)
        begin = jnp.where(reached, index * BITS, begin)
    return jnp.bitwise_and(jnp.right_shift(word, places - begin), 1)


def pick_half(index, halves):
    half = half_of(halves[0])
    for place in range(1, len(halves)):
        half = jnp.where(index == place, half_of(halves[place]), half)
    return half


def weight_kernel(sky_count, halves, chunk, sky_ref, words_ref, variance_ref, weight_ref):
    rows, side = variance_ref.shape
    start = start_column(sky_ref)
    first_row = (pick_half(pl.program_id(0), halves) * CHUNKS + chunk) * rows
    lanes = lax.broadcasted_iota(jnp.int32, (8, side), 1)
    column_bad = bad_bits(words_ref, 0, 0, words_ref.shape[1], lanes)[0:1, :]
    places = first_row + lax.broadcasted_iota(jnp.int32, (rows, TILE), 0)
    row_bad = bad_bits(words_ref, 1, first_row // BITS, rows // BITS + 2, places)
    if sky_count * TILE != side:
        weight_ref[...] = jnp.zeros_like(weight_ref)
    for tile in range(side // TILE):
        window = slice(tile * TILE, (tile + 1) * TILE)
        bad = row_bad + column_bad[:, window]
        kept = jnp.where(bad == 0, variance_ref[:, window].astype(F32), 0.0)
        target = lax.rem(start + tile, sky_count) * TILE
        weight_ref[0, :, pl.ds(pl.multiple_of(target, TILE), TILE)] = kept.astype(BF16)


def weigh(inv_variance, words, sky_columns, halves, chunk, rows, sky_count):
    side = inv_variance.shape[0]
    stripe = sky_count * TILE
    return pl.pallas_call(
        functools.partial(weight_kernel, sky_count, halves, chunk),
        out_shape=jax.ShapeDtypeStruct((len(halves), rows, stripe), BF16),
        grid_spec=pltpu.PrefetchScalarGridSpec(
            num_scalar_prefetch=2,
            grid=(len(halves),),
            in_specs=[pl.BlockSpec((rows, side), lambda i, m, w: (pick_half(i, halves) * CHUNKS + chunk, 0))],
            out_specs=pl.BlockSpec((1, rows, stripe), lambda i, m, w: (i, 0, 0)),
        ),
        cost_estimate=pl.CostEstimate(
            flops=len(halves) * rows * side * 8, bytes_accessed=len(halves) * rows * side * 4, transcendentals=0
        ),
        compiler_params=pltpu.CompilerParams(vmem_limit_bytes=EARLY_GRANT),
        name="weigh",
    )(sky_columns, words, inv_variance)


def match_kernel(
    sky_count,
    which,
    offset,
    half_blocks,
    sky_ref,
    above_ref,
    main_ref,
    below_ref,
    column_ref,
    row_ref,
    weight_ref,
    matched_ref,
    product_ref,
    windows,
    stacked,
):
    side = main_ref.shape[1]
    start = start_column(sky_ref)
    block = half_of(which) * half_blocks + offset + pl.program_id(0)
    last_block = side // TILE - 1
    nothing = jnp.zeros((TILE, SHIFT), BF16)

    def spread(values):
        edge = nothing[: values.shape[0]]
        return jnp.concatenate([edge, values, edge], axis=1)

    above, below = above_ref[...], below_ref[...]
    tiles = side // TILE
    parts = (
        (0, spread(jnp.where(block > 0, above, jnp.zeros_like(above)))),
        (EDGE, spread(main_ref[...])),
        (EDGE + TILE, spread(jnp.where(block < last_block, below, jnp.zeros_like(below)))),
    )
    for tile in range(tiles):
        for row, part in parts:
            row = tile * WINDOW + row
            windows[row : row + part.shape[0], :] = part[:, tile * TILE : (tile + 2) * TILE]
    for group in range(0, NB, 2):
        bands = range(group, min(group + 2, NB))
        passed = jnp.dot(
            windows[...], column_ref[:, group * TILE : (bands[-1] + 1) * TILE], preferred_element_type=F32
        ).astype(BF16)
        for k in bands:
            for tile in range(tiles):
                stacked[k * WINDOW : (k + 1) * WINDOW, tile * TILE : (tile + 1) * TILE] = passed[
                    tile * WINDOW : (tile + 1) * WINDOW, (k - group) * TILE : (k - group + 1) * TILE
                ]
    if sky_count != tiles:
        product_ref[...] = jnp.zeros_like(product_ref)
    for pair in range(tiles // 2):
        both = slice(pair * 2 * TILE, (pair + 1) * 2 * TILE)
        summed = jnp.dot(row_ref[...], stacked[:, both], preferred_element_type=F32).astype(BF16)
        matched_ref[:, both] = summed
        for part in range(2):
            target = pl.multiple_of(lax.rem(start + 2 * pair + part, sky_count) * TILE, TILE)
            weight = weight_ref[:, pl.ds(target, TILE)].astype(F32)
            product = weight * summed[:, part * TILE : (part + 1) * TILE].astype(F32)
            product_ref[:, pl.ds(target, TILE)] = product.astype(BF16)


def match(picture, column_band, row_band, weight, which_weight, sky_columns, which, chunk, half_rows, sky_count):
    side = picture.shape[0]
    chunk_rows = half_rows // CHUNKS
    steps = chunk_rows // TILE
    stripe = sky_count * TILE
    edges = TILE // EDGE

    def block(i):
        return (half_of(which) * CHUNKS + chunk) * steps + i

    return pl.pallas_call(
        functools.partial(match_kernel, sky_count, which, chunk * steps, CHUNKS * steps),
        out_shape=(
            jax.ShapeDtypeStruct((chunk_rows, side), BF16),
            jax.ShapeDtypeStruct((chunk_rows, stripe), BF16),
        ),
        grid_spec=pltpu.PrefetchScalarGridSpec(
            num_scalar_prefetch=1,
            grid=(steps,),
            in_specs=[
                pl.BlockSpec((EDGE, side), lambda i, m: (jnp.maximum(block(i) * edges - 1, 0), 0)),
                pl.BlockSpec((TILE, side), lambda i, m: (block(i), 0)),
                pl.BlockSpec((EDGE, side), lambda i, m: (jnp.minimum((block(i) + 1) * edges, side // EDGE - 1), 0)),
                pl.BlockSpec(column_band.shape, lambda i, m: (0, 0), pipeline_mode=pl.Buffered(1)),
                pl.BlockSpec(row_band.shape, lambda i, m: (0, 0), pipeline_mode=pl.Buffered(1)),
                pl.BlockSpec((None, TILE, stripe), lambda i, m: (which_weight, i, 0)),
            ],
            out_specs=(
                pl.BlockSpec((TILE, side), lambda i, m: (i, 0)),
                pl.BlockSpec((TILE, stripe), lambda i, m: (i, 0)),
            ),
            scratch_shapes=[
                pltpu.VMEM((side // TILE * WINDOW, 2 * TILE), BF16),
                pltpu.VMEM((NB * WINDOW, side), BF16),
            ],
        ),
        cost_estimate=pl.CostEstimate(
            flops=2 * chunk_rows * side * NB * (2 * TILE + WINDOW), bytes_accessed=chunk_rows * side * 8, transcendentals=0
        ),
        compiler_params=pltpu.CompilerParams(vmem_limit_bytes=EARLY_GRANT),
        name="match",
    )(sky_columns, picture, picture, picture, column_band, row_band, weight)


def row_of(place, line, chunk_rows):
    row = 0
    for bit in range(line.bit_length() - 1):
        row = row + lax.rem(place >> bit, 2) * (chunk_rows >> (bit + 1))
    return row


def piece_rows(step, line, chunk_rows, part_rows):
    row = row_of(lax.axis_index("sky") // 2 ^ step, line, chunk_rows)
    return pl.ds(pl.multiple_of(row, part_rows), part_rows)


def difference_kernel(sky_count, pair, line, sky_ref, *refs):
    matched = refs[:pair]
    pieces = refs[pair : pair + pair * line]
    out_ref = refs[-1]
    start = start_column(sky_ref)
    part_rows = pieces[0].shape[0]
    chunk_rows, side = matched[0].shape
    for group in range(pair):
        half = half_of((OWN, OTHER)[group])
        for step in range(line):
            rows = piece_rows(step, line, chunk_rows, part_rows)
            piece = pieces[group * line + step]
            for tile in range(side // TILE):
                window = slice(tile * TILE, (tile + 1) * TILE)
                source = pl.multiple_of(lax.rem(start + tile, sky_count) * TILE, TILE)
                picked = piece[:, pl.ds(source, TILE)].astype(F32)
                out_ref[half, 0, rows, window] = (matched[group][rows, window].astype(F32) - picked).astype(BF16)


def subtract(matched, pieces, sky_columns, chunk, before, sky_count):
    chunk_rows, side = matched[0].shape
    pair = len(matched)
    line = len(pieces) // pair
    operands = [*matched, *pieces]
    specs = [pl.BlockSpec(array.shape, lambda i, m: (0, 0)) for array in operands]
    aliases = {}
    if before is not None:
        operands.append(before)
        specs.append(pl.BlockSpec(memory_space=pl.ANY))
        aliases = {len(operands): 0}
    return pl.pallas_call(
        functools.partial(difference_kernel, sky_count, pair, line),
        out_shape=jax.ShapeDtypeStruct((pair, CHUNKS, chunk_rows, side), BF16),
        grid_spec=pltpu.PrefetchScalarGridSpec(
            num_scalar_prefetch=1,
            grid=(1,),
            in_specs=specs,
            out_specs=pl.BlockSpec((pair, 1, chunk_rows, side), lambda i, m: (0, chunk, 0, 0)),
        ),
        input_output_aliases=aliases,
        cost_estimate=pl.CostEstimate(
            flops=pair * chunk_rows * side, bytes_accessed=pair * chunk_rows * side * 6, transcendentals=0
        ),
        compiler_params=pltpu.CompilerParams(vmem_limit_bytes=24 << 20),
        name="subtract",
    )(sky_columns, *operands)


def smooth_kernel(sky_count, pair, line, sky_ref, across_ref, *refs):
    pieces, out_ref = refs[:-1], refs[-1]
    part_rows = pieces[0].shape[0]
    chunk_rows = out_ref.shape[1]

    def column(piece, away):
        source = lax.rem(lax.axis_index("sky") + away, sky_count) * TILE
        return piece[:, pl.ds(pl.multiple_of(source, TILE), TILE)]

    for group in range(pair):
        half = half_of((OWN, OTHER)[group])
        for step in range(line):
            rows = piece_rows(step, line, chunk_rows, part_rows)
            piece = pieces[group * line + step]
            window = jnp.concatenate(
                [column(piece, sky_count - 1)[:, SHIFT:], column(piece, 0), column(piece, 1)[:, :SHIFT]], axis=1
            )
            out_ref[half, rows, :] = jnp.dot(window, across_ref[...], preferred_element_type=F32).astype(BF16)


def smooth(pieces, across_band, sky_columns, pair, chunk_rows, sky_count):
    line = len(pieces) // pair
    operands = [across_band, *pieces]
    return pl.pallas_call(
        functools.partial(smooth_kernel, sky_count, pair, line),
        out_shape=jax.ShapeDtypeStruct((pair, chunk_rows, TILE), BF16),
        grid_spec=pltpu.PrefetchScalarGridSpec(
            num_scalar_prefetch=1,
            grid=(1,),
            in_specs=[pl.BlockSpec(array.shape, lambda i, m: (0, 0)) for array in operands],
            out_specs=pl.BlockSpec((pair, chunk_rows, TILE), lambda i, m: (0, 0, 0)),
        ),
        cost_estimate=pl.CostEstimate(
            flops=pair * chunk_rows * TILE * 512, bytes_accessed=pair * chunk_rows * sky_count * TILE * 2, transcendentals=0
        ),
        compiler_params=pltpu.CompilerParams(vmem_limit_bytes=20 << 20),
        name="smooth",
    )(sky_columns, *operands)


def power_kernel(band_count, sky_ref, down_ref, *refs):
    sources, powers, smoothed = refs[:CHUNKS], refs[CHUNKS : CHUNKS + band_count], refs[-1]
    pair, chunk_rows = sources[0].shape[:2]
    side = pair * CHUNKS * chunk_rows
    rows = side // band_count
    smoothed[0:EDGE, :] = jnp.zeros((EDGE, TILE), BF16)
    smoothed[EDGE + side :, :] = jnp.zeros((EDGE, TILE), BF16)
    for half in range(pair):
        for chunk in range(CHUNKS):
            first = EDGE + (half * CHUNKS + chunk) * chunk_rows
            smoothed[first : first + chunk_rows, :] = sources[chunk][half]
    for step in range(band_count):
        first = lax.rem(lax.axis_index("band") + step, band_count) * rows
        for inner in range(rows // TILE):
            source = pl.multiple_of(first + inner * TILE, TILE)
            filtered = jnp.dot(down_ref[...], smoothed[pl.ds(source, WINDOW), :], preferred_element_type=F32)
            powers[step][inner * TILE : (inner + 1) * TILE, :] = (filtered * filtered).astype(powers[step].dtype)


def power(sources, down_band, sky_columns, band_count):
    side = CHUNKS * sources[0].shape[0] * sources[0].shape[1]
    return pl.pallas_call(
        functools.partial(power_kernel, band_count),
        out_shape=[
            jax.ShapeDtypeStruct((side // band_count, TILE), BF16 if step else F32) for step in range(band_count)
        ],
        grid_spec=pltpu.PrefetchScalarGridSpec(
            num_scalar_prefetch=1,
            grid=(1,),
            in_specs=[pl.BlockSpec(down_band.shape, lambda i, m: (0, 0))]
            + [pl.BlockSpec(array.shape, lambda i, m: (0, 0, 0)) for array in sources],
            out_specs=[pl.BlockSpec((side // band_count, TILE), lambda i, m: (0, 0))] * band_count,
            scratch_shapes=[pltpu.VMEM((side + 2 * EDGE, TILE), BF16)],
        ),
        cost_estimate=pl.CostEstimate(flops=side * TILE * 320, bytes_accessed=side * TILE * 6, transcendentals=0),
        compiler_params=pltpu.CompilerParams(vmem_limit_bytes=16 << 20),
        name="power",
    )(sky_columns, down_band, *sources)


def body(exposures, inv_variance, mask_planes, sky_columns, basis_rows, basis_cols, match_coeffs, detect_taps):
    picture = exposures[0, 0]
    side = picture.shape[0]
    sky_count = lax.axis_size("sky")
    band_count = lax.axis_size("band")
    own_sky = lax.axis_index("sky")
    pair = 2
    line = sky_count // pair
    half_rows = side // pair
    chunk_rows = half_rows // CHUNKS

    def exchange(block, bit):
        return lax.ppermute(block, "sky", [(i, i ^ (1 << bit)) for i in range(sky_count)])

    def reduce_line(terms):
        rows = chunk_rows
        bit = 1
        while 1 << bit < sky_count:
            rows = rows // 2
            mine = lax.rem(own_sky >> bit, 2)
            leaving = sum(lax.dynamic_slice_in_dim(t, (1 - mine) * rows, rows, -2).astype(F32) for t in terms)
            arrived = exchange(leaving.astype(BF16), bit)
            terms = [lax.dynamic_slice_in_dim(t, mine * rows, rows, -2) for t in terms] + [arrived]
            bit += 1
        return terms

    def total(terms):
        return sum(t.astype(F32) for t in terms)

    words = mask_planes[0, 0]
    variance = inv_variance[0, 0]

    def weighing(halves, chunk):
        return weigh(variance, words, sky_columns, halves, chunk, chunk_rows, sky_count)

    def matching(weight, which, half_slot, chunk):
        return match(
            picture, column_band, row_band, weight, which, sky_columns, half_slot, chunk, half_rows, sky_count
        )

    weight_other = weighing((OTHER,), 0)
    weight_in = exchange(weight_other[0], 0)
    weight_both = weighing((OTHER, OWN), 1)
    both_terms = reduce_line([weight_both])
    column_band, row_band, across_band, down_band = prepare(
        match_coeffs[0, 0], basis_cols, basis_rows, detect_taps
    )
    weight_own = weighing((OWN,), 0)

    away, product_in, home, product_own = ([None] * CHUNKS for _ in range(4))
    for c in range(CHUNKS):
        away[c], product = matching(weight_both if c else weight_other, 0, OTHER, c)
        product_in[c] = exchange(product, 0)
    for c in range(CHUNKS):
        home[c], product_own[c] = matching(weight_both if c else weight_own, c, OWN, c)
    both_in = exchange(total([t[0] for t in both_terms]).astype(BF16), 0)
    denoms = [
        total(reduce_line([weight_own[0], weight_in])),
        total([t[1] for t in both_terms] + [both_in]),
    ]

    smoothed = [None] * CHUNKS
    difference = None
    for c in range(CHUNKS):
        numer = total(reduce_line([product_own[c], product_in[c]]))
        if c:
            numer, _ = lax.optimization_barrier((numer, block))
        block = (numer / jnp.maximum(denoms[c], 1.0)).astype(BF16)
        near, far = {0: block}, {}
        far[0] = exchange(block, 0)
        for bit in reversed(range(line.bit_length() - 1)):
            for held in list(near):
                step = held | 1 << bit
                near[step] = exchange(near[held], bit + 1)
        for step in range(1, line):
            far[step] = exchange(near[step], 0)
        pieces = [near[step] for step in range(line)] + [far[step] for step in range(line)]
        smoothed[c] = smooth(pieces, across_band, sky_columns, pair, chunk_rows, sky_count)
        difference = subtract([home[c], away[c]], pieces, sky_columns, c, difference, sky_count)

    powers = power(smoothed, down_band, sky_columns, band_count)
    detection = powers[0]
    for step in range(1, band_count):
        ring = [(i, (i + step) % band_count) for i in range(band_count)]
        detection = detection + lax.ppermute(powers[step], "band", ring).astype(F32)
    return (difference.reshape(1, 1, side, side), detection)


def solution(mesh):
    in_specs = (
        P("sky", "band", None, None),
        P("sky", "band", None, None),
        P("sky", "band", None, None),
        P(),
        P(),
        P(),
        P("sky", "band", None),
        P("band", None),
    )
    out_specs = (P("sky", "band", None, None), P("band", "sky"))

    return jax.shard_map(body, mesh=mesh, in_specs=in_specs, out_specs=out_specs, check_vma=False)
```

```python
import functools

import jax
import jax.numpy as jnp
from jax import lax
from jax.experimental import pallas as pl
from jax.experimental.pallas import tpu as pltpu
from jax.sharding import PartitionSpec as P


TILE = 128
NB = 9
TAPS = 25
DTAPS = 31
BITS = 30
EDGE = 16
WINDOW = TILE + 2 * EDGE
SHIFT = TILE // 2
CHUNKS = 2
OWN, OTHER = 0, 1
EARLY_GRANT = 20 << 20
LATE_GRANT = 24 << 20
F32 = jnp.float32
BF16 = jnp.bfloat16


def in_hbm(array):
    return pltpu.with_memory_space_constraint(array, pltpu.HBM)


def start_column(sky_ref):
    return sky_ref[lax.axis_index("sky"), lax.axis_index("band"), 0]


def half_of(which):
    low = lax.rem(lax.axis_index("sky"), 2)
    return low if which == OWN else 1 - low


def toeplitz(base_row, rows):
    wide = jnp.broadcast_to(base_row, (rows, base_row.shape[1]))
    return pltpu.roll(wide, 0, 1, stride=1, stride_axis=0)


def prepare_kernel(base_ref, column_ref, row_ref, across_ref, down_ref):
    for k in range(NB):
        column_ref[:, k * TILE : (k + 1) * TILE] = toeplitz(base_ref[k : k + 1, :], TILE).T.astype(BF16)
        row_ref[:, k * WINDOW : (k + 1) * WINDOW] = toeplitz(base_ref[NB + k : NB + k + 1, :], TILE)[
            :, :WINDOW
        ].astype(BF16)
    across_ref[...] = toeplitz(base_ref[2 * NB : 2 * NB + 1, :], TILE).T.astype(BF16)
    down_ref[...] = toeplitz(base_ref[2 * NB + 1 : 2 * NB + 2, :], TILE)[:, :WINDOW].astype(BF16)


def place_left(taps, offset):
    return jnp.pad(taps, ((0, 0), (offset, 2 * TILE - offset - taps.shape[1])))


def prepare(match_coeffs, basis_cols, basis_rows, detect_taps):
    column_taps = (match_coeffs[:, None] * basis_cols).astype(BF16).astype(F32)
    row_taps = basis_rows.astype(BF16).astype(F32)
    taps = detect_taps.astype(BF16).astype(F32)
    base = jnp.concatenate(
        [
            place_left(column_taps, SHIFT - TAPS // 2),
            place_left(row_taps, EDGE - TAPS // 2),
            place_left(taps, SHIFT - DTAPS // 2),
            place_left(taps, EDGE - DTAPS // 2),
        ],
        0,
    )
    return pl.pallas_call(
        prepare_kernel,
        out_shape=(
            jax.ShapeDtypeStruct((2 * TILE, NB * TILE), BF16),
            jax.ShapeDtypeStruct((TILE, NB * WINDOW), BF16),
            jax.ShapeDtypeStruct((2 * TILE, TILE), BF16),
            jax.ShapeDtypeStruct((TILE, WINDOW), BF16),
        ),
        compiler_params=pltpu.CompilerParams(vmem_limit_bytes=16 << 20),
        name="prepare",
    )(base)


def bad_bits(words_ref, plane, first_word, count, places):
    last = words_ref.shape[1] - 1
    word = jnp.full(places.shape, words_ref[plane, jnp.minimum(first_word, last)])
    begin = jnp.full(places.shape, first_word * BITS)
    for step in range(1, count):
        index = first_word + step
        reached = places >= index * BITS
        word = jnp.where(reached, words_ref[plane, jnp.minimum(index, last)], word)
        begin = jnp.where(reached, index * BITS, begin)
    return jnp.bitwise_and(jnp.right_shift(word, places - begin), 1)


def pick_block(index, halves, chunk, blocks):
    half = half_of(halves[0])
    for place in range(1, len(halves)):
        half = jnp.where(index >= place * blocks, half_of(halves[place]), half)
    return (half * CHUNKS + chunk) * blocks + lax.rem(index, blocks)


def weight_kernel(sky_count, halves, chunk, blocks, sky_ref, words_ref, variance_ref, weight_ref):
    rows, side = variance_ref.shape
    start = start_column(sky_ref)
    first_row = pick_block(pl.program_id(0), halves, chunk, blocks) * rows
    lanes = lax.broadcasted_iota(jnp.int32, (8, side), 1)
    column_bad = bad_bits(words_ref, 0, 0, words_ref.shape[1], lanes)[0:1, :]
    places = first_row + lax.broadcasted_iota(jnp.int32, (rows, TILE), 0)
    row_bad = bad_bits(words_ref, 1, first_row // BITS, rows // BITS + 2, places)
    if sky_count * TILE != side:
        weight_ref[...] = jnp.zeros_like(weight_ref)
    for tile in range(side // TILE):
        window = slice(tile * TILE, (tile + 1) * TILE)
        bad = row_bad + column_bad[:, window]
        kept = jnp.where(bad == 0, variance_ref[:, window].astype(F32), 0.0)
        target = lax.rem(start + tile, sky_count) * TILE
        weight_ref[0, :, pl.ds(pl.multiple_of(target, TILE), TILE)] = kept.astype(BF16)


def weigh(inv_variance, words, sky_columns, halves, chunk, chunk_rows, sky_count):
    side = inv_variance.shape[0]
    stripe = sky_count * TILE
    rows = min(TILE, chunk_rows)
    blocks = chunk_rows // rows
    return pl.pallas_call(
        functools.partial(weight_kernel, sky_count, halves, chunk, blocks),
        out_shape=jax.ShapeDtypeStruct((len(halves), chunk_rows, stripe), BF16),
        grid_spec=pltpu.PrefetchScalarGridSpec(
            num_scalar_prefetch=2,
            grid=(len(halves) * blocks,),
            in_specs=[pl.BlockSpec((rows, side), lambda i, m, w: (pick_block(i, halves, chunk, blocks), 0))],
            out_specs=pl.BlockSpec((1, rows, stripe), lambda i, m, w: (i // blocks, lax.rem(i, blocks), 0)),
        ),
        cost_estimate=pl.CostEstimate(
            flops=len(halves) * chunk_rows * side * 8,
            bytes_accessed=len(halves) * chunk_rows * side * 4,
            transcendentals=0,
        ),
        compiler_params=pltpu.CompilerParams(vmem_limit_bytes=EARLY_GRANT),
        name="weigh",
    )(in_hbm(sky_columns), in_hbm(words), in_hbm(inv_variance))


def match_kernel(
    sky_count,
    which,
    offset,
    half_blocks,
    sky_ref,
    above_ref,
    main_ref,
    below_ref,
    column_ref,
    row_ref,
    weight_ref,
    matched_ref,
    product_ref,
    windows,
    stacked,
):
    side = main_ref.shape[1]
    start = start_column(sky_ref)
    block = half_of(which) * half_blocks + offset + pl.program_id(0)
    last_block = side // TILE - 1
    nothing = jnp.zeros((TILE, SHIFT), BF16)

    def spread(values):
        edge = nothing[: values.shape[0]]
        return jnp.concatenate([edge, values, edge], axis=1)

    above, below = above_ref[...], below_ref[...]
    tiles = side // TILE
    parts = (
        (0, spread(jnp.where(block > 0, above, jnp.zeros_like(above)))),
        (EDGE, spread(main_ref[...])),
        (EDGE + TILE, spread(jnp.where(block < last_block, below, jnp.zeros_like(below)))),
    )
    for tile in range(tiles):
        for row, part in parts:
            row = tile * WINDOW + row
            windows[row : row + part.shape[0], :] = part[:, tile * TILE : (tile + 2) * TILE]
    for group in range(0, NB, 2):
        bands = range(group, min(group + 2, NB))
        passed = jnp.dot(
            windows[...], column_ref[:, group * TILE : (bands[-1] + 1) * TILE], preferred_element_type=F32
        ).astype(BF16)
        for k in bands:
            for tile in range(tiles):
                stacked[k * WINDOW : (k + 1) * WINDOW, tile * TILE : (tile + 1) * TILE] = passed[
                    tile * WINDOW : (tile + 1) * WINDOW, (k - group) * TILE : (k - group + 1) * TILE
                ]
    if sky_count != tiles:
        product_ref[...] = jnp.zeros_like(product_ref)
    for pair in range(tiles // 2):
        both = slice(pair * 2 * TILE, (pair + 1) * 2 * TILE)
        summed = jnp.dot(row_ref[...], stacked[:, both], preferred_element_type=F32).astype(BF16)
        matched_ref[:, both] = summed
        for part in range(2):
            target = pl.multiple_of(lax.rem(start + 2 * pair + part, sky_count) * TILE, TILE)
            weight = weight_ref[:, pl.ds(target, TILE)].astype(F32)
            product = weight * summed[:, part * TILE : (part + 1) * TILE].astype(F32)
            product_ref[:, pl.ds(target, TILE)] = product.astype(BF16)


def match(picture, column_band, row_band, weight, which_weight, sky_columns, which, chunk, half_rows, sky_count):
    side = picture.shape[0]
    chunk_rows = half_rows // CHUNKS
    steps = chunk_rows // TILE
    stripe = sky_count * TILE
    edges = TILE // EDGE

    def block(i):
        return (half_of(which) * CHUNKS + chunk) * steps + i

    return pl.pallas_call(
        functools.partial(match_kernel, sky_count, which, chunk * steps, CHUNKS * steps),
        out_shape=(
            pltpu.HBM((chunk_rows, side), BF16),
            pltpu.HBM((chunk_rows, stripe), BF16)
            if which == OTHER
            else jax.ShapeDtypeStruct((chunk_rows, stripe), BF16),
        ),
        grid_spec=pltpu.PrefetchScalarGridSpec(
            num_scalar_prefetch=1,
            grid=(steps,),
            in_specs=[
                pl.BlockSpec((EDGE, side), lambda i, m: (jnp.maximum(block(i) * edges - 1, 0), 0)),
                pl.BlockSpec((TILE, side), lambda i, m: (block(i), 0)),
                pl.BlockSpec((EDGE, side), lambda i, m: (jnp.minimum((block(i) + 1) * edges, side // EDGE - 1), 0)),
                pl.BlockSpec(column_band.shape, lambda i, m: (0, 0), pipeline_mode=pl.Buffered(1)),
                pl.BlockSpec(row_band.shape, lambda i, m: (0, 0), pipeline_mode=pl.Buffered(1)),
                pl.BlockSpec((None, TILE, stripe), lambda i, m: (which_weight, i, 0)),
            ],
            out_specs=(
                pl.BlockSpec((TILE, side), lambda i, m: (i, 0)),
                pl.BlockSpec((TILE, stripe), lambda i, m: (i, 0)),
            ),
            scratch_shapes=[
                pltpu.VMEM((side // TILE * WINDOW, 2 * TILE), BF16),
                pltpu.VMEM((NB * WINDOW, side), BF16),
            ],
        ),
        cost_estimate=pl.CostEstimate(
            flops=2 * chunk_rows * side * NB * (2 * TILE + WINDOW), bytes_accessed=chunk_rows * side * 8, transcendentals=0
        ),
        compiler_params=pltpu.CompilerParams(vmem_limit_bytes=EARLY_GRANT),
        name="match",
    )(in_hbm(sky_columns), *[in_hbm(picture)] * 3, column_band, row_band, weight)


def row_of(place, line, chunk_rows):
    row = 0
    for bit in range(line.bit_length() - 1):
        row = row + lax.rem(place >> bit, 2) * (chunk_rows >> (bit + 1))
    return row


def piece_rows(step, line, chunk_rows, part_rows):
    row = row_of(lax.axis_index("sky") // 2 ^ step, line, chunk_rows)
    return pl.ds(pl.multiple_of(row, part_rows), part_rows)


def difference_kernel(sky_count, pair, line, sky_ref, *refs):
    matched = refs[:pair]
    pieces = refs[pair : pair + pair * line]
    out_ref = refs[-1]
    start = start_column(sky_ref)
    part_rows = pieces[0].shape[0]
    chunk_rows, side = matched[0].shape
    for group in range(pair):
        half = half_of((OWN, OTHER)[group])
        for step in range(line):
            rows = piece_rows(step, line, chunk_rows, part_rows)
            piece = pieces[group * line + step]
            for tile in range(side // TILE):
                window = slice(tile * TILE, (tile + 1) * TILE)
                source = pl.multiple_of(lax.rem(start + tile, sky_count) * TILE, TILE)
                picked = piece[:, pl.ds(source, TILE)].astype(F32)
                out_ref[half, 0, rows, window] = (matched[group][rows, window].astype(F32) - picked).astype(BF16)


def subtract(matched, pieces, sky_columns, chunk, before, sky_count):
    chunk_rows, side = matched[0].shape
    pair = len(matched)
    line = len(pieces) // pair
    operands = [*matched, *pieces]
    specs = [pl.BlockSpec(array.shape, lambda i, m: (0, 0)) for array in operands]
    aliases = {}
    if before is not None:
        operands.append(before)
        specs.append(pl.BlockSpec(memory_space=pl.ANY))
        aliases = {len(operands): 0}
    return pl.pallas_call(
        functools.partial(difference_kernel, sky_count, pair, line),
        out_shape=jax.ShapeDtypeStruct((pair, CHUNKS, chunk_rows, side), BF16),
        grid_spec=pltpu.PrefetchScalarGridSpec(
            num_scalar_prefetch=1,
            grid=(1,),
            in_specs=specs,
            out_specs=pl.BlockSpec((pair, 1, chunk_rows, side), lambda i, m: (0, chunk, 0, 0)),
        ),
        input_output_aliases=aliases,
        cost_estimate=pl.CostEstimate(
            flops=pair * chunk_rows * side, bytes_accessed=pair * chunk_rows * side * 6, transcendentals=0
        ),
        compiler_params=pltpu.CompilerParams(vmem_limit_bytes=24 << 20),
        name="subtract",
    )(in_hbm(sky_columns), *operands)


def smooth_pieces(sky_count, line, across, pieces, chunk_rows, store):
    def column(piece, away):
        source = lax.rem(lax.axis_index("sky") + away, sky_count) * TILE
        return piece[:, pl.ds(pl.multiple_of(source, TILE), TILE)]

    for group in range(len(pieces) // line):
        for step in range(line):
            piece = pieces[group * line + step]
            window = jnp.concatenate(
                [column(piece, sky_count - 1)[:, SHIFT:], column(piece, 0), column(piece, 1)[:, :SHIFT]], axis=1
            )
            row = row_of(lax.axis_index("sky") // 2 ^ step, line, chunk_rows)
            store(half_of((OWN, OTHER)[group]), row, jnp.dot(window, across, preferred_element_type=F32).astype(BF16))


def smooth_kernel(sky_count, line, sky_ref, across_ref, *refs):
    pieces, out_ref = refs[:-1], refs[-1]
    part_rows, chunk_rows = pieces[0].shape[0], out_ref.shape[1]

    def store(half, row, values):
        out_ref[half, pl.ds(pl.multiple_of(row, part_rows), part_rows), :] = values

    smooth_pieces(sky_count, line, across_ref[...], pieces, chunk_rows, store)


def smooth(pieces, across_band, sky_columns, pair, chunk_rows, sky_count):
    line = len(pieces) // pair
    operands = [across_band, *pieces]
    return pl.pallas_call(
        functools.partial(smooth_kernel, sky_count, line),
        out_shape=jax.ShapeDtypeStruct((pair, chunk_rows, TILE), BF16),
        grid_spec=pltpu.PrefetchScalarGridSpec(
            num_scalar_prefetch=1,
            grid=(1,),
            in_specs=[pl.BlockSpec(array.shape, lambda i, m: (0, 0)) for array in operands],
            out_specs=pl.BlockSpec((pair, chunk_rows, TILE), lambda i, m: (0, 0, 0)),
        ),
        cost_estimate=pl.CostEstimate(
            flops=pair * chunk_rows * TILE * 512, bytes_accessed=pair * chunk_rows * sky_count * TILE * 2, transcendentals=0
        ),
        compiler_params=pltpu.CompilerParams(vmem_limit_bytes=LATE_GRANT),
        name="smooth",
    )(in_hbm(sky_columns), *operands)


def power_kernel(sky_count, line, band_count, sky_ref, across_ref, down_ref, *refs):
    sources = refs[: CHUNKS - 1]
    pieces = refs[CHUNKS - 1 : -band_count - 1]
    powers, smoothed = refs[-band_count - 1 : -1], refs[-1]
    part_rows = pieces[0].shape[0]
    pair = len(pieces) // line
    chunk_rows = part_rows * line
    side = pair * CHUNKS * chunk_rows
    rows = side // band_count
    smoothed[0:EDGE, :] = jnp.zeros((EDGE, TILE), BF16)
    smoothed[EDGE + side :, :] = jnp.zeros((EDGE, TILE), BF16)
    for half in range(pair):
        for chunk in range(CHUNKS - 1):
            first = EDGE + (half * CHUNKS + chunk) * chunk_rows
            smoothed[first : first + chunk_rows, :] = sources[chunk][half]

    def store(half, row, values):
        first = EDGE + (half * CHUNKS + CHUNKS - 1) * chunk_rows + row
        smoothed[pl.ds(pl.multiple_of(first, EDGE), part_rows), :] = values

    smooth_pieces(sky_count, line, across_ref[...], pieces, chunk_rows, store)
    for step in range(band_count):
        first = lax.rem(lax.axis_index("band") + step, band_count) * rows
        for inner in range(rows // TILE):
            source = pl.multiple_of(first + inner * TILE, TILE)
            filtered = jnp.dot(down_ref[...], smoothed[pl.ds(source, WINDOW), :], preferred_element_type=F32)
            powers[step][inner * TILE : (inner + 1) * TILE, :] = (filtered * filtered).astype(powers[step].dtype)


def power(sources, pieces, across_band, down_band, sky_columns, pair, sky_count, band_count):
    line = len(pieces) // pair
    side = CHUNKS * pair * line * pieces[0].shape[0]
    operands = [across_band, down_band, *sources, *pieces]
    return pl.pallas_call(
        functools.partial(power_kernel, sky_count, line, band_count),
        out_shape=[
            jax.ShapeDtypeStruct((side // band_count, TILE), BF16 if step else F32) for step in range(band_count)
        ],
        grid_spec=pltpu.PrefetchScalarGridSpec(
            num_scalar_prefetch=1,
            grid=(1,),
            in_specs=[pl.BlockSpec(array.shape, lambda i, m, n=array.ndim: (0,) * n) for array in operands],
            out_specs=[pl.BlockSpec((side // band_count, TILE), lambda i, m: (0, 0))] * band_count,
            scratch_shapes=[pltpu.VMEM((side + 2 * EDGE, TILE), BF16)],
        ),
        cost_estimate=pl.CostEstimate(flops=side * TILE * 600, bytes_accessed=side * TILE * 12, transcendentals=0),
        compiler_params=pltpu.CompilerParams(vmem_limit_bytes=LATE_GRANT),
        name="power",
    )(in_hbm(sky_columns), *operands)


def body(exposures, inv_variance, mask_planes, sky_columns, basis_rows, basis_cols, match_coeffs, detect_taps):
    picture = exposures[0, 0]
    side = picture.shape[0]
    sky_count = lax.axis_size("sky")
    band_count = lax.axis_size("band")
    own_sky = lax.axis_index("sky")
    pair = 2
    line = sky_count // pair
    half_rows = side // pair
    chunk_rows = half_rows // CHUNKS

    def exchange(block, bit):
        return lax.ppermute(block, "sky", [(i, i ^ (1 << bit)) for i in range(sky_count)])

    def reduce_line(terms):
        rows = chunk_rows
        bit = 1
        while 1 << bit < sky_count:
            rows = rows // 2
            mine = lax.rem(own_sky >> bit, 2)
            leaving = sum(lax.dynamic_slice_in_dim(t, (1 - mine) * rows, rows, -2).astype(F32) for t in terms)
            arrived = exchange(leaving.astype(BF16), bit)
            terms = [lax.dynamic_slice_in_dim(t, mine * rows, rows, -2) for t in terms] + [arrived]
            bit += 1
        return terms

    def total(terms):
        return sum(t.astype(F32) for t in terms)

    words = mask_planes[0, 0]
    variance = inv_variance[0, 0]

    def weighing(halves, chunk):
        return weigh(variance, words, sky_columns, halves, chunk, chunk_rows, sky_count)

    def matching(weight, which, half_slot, chunk):
        return match(
            picture, column_band, row_band, weight, which, sky_columns, half_slot, chunk, half_rows, sky_count
        )

    weight_other = weighing((OTHER,), 0)
    weight_in = exchange(weight_other[0], 0)
    weight_both = weighing((OTHER, OWN), 1)
    both_terms = reduce_line([weight_both])
    column_band, row_band, across_band, down_band = prepare(
        match_coeffs[0, 0], basis_cols, basis_rows, detect_taps
    )
    weight_own = weighing((OWN,), 0)

    away, product_in, home, product_own = ([None] * CHUNKS for _ in range(4))
    for c in range(CHUNKS):
        away[c], product = matching(weight_both if c else weight_other, 0, OTHER, c)
        product_in[c] = exchange(product, 0)
    for c in range(CHUNKS):
        home[c], product_own[c] = matching(weight_both if c else weight_own, c, OWN, c)
    both_in = exchange(total([t[0] for t in both_terms]).astype(BF16), 0)
    denoms = [
        total(reduce_line([weight_own[0], weight_in])),
        total([t[1] for t in both_terms] + [both_in]),
    ]

    smoothed = [None] * CHUNKS
    difference = None
    for c in range(CHUNKS):
        numer = total(reduce_line([product_own[c], product_in[c]]))
        if c:
            numer, _ = lax.optimization_barrier((numer, block))
        block = (numer / jnp.maximum(denoms[c], 1.0)).astype(BF16)
        near, far = {0: block}, {}
        far[0] = exchange(block, 0)
        for bit in reversed(range(line.bit_length() - 1)):
            for held in list(near):
                step = held | 1 << bit
                near[step] = exchange(near[held], bit + 1)
        for step in range(1, line):
            far[step] = exchange(near[step], 0)
        pieces = [near[step] for step in range(line)] + [far[step] for step in range(line)]
        if c < CHUNKS - 1:
            smoothed[c] = smooth(pieces, across_band, sky_columns, pair, chunk_rows, sky_count)
        else:
            powers = power(
                smoothed[:-1], pieces, across_band, down_band, sky_columns, pair, sky_count, band_count
            )
        difference = subtract([home[c], away[c]], pieces, sky_columns, c, difference, sky_count)

    detection = powers[0]
    for step in range(1, band_count):
        ring = [(i, (i + step) % band_count) for i in range(band_count)]
        detection = detection + lax.ppermute(powers[step], "band", ring).astype(F32)
    return (difference.reshape(1, 1, side, side), detection)


def solution(mesh):
    in_specs = (
        P("sky", "band", None, None),
        P("sky", "band", None, None),
        P("sky", "band", None, None),
        P(),
        P(),
        P(),
        P("sky", "band", None),
        P("band", None),
    )
    out_specs = (P("sky", "band", None, None), P("band", "sky"))

    return jax.shard_map(body, mesh=mesh, in_specs=in_specs, out_specs=out_specs, check_vma=False)
```

```python
import functools

import jax
import jax.numpy as jnp
from jax import lax
from jax.experimental import pallas as pl
from jax.experimental.pallas import tpu as pltpu
from jax.sharding import PartitionSpec as P


TILE = 128
NB = 9
TAPS = 25
DTAPS = 31
BITS = 30
EDGE = 16
WINDOW = TILE + 2 * EDGE
SHIFT = TILE // 2
CHUNKS = 2
OWN, OTHER = 0, 1
EARLY_GRANT = 20 << 20
LATE_GRANT = 24 << 20
SCALARS = pl.BlockSpec(memory_space=pltpu.SMEM)
F32 = jnp.float32
BF16 = jnp.bfloat16


def in_hbm(array):
    return pltpu.with_memory_space_constraint(array, pltpu.HBM)


def start_column(sky_ref):
    return sky_ref[lax.axis_index("sky"), lax.axis_index("band"), 0]


def half_of(which):
    low = lax.rem(lax.axis_index("sky"), 2)
    return low if which == OWN else 1 - low


def toeplitz(base_row, rows):
    wide = jnp.broadcast_to(base_row, (rows, base_row.shape[1]))
    return pltpu.roll(wide, 0, 1, stride=1, stride_axis=0)


def prepare_kernel(base_ref, column_ref, row_ref, across_ref, down_ref):
    for k in range(NB):
        column_ref[:, k * TILE : (k + 1) * TILE] = toeplitz(base_ref[k : k + 1, :], TILE).T.astype(BF16)
        row_ref[:, k * WINDOW : (k + 1) * WINDOW] = toeplitz(base_ref[NB + k : NB + k + 1, :], TILE)[
            :, :WINDOW
        ].astype(BF16)
    across_ref[...] = toeplitz(base_ref[2 * NB : 2 * NB + 1, :], TILE).T.astype(BF16)
    down_ref[...] = toeplitz(base_ref[2 * NB + 1 : 2 * NB + 2, :], TILE)[:, :WINDOW].astype(BF16)


def place_left(taps, offset):
    return jnp.pad(taps, ((0, 0), (offset, 2 * TILE - offset - taps.shape[1])))


def prepare(match_coeffs, basis_cols, basis_rows, detect_taps):
    column_taps = (match_coeffs[:, None] * basis_cols).astype(BF16).astype(F32)
    row_taps = basis_rows.astype(BF16).astype(F32)
    taps = detect_taps.astype(BF16).astype(F32)
    base = jnp.concatenate(
        [
            place_left(column_taps, SHIFT - TAPS // 2),
            place_left(row_taps, EDGE - TAPS // 2),
            place_left(taps, SHIFT - DTAPS // 2),
            place_left(taps, EDGE - DTAPS // 2),
        ],
        0,
    )
    return pl.pallas_call(
        prepare_kernel,
        out_shape=(
            jax.ShapeDtypeStruct((2 * TILE, NB * TILE), BF16),
            jax.ShapeDtypeStruct((TILE, NB * WINDOW), BF16),
            jax.ShapeDtypeStruct((2 * TILE, TILE), BF16),
            jax.ShapeDtypeStruct((TILE, WINDOW), BF16),
        ),
        compiler_params=pltpu.CompilerParams(vmem_limit_bytes=16 << 20),
        name="prepare",
    )(base)


def bad_bits(words_ref, plane, first_word, count, places):
    last = words_ref.shape[1] - 1
    word = jnp.full(places.shape, words_ref[plane, jnp.minimum(first_word, last)])
    begin = jnp.full(places.shape, first_word * BITS)
    for step in range(1, count):
        index = first_word + step
        reached = places >= index * BITS
        word = jnp.where(reached, words_ref[plane, jnp.minimum(index, last)], word)
        begin = jnp.where(reached, index * BITS, begin)
    return jnp.bitwise_and(jnp.right_shift(word, places - begin), 1)


def pick_block(index, halves, chunk, blocks):
    half = half_of(halves[0])
    for place in range(1, len(halves)):
        half = jnp.where(index >= place * blocks, half_of(halves[place]), half)
    return (half * CHUNKS + chunk) * blocks + lax.rem(index, blocks)


def weight_kernel(sky_count, halves, chunk, blocks, sky_ref, words_ref, variance_ref, weight_ref):
    rows, side = variance_ref.shape
    start = start_column(sky_ref)
    first_row = pick_block(pl.program_id(0), halves, chunk, blocks) * rows
    lanes = lax.broadcasted_iota(jnp.int32, (8, side), 1)
    column_bad = bad_bits(words_ref, 0, 0, words_ref.shape[1], lanes)[0:1, :]
    places = first_row + lax.broadcasted_iota(jnp.int32, (rows, TILE), 0)
    row_bad = bad_bits(words_ref, 1, first_row // BITS, rows // BITS + 2, places)
    if sky_count * TILE != side:
        weight_ref[...] = jnp.zeros_like(weight_ref)
    for tile in range(side // TILE):
        window = slice(tile * TILE, (tile + 1) * TILE)
        bad = row_bad + column_bad[:, window]
        kept = jnp.where(bad == 0, variance_ref[:, window].astype(F32), 0.0)
        target = lax.rem(start + tile, sky_count) * TILE
        weight_ref[0, :, pl.ds(pl.multiple_of(target, TILE), TILE)] = kept.astype(BF16)


def weigh(inv_variance, words, sky_columns, halves, chunk, chunk_rows, sky_count):
    side = inv_variance.shape[0]
    stripe = sky_count * TILE
    rows = min(TILE, chunk_rows)
    blocks = chunk_rows // rows
    return pl.pallas_call(
        functools.partial(weight_kernel, sky_count, halves, chunk, blocks),
        out_shape=jax.ShapeDtypeStruct((len(halves), chunk_rows, stripe), BF16),
        grid_spec=pltpu.PrefetchScalarGridSpec(
            num_scalar_prefetch=0,
            grid=(len(halves) * blocks,),
            in_specs=[SCALARS, SCALARS, pl.BlockSpec((rows, side), lambda i: (pick_block(i, halves, chunk, blocks), 0))],
            out_specs=pl.BlockSpec((1, rows, stripe), lambda i: (i // blocks, lax.rem(i, blocks), 0)),
        ),
        cost_estimate=pl.CostEstimate(
            flops=len(halves) * chunk_rows * side * 8,
            bytes_accessed=len(halves) * chunk_rows * side * 4,
            transcendentals=0,
        ),
        compiler_params=pltpu.CompilerParams(vmem_limit_bytes=EARLY_GRANT),
        name="weigh",
    )(in_hbm(sky_columns), in_hbm(words), in_hbm(inv_variance))


def match_kernel(
    sky_count,
    which,
    offset,
    half_blocks,
    sky_ref,
    above_ref,
    main_ref,
    below_ref,
    column_ref,
    row_ref,
    weight_ref,
    matched_ref,
    product_ref,
    windows,
    stacked,
):
    side = main_ref.shape[1]
    start = start_column(sky_ref)
    block = half_of(which) * half_blocks + offset + pl.program_id(0)
    last_block = side // TILE - 1
    nothing = jnp.zeros((TILE, SHIFT), BF16)

    def spread(values):
        edge = nothing[: values.shape[0]]
        return jnp.concatenate([edge, values, edge], axis=1)

    above, below = above_ref[...], below_ref[...]
    tiles = side // TILE
    parts = (
        (0, spread(jnp.where(block > 0, above, jnp.zeros_like(above)))),
        (EDGE, spread(main_ref[...])),
        (EDGE + TILE, spread(jnp.where(block < last_block, below, jnp.zeros_like(below)))),
    )
    for tile in range(tiles):
        for row, part in parts:
            row = tile * WINDOW + row
            windows[row : row + part.shape[0], :] = part[:, tile * TILE : (tile + 2) * TILE]
    for group in range(0, NB, 2):
        bands = range(group, min(group + 2, NB))
        passed = jnp.dot(
            windows[...], column_ref[:, group * TILE : (bands[-1] + 1) * TILE], preferred_element_type=F32
        ).astype(BF16)
        for k in bands:
            for tile in range(tiles):
                stacked[k * WINDOW : (k + 1) * WINDOW, tile * TILE : (tile + 1) * TILE] = passed[
                    tile * WINDOW : (tile + 1) * WINDOW, (k - group) * TILE : (k - group + 1) * TILE
                ]
    if sky_count != tiles:
        product_ref[...] = jnp.zeros_like(product_ref)
    for pair in range(tiles // 2):
        both = slice(pair * 2 * TILE, (pair + 1) * 2 * TILE)
        summed = jnp.dot(row_ref[...], stacked[:, both], preferred_element_type=F32).astype(BF16)
        matched_ref[:, both] = summed
        for part in range(2):
            target = pl.multiple_of(lax.rem(start + 2 * pair + part, sky_count) * TILE, TILE)
            weight = weight_ref[:, pl.ds(target, TILE)].astype(F32)
            product = weight * summed[:, part * TILE : (part + 1) * TILE].astype(F32)
            product_ref[:, pl.ds(target, TILE)] = product.astype(BF16)


def match(picture, column_band, row_band, weight, which_weight, sky_columns, which, chunk, half_rows, sky_count):
    side = picture.shape[0]
    chunk_rows = half_rows // CHUNKS
    steps = chunk_rows // TILE
    stripe = sky_count * TILE
    edges = TILE // EDGE

    def block(i):
        return (half_of(which) * CHUNKS + chunk) * steps + i

    return pl.pallas_call(
        functools.partial(match_kernel, sky_count, which, chunk * steps, CHUNKS * steps),
        out_shape=(
            pltpu.HBM((chunk_rows, side), BF16),
            pltpu.HBM((chunk_rows, stripe), BF16)
            if which == OTHER
            else jax.ShapeDtypeStruct((chunk_rows, stripe), BF16),
        ),
        grid_spec=pltpu.PrefetchScalarGridSpec(
            num_scalar_prefetch=0,
            grid=(steps,),
            in_specs=[
                SCALARS,
                pl.BlockSpec((EDGE, side), lambda i: (jnp.maximum(block(i) * edges - 1, 0), 0)),
                pl.BlockSpec((TILE, side), lambda i: (block(i), 0)),
                pl.BlockSpec((EDGE, side), lambda i: (jnp.minimum((block(i) + 1) * edges, side // EDGE - 1), 0)),
                pl.BlockSpec(column_band.shape, lambda i: (0, 0), pipeline_mode=pl.Buffered(1)),
                pl.BlockSpec(row_band.shape, lambda i: (0, 0), pipeline_mode=pl.Buffered(1)),
                pl.BlockSpec((None, TILE, stripe), lambda i: (which_weight, i, 0)),
            ],
            out_specs=(
                pl.BlockSpec((TILE, side), lambda i: (i, 0)),
                pl.BlockSpec((TILE, stripe), lambda i: (i, 0)),
            ),
            scratch_shapes=[
                pltpu.VMEM((side // TILE * WINDOW, 2 * TILE), BF16),
                pltpu.VMEM((NB * WINDOW, side), BF16),
            ],
        ),
        cost_estimate=pl.CostEstimate(
            flops=2 * chunk_rows * side * NB * (2 * TILE + WINDOW), bytes_accessed=chunk_rows * side * 8, transcendentals=0
        ),
        compiler_params=pltpu.CompilerParams(vmem_limit_bytes=EARLY_GRANT),
        name="match",
    )(in_hbm(sky_columns), *[in_hbm(picture)] * 3, column_band, row_band, weight)


def row_of(place, line, chunk_rows):
    row = 0
    for bit in range(line.bit_length() - 1):
        row = row + lax.rem(place >> bit, 2) * (chunk_rows >> (bit + 1))
    return row


def piece_rows(step, line, chunk_rows, part_rows):
    row = row_of(lax.axis_index("sky") // 2 ^ step, line, chunk_rows)
    return pl.ds(pl.multiple_of(row, part_rows), part_rows)


def difference_kernel(sky_count, pair, line, sky_ref, *refs):
    matched = refs[:pair]
    pieces = refs[pair : pair + pair * line]
    out_ref = refs[-1]
    start = start_column(sky_ref)
    part_rows = pieces[0].shape[0]
    chunk_rows, side = matched[0].shape
    for group in range(pair):
        half = half_of((OWN, OTHER)[group])
        for step in range(line):
            rows = piece_rows(step, line, chunk_rows, part_rows)
            piece = pieces[group * line + step]
            for tile in range(side // TILE):
                window = slice(tile * TILE, (tile + 1) * TILE)
                source = pl.multiple_of(lax.rem(start + tile, sky_count) * TILE, TILE)
                picked = piece[:, pl.ds(source, TILE)].astype(F32)
                out_ref[half, 0, rows, window] = (matched[group][rows, window].astype(F32) - picked).astype(BF16)


def subtract(matched, pieces, sky_columns, chunk, before, sky_count):
    chunk_rows, side = matched[0].shape
    pair = len(matched)
    line = len(pieces) // pair
    operands = [*map(in_hbm, matched), *pieces]
    specs = [SCALARS] + [pl.BlockSpec(array.shape, lambda i: (0, 0)) for array in operands]
    aliases = {}
    if before is not None:
        operands.append(before)
        specs.append(pl.BlockSpec(memory_space=pl.ANY))
        aliases = {len(operands): 0}
    return pl.pallas_call(
        functools.partial(difference_kernel, sky_count, pair, line),
        out_shape=jax.ShapeDtypeStruct((pair, CHUNKS, chunk_rows, side), BF16),
        grid_spec=pltpu.PrefetchScalarGridSpec(
            num_scalar_prefetch=0,
            grid=(1,),
            in_specs=specs,
            out_specs=pl.BlockSpec((pair, 1, chunk_rows, side), lambda i: (0, chunk, 0, 0)),
        ),
        input_output_aliases=aliases,
        cost_estimate=pl.CostEstimate(
            flops=pair * chunk_rows * side, bytes_accessed=pair * chunk_rows * side * 6, transcendentals=0
        ),
        compiler_params=pltpu.CompilerParams(vmem_limit_bytes=24 << 20),
        name="subtract",
    )(in_hbm(sky_columns), *operands)


def smooth_pieces(sky_count, line, across, pieces, chunk_rows, store):
    def column(piece, away):
        source = lax.rem(lax.axis_index("sky") + away, sky_count) * TILE
        return piece[:, pl.ds(pl.multiple_of(source, TILE), TILE)]

    for group in range(len(pieces) // line):
        for step in range(line):
            piece = pieces[group * line + step]
            window = jnp.concatenate(
                [column(piece, sky_count - 1)[:, SHIFT:], column(piece, 0), column(piece, 1)[:, :SHIFT]], axis=1
            )
            row = row_of(lax.axis_index("sky") // 2 ^ step, line, chunk_rows)
            store(half_of((OWN, OTHER)[group]), row, jnp.dot(window, across, preferred_element_type=F32).astype(BF16))


def smooth_kernel(sky_count, line, sky_ref, across_ref, *refs):
    pieces, out_ref = refs[:-1], refs[-1]
    part_rows, chunk_rows = pieces[0].shape[0], out_ref.shape[1]

    def store(half, row, values):
        out_ref[half, pl.ds(pl.multiple_of(row, part_rows), part_rows), :] = values

    smooth_pieces(sky_count, line, across_ref[...], pieces, chunk_rows, store)


def smooth(pieces, across_band, sky_columns, pair, chunk_rows, sky_count):
    line = len(pieces) // pair
    operands = [across_band, *pieces]
    return pl.pallas_call(
        functools.partial(smooth_kernel, sky_count, line),
        out_shape=jax.ShapeDtypeStruct((pair, chunk_rows, TILE), BF16),
        grid_spec=pltpu.PrefetchScalarGridSpec(
            num_scalar_prefetch=0,
            grid=(1,),
            in_specs=[SCALARS] + [pl.BlockSpec(array.shape, lambda i: (0, 0)) for array in operands],
            out_specs=pl.BlockSpec((pair, chunk_rows, TILE), lambda i: (0, 0, 0)),
        ),
        cost_estimate=pl.CostEstimate(
            flops=pair * chunk_rows * TILE * 512, bytes_accessed=pair * chunk_rows * sky_count * TILE * 2, transcendentals=0
        ),
        compiler_params=pltpu.CompilerParams(vmem_limit_bytes=LATE_GRANT),
        name="smooth",
    )(in_hbm(sky_columns), *operands)


def power_kernel(sky_count, line, band_count, sky_ref, across_ref, down_ref, *refs):
    sources = refs[: CHUNKS - 1]
    pieces = refs[CHUNKS - 1 : -band_count - 1]
    powers, smoothed = refs[-band_count - 1 : -1], refs[-1]
    part_rows = pieces[0].shape[0]
    pair = len(pieces) // line
    chunk_rows = part_rows * line
    side = pair * CHUNKS * chunk_rows
    rows = side // band_count
    smoothed[0:EDGE, :] = jnp.zeros((EDGE, TILE), BF16)
    smoothed[EDGE + side :, :] = jnp.zeros((EDGE, TILE), BF16)
    for half in range(pair):
        for chunk in range(CHUNKS - 1):
            first = EDGE + (half * CHUNKS + chunk) * chunk_rows
            smoothed[first : first + chunk_rows, :] = sources[chunk][half]

    def store(half, row, values):
        first = EDGE + (half * CHUNKS + CHUNKS - 1) * chunk_rows + row
        smoothed[pl.ds(pl.multiple_of(first, EDGE), part_rows), :] = values

    smooth_pieces(sky_count, line, across_ref[...], pieces, chunk_rows, store)
    for step in range(band_count):
        first = lax.rem(lax.axis_index("band") + step, band_count) * rows
        for inner in range(rows // TILE):
            source = pl.multiple_of(first + inner * TILE, TILE)
            filtered = jnp.dot(down_ref[...], smoothed[pl.ds(source, WINDOW), :], preferred_element_type=F32)
            powers[step][inner * TILE : (inner + 1) * TILE, :] = (filtered * filtered).astype(powers[step].dtype)


def power(sources, pieces, across_band, down_band, sky_columns, pair, sky_count, band_count):
    line = len(pieces) // pair
    side = CHUNKS * pair * line * pieces[0].shape[0]
    operands = [across_band, down_band, *sources, *pieces]
    return pl.pallas_call(
        functools.partial(power_kernel, sky_count, line, band_count),
        out_shape=[
            jax.ShapeDtypeStruct((side // band_count, TILE), BF16 if step else F32) for step in range(band_count)
        ],
        grid_spec=pltpu.PrefetchScalarGridSpec(
            num_scalar_prefetch=0,
            grid=(1,),
            in_specs=[SCALARS]
            + [pl.BlockSpec(array.shape, lambda i, n=array.ndim: (0,) * n) for array in operands],
            out_specs=[pl.BlockSpec((side // band_count, TILE), lambda i: (0, 0))] * band_count,
            scratch_shapes=[pltpu.VMEM((side + 2 * EDGE, TILE), BF16)],
        ),
        cost_estimate=pl.CostEstimate(flops=side * TILE * 600, bytes_accessed=side * TILE * 12, transcendentals=0),
        compiler_params=pltpu.CompilerParams(vmem_limit_bytes=LATE_GRANT),
        name="power",
    )(in_hbm(sky_columns), *operands)


def body(exposures, inv_variance, mask_planes, sky_columns, basis_rows, basis_cols, match_coeffs, detect_taps):
    picture = exposures[0, 0]
    side = picture.shape[0]
    sky_count = lax.axis_size("sky")
    band_count = lax.axis_size("band")
    own_sky = lax.axis_index("sky")
    pair = 2
    line = sky_count // pair
    half_rows = side // pair
    chunk_rows = half_rows // CHUNKS

    def exchange(block, bit):
        return lax.ppermute(block, "sky", [(i, i ^ (1 << bit)) for i in range(sky_count)])

    def reduce_line(terms):
        rows = chunk_rows
        bit = 1
        while 1 << bit < sky_count:
            rows = rows // 2
            mine = lax.rem(own_sky >> bit, 2)
            leaving = sum(lax.dynamic_slice_in_dim(t, (1 - mine) * rows, rows, -2).astype(F32) for t in terms)
            arrived = exchange(leaving.astype(BF16), bit)
            terms = [lax.dynamic_slice_in_dim(t, mine * rows, rows, -2) for t in terms] + [arrived]
            bit += 1
        return terms

    def total(terms):
        return sum(t.astype(F32) for t in terms)

    words = mask_planes[0, 0]
    variance = inv_variance[0, 0]

    def weighing(halves, chunk):
        return weigh(variance, words, sky_columns, halves, chunk, chunk_rows, sky_count)

    def matching(weight, which, half_slot, chunk):
        return match(
            picture, column_band, row_band, weight, which, sky_columns, half_slot, chunk, half_rows, sky_count
        )

    weight_other = weighing((OTHER,), 0)
    weight_in = exchange(weight_other[0], 0)
    weight_both = weighing((OTHER, OWN), 1)
    both_terms = reduce_line([weight_both])
    column_band, row_band, across_band, down_band = prepare(
        match_coeffs[0, 0], basis_cols, basis_rows, detect_taps
    )
    weight_own = weighing((OWN,), 0)

    away, product_in, home, product_own = ([None] * CHUNKS for _ in range(4))
    for c in range(CHUNKS):
        away[c], product = matching(weight_both if c else weight_other, 0, OTHER, c)
        product_in[c] = exchange(product, 0)
    for c in range(CHUNKS):
        home[c], product_own[c] = matching(weight_both if c else weight_own, c, OWN, c)
    both_in = exchange(total([t[0] for t in both_terms]).astype(BF16), 0)
    denoms = [
        total(reduce_line([weight_own[0], weight_in])),
        total([t[1] for t in both_terms] + [both_in]),
    ]

    smoothed = [None] * CHUNKS
    difference = None
    for c in range(CHUNKS):
        numer = total(reduce_line([product_own[c], product_in[c]]))
        if c:
            numer, _ = lax.optimization_barrier((numer, block))
        block = (numer / jnp.maximum(denoms[c], 1.0)).astype(BF16)
        near, far = {0: block}, {}
        far[0] = exchange(block, 0)
        for bit in reversed(range(line.bit_length() - 1)):
            for held in list(near):
                step = held | 1 << bit
                near[step] = exchange(near[held], bit + 1)
        for step in range(1, line):
            far[step] = exchange(near[step], 0)
        pieces = [near[step] for step in range(line)] + [far[step] for step in range(line)]
        if c < CHUNKS - 1:
            smoothed[c] = smooth(pieces, across_band, sky_columns, pair, chunk_rows, sky_count)
        else:
            powers = power(
                smoothed[:-1], pieces, across_band, down_band, sky_columns, pair, sky_count, band_count
            )
        difference = subtract([home[c], away[c]], pieces, sky_columns, c, difference, sky_count)

    detection = powers[0]
    for step in range(1, band_count):
        ring = [(i, (i + step) % band_count) for i in range(band_count)]
        detection = detection + lax.ppermute(powers[step], "band", ring).astype(F32)
    return (difference.reshape(1, 1, side, side), detection)


def solution(mesh):
    in_specs = (
        P("sky", "band", None, None),
        P("sky", "band", None, None),
        P("sky", "band", None, None),
        P(),
        P(),
        P(),
        P("sky", "band", None),
        P("band", None),
    )
    out_specs = (P("sky", "band", None, None), P("band", "sky"))

    return jax.shard_map(body, mesh=mesh, in_specs=in_specs, out_specs=out_specs, check_vma=False)
```

```python
import functools

import jax
import jax.numpy as jnp
from jax import lax
from jax.experimental import pallas as pl
from jax.experimental.pallas import tpu as pltpu
from jax.sharding import PartitionSpec as P


TILE = 128
NB = 9
TAPS = 25
DTAPS = 31
BITS = 30
EDGE = 16
WINDOW = TILE + 2 * EDGE
SHIFT = TILE // 2
CHUNKS = 2
OWN, OTHER = 0, 1
EARLY_GRANT = 20 << 20
LATE_GRANT = 24 << 20
SCALARS = pl.BlockSpec(memory_space=pltpu.SMEM)
F32 = jnp.float32
BF16 = jnp.bfloat16


def in_hbm(array):
    return pltpu.with_memory_space_constraint(array, pltpu.HBM)


def start_column(sky_ref):
    return sky_ref[lax.axis_index("sky"), lax.axis_index("band"), 0]


def half_of(which):
    low = lax.rem(lax.axis_index("sky"), 2)
    return low if which == OWN else 1 - low


def toeplitz(base_row, rows):
    wide = jnp.broadcast_to(base_row, (rows, base_row.shape[1]))
    return pltpu.roll(wide, 0, 1, stride=1, stride_axis=0)


def prepare_kernel(base_ref, column_ref, row_ref, across_ref, down_ref):
    for k in range(NB):
        column_ref[:, k * TILE : (k + 1) * TILE] = toeplitz(base_ref[k : k + 1, :], TILE).T.astype(BF16)
        row_ref[:, k * WINDOW : (k + 1) * WINDOW] = toeplitz(base_ref[NB + k : NB + k + 1, :], TILE)[
            :, :WINDOW
        ].astype(BF16)
    across_ref[...] = toeplitz(base_ref[2 * NB : 2 * NB + 1, :], TILE).T.astype(BF16)
    down_ref[...] = toeplitz(base_ref[2 * NB + 1 : 2 * NB + 2, :], TILE)[:, :WINDOW].astype(BF16)


def place_left(taps, offset):
    return jnp.pad(taps, ((0, 0), (offset, 2 * TILE - offset - taps.shape[1])))


def prepare(match_coeffs, basis_cols, basis_rows, detect_taps):
    column_taps = (match_coeffs[:, None] * basis_cols).astype(BF16).astype(F32)
    row_taps = basis_rows.astype(BF16).astype(F32)
    taps = detect_taps.astype(BF16).astype(F32)
    base = jnp.concatenate(
        [
            place_left(column_taps, SHIFT - TAPS // 2),
            place_left(row_taps, EDGE - TAPS // 2),
            place_left(taps, SHIFT - DTAPS // 2),
            place_left(taps, EDGE - DTAPS // 2),
        ],
        0,
    )
    return pl.pallas_call(
        prepare_kernel,
        out_shape=(
            jax.ShapeDtypeStruct((2 * TILE, NB * TILE), BF16),
            jax.ShapeDtypeStruct((TILE, NB * WINDOW), BF16),
            jax.ShapeDtypeStruct((2 * TILE, TILE), BF16),
            jax.ShapeDtypeStruct((TILE, WINDOW), BF16),
        ),
        compiler_params=pltpu.CompilerParams(vmem_limit_bytes=16 << 20),
        name="prepare",
    )(base)


def bad_bits(words_ref, plane, first_word, count, places):
    last = words_ref.shape[1] - 1
    word = jnp.full(places.shape, words_ref[plane, jnp.minimum(first_word, last)])
    begin = jnp.full(places.shape, first_word * BITS)
    for step in range(1, count):
        index = first_word + step
        reached = places >= index * BITS
        word = jnp.where(reached, words_ref[plane, jnp.minimum(index, last)], word)
        begin = jnp.where(reached, index * BITS, begin)
    return jnp.bitwise_and(jnp.right_shift(word, places - begin), 1)


def pick_block(index, halves, chunk, blocks):
    half = half_of(halves[0])
    for place in range(1, len(halves)):
        half = jnp.where(index >= place * blocks, half_of(halves[place]), half)
    return (half * CHUNKS + chunk) * blocks + lax.rem(index, blocks)


def weight_kernel(sky_count, halves, chunk, blocks, sky_ref, words_ref, variance_ref, weight_ref):
    rows, side = variance_ref.shape
    start = start_column(sky_ref)
    first_row = pick_block(pl.program_id(0), halves, chunk, blocks) * rows
    lanes = lax.broadcasted_iota(jnp.int32, (8, side), 1)
    column_bad = bad_bits(words_ref, 0, 0, words_ref.shape[1], lanes)[0:1, :]
    places = first_row + lax.broadcasted_iota(jnp.int32, (rows, TILE), 0)
    row_bad = bad_bits(words_ref, 1, first_row // BITS, rows // BITS + 2, places)
    if sky_count * TILE != side:
        weight_ref[...] = jnp.zeros_like(weight_ref)
    for tile in range(side // TILE):
        window = slice(tile * TILE, (tile + 1) * TILE)
        bad = row_bad + column_bad[:, window]
        kept = jnp.where(bad == 0, variance_ref[:, window].astype(F32), 0.0)
        target = lax.rem(start + tile, sky_count) * TILE
        weight_ref[0, :, pl.ds(pl.multiple_of(target, TILE), TILE)] = kept.astype(BF16)


def weigh(inv_variance, words, sky_columns, halves, chunk, chunk_rows, sky_count):
    side = inv_variance.shape[0]
    stripe = sky_count * TILE
    rows = min(TILE, chunk_rows)
    blocks = chunk_rows // rows
    return pl.pallas_call(
        functools.partial(weight_kernel, sky_count, halves, chunk, blocks),
        out_shape=jax.ShapeDtypeStruct((len(halves), chunk_rows, stripe), BF16),
        grid_spec=pltpu.PrefetchScalarGridSpec(
            num_scalar_prefetch=0,
            grid=(len(halves) * blocks,),
            in_specs=[SCALARS, SCALARS, pl.BlockSpec((rows, side), lambda i: (pick_block(i, halves, chunk, blocks), 0))],
            out_specs=pl.BlockSpec((1, rows, stripe), lambda i: (i // blocks, lax.rem(i, blocks), 0)),
        ),
        cost_estimate=pl.CostEstimate(
            flops=len(halves) * chunk_rows * side * 8,
            bytes_accessed=len(halves) * chunk_rows * side * 4,
            transcendentals=0,
        ),
        compiler_params=pltpu.CompilerParams(vmem_limit_bytes=EARLY_GRANT),
        name="weigh",
    )(in_hbm(sky_columns), in_hbm(words), in_hbm(inv_variance))


def match_kernel(
    sky_count,
    which,
    offset,
    half_blocks,
    sky_ref,
    above_ref,
    main_ref,
    below_ref,
    column_ref,
    row_ref,
    weight_ref,
    matched_ref,
    product_ref,
    windows,
    stacked,
):
    side = main_ref.shape[1]
    start = start_column(sky_ref)
    block = half_of(which) * half_blocks + offset + pl.program_id(0)
    last_block = side // TILE - 1
    nothing = jnp.zeros((TILE, SHIFT), BF16)

    def spread(values):
        edge = nothing[: values.shape[0]]
        return jnp.concatenate([edge, values, edge], axis=1)

    above, below = above_ref[...], below_ref[...]
    tiles = side // TILE
    parts = (
        (0, spread(jnp.where(block > 0, above, jnp.zeros_like(above)))),
        (EDGE, spread(main_ref[...])),
        (EDGE + TILE, spread(jnp.where(block < last_block, below, jnp.zeros_like(below)))),
    )
    for tile in range(tiles):
        for row, part in parts:
            row = tile * WINDOW + row
            windows[row : row + part.shape[0], :] = part[:, tile * TILE : (tile + 2) * TILE]
    for group in range(0, NB, 2):
        bands = range(group, min(group + 2, NB))
        passed = jnp.dot(
            windows[...], column_ref[:, group * TILE : (bands[-1] + 1) * TILE], preferred_element_type=F32
        ).astype(BF16)
        for k in bands:
            for tile in range(tiles):
                stacked[k * WINDOW : (k + 1) * WINDOW, tile * TILE : (tile + 1) * TILE] = passed[
                    tile * WINDOW : (tile + 1) * WINDOW, (k - group) * TILE : (k - group + 1) * TILE
                ]
    if sky_count != tiles:
        product_ref[...] = jnp.zeros_like(product_ref)
    for pair in range(tiles // 2):
        both = slice(pair * 2 * TILE, (pair + 1) * 2 * TILE)
        summed = jnp.dot(row_ref[...], stacked[:, both], preferred_element_type=F32).astype(BF16)
        matched_ref[:, both] = summed
        for part in range(2):
            target = pl.multiple_of(lax.rem(start + 2 * pair + part, sky_count) * TILE, TILE)
            weight = weight_ref[:, pl.ds(target, TILE)].astype(F32)
            product = weight * summed[:, part * TILE : (part + 1) * TILE].astype(F32)
            product_ref[:, pl.ds(target, TILE)] = product.astype(BF16)


def match(picture, column_band, row_band, weight, which_weight, sky_columns, which, chunk, half_rows, sky_count):
    side = picture.shape[0]
    chunk_rows = half_rows // CHUNKS
    steps = chunk_rows // TILE
    stripe = sky_count * TILE
    edges = TILE // EDGE

    def block(i):
        return (half_of(which) * CHUNKS + chunk) * steps + i

    return pl.pallas_call(
        functools.partial(match_kernel, sky_count, which, chunk * steps, CHUNKS * steps),
        out_shape=(
            pltpu.HBM((chunk_rows, side), BF16),
            pltpu.HBM((chunk_rows, stripe), BF16)
            if which == OTHER
            else jax.ShapeDtypeStruct((chunk_rows, stripe), BF16),
        ),
        grid_spec=pltpu.PrefetchScalarGridSpec(
            num_scalar_prefetch=0,
            grid=(steps,),
            in_specs=[
                SCALARS,
                pl.BlockSpec((EDGE, side), lambda i: (jnp.maximum(block(i) * edges - 1, 0), 0)),
                pl.BlockSpec((TILE, side), lambda i: (block(i), 0)),
                pl.BlockSpec((EDGE, side), lambda i: (jnp.minimum((block(i) + 1) * edges, side // EDGE - 1), 0)),
                pl.BlockSpec(column_band.shape, lambda i: (0, 0), pipeline_mode=pl.Buffered(1)),
                pl.BlockSpec(row_band.shape, lambda i: (0, 0), pipeline_mode=pl.Buffered(1)),
                pl.BlockSpec((None, TILE, stripe), lambda i: (which_weight, i, 0)),
            ],
            out_specs=(
                pl.BlockSpec((TILE, side), lambda i: (i, 0)),
                pl.BlockSpec((TILE, stripe), lambda i: (i, 0)),
            ),
            scratch_shapes=[
                pltpu.VMEM((side // TILE * WINDOW, 2 * TILE), BF16),
                pltpu.VMEM((NB * WINDOW, side), BF16),
            ],
        ),
        cost_estimate=pl.CostEstimate(
            flops=2 * chunk_rows * side * NB * (2 * TILE + WINDOW), bytes_accessed=chunk_rows * side * 8, transcendentals=0
        ),
        compiler_params=pltpu.CompilerParams(vmem_limit_bytes=EARLY_GRANT),
        name="match",
    )(in_hbm(sky_columns), *[in_hbm(picture)] * 3, column_band, row_band, weight)


def row_of(place, line, chunk_rows):
    row = 0
    for bit in range(line.bit_length() - 1):
        row = row + lax.rem(place >> bit, 2) * (chunk_rows >> (bit + 1))
    return row


def piece_rows(step, line, chunk_rows, part_rows):
    row = row_of(lax.axis_index("sky") // 2 ^ step, line, chunk_rows)
    return pl.ds(pl.multiple_of(row, part_rows), part_rows)


def difference_kernel(sky_count, pair, line, sky_ref, *refs):
    matched = refs[:pair]
    pieces = refs[pair : pair + pair * line]
    out_ref = refs[-1]
    start = start_column(sky_ref)
    part_rows = pieces[0].shape[0]
    chunk_rows, side = matched[0].shape
    for group in range(pair):
        half = half_of((OWN, OTHER)[group])
        for step in range(line):
            rows = piece_rows(step, line, chunk_rows, part_rows)
            piece = pieces[group * line + step]
            for tile in range(side // TILE):
                window = slice(tile * TILE, (tile + 1) * TILE)
                source = pl.multiple_of(lax.rem(start + tile, sky_count) * TILE, TILE)
                picked = piece[:, pl.ds(source, TILE)].astype(F32)
                out_ref[half, 0, rows, window] = (matched[group][rows, window].astype(F32) - picked).astype(BF16)


def subtract(matched, pieces, sky_columns, chunk, before, sky_count):
    chunk_rows, side = matched[0].shape
    pair = len(matched)
    line = len(pieces) // pair
    operands = [*map(in_hbm, matched), *pieces]
    specs = [SCALARS] + [pl.BlockSpec(array.shape, lambda i: (0, 0)) for array in operands]
    aliases = {}
    if before is not None:
        operands.append(before)
        specs.append(pl.BlockSpec(memory_space=pl.ANY))
        aliases = {len(operands): 0}
    return pl.pallas_call(
        functools.partial(difference_kernel, sky_count, pair, line),
        out_shape=jax.ShapeDtypeStruct((pair, CHUNKS, chunk_rows, side), BF16),
        grid_spec=pltpu.PrefetchScalarGridSpec(
            num_scalar_prefetch=0,
            grid=(1,),
            in_specs=specs,
            out_specs=pl.BlockSpec((pair, 1, chunk_rows, side), lambda i: (0, chunk, 0, 0)),
        ),
        input_output_aliases=aliases,
        cost_estimate=pl.CostEstimate(
            flops=pair * chunk_rows * side, bytes_accessed=pair * chunk_rows * side * 6, transcendentals=0
        ),
        compiler_params=pltpu.CompilerParams(vmem_limit_bytes=24 << 20),
        name="subtract",
    )(in_hbm(sky_columns), *operands)


def smooth_pieces(sky_count, line, across, pieces, chunk_rows, store):
    def column(piece, away):
        source = lax.rem(lax.axis_index("sky") + away, sky_count) * TILE
        return piece[:, pl.ds(pl.multiple_of(source, TILE), TILE)]

    for group in range(len(pieces) // line):
        for step in range(line):
            piece = pieces[group * line + step]
            window = jnp.concatenate(
                [column(piece, sky_count - 1)[:, SHIFT:], column(piece, 0), column(piece, 1)[:, :SHIFT]], axis=1
            )
            row = row_of(lax.axis_index("sky") // 2 ^ step, line, chunk_rows)
            store(half_of((OWN, OTHER)[group]), row, jnp.dot(window, across, preferred_element_type=F32).astype(BF16))


def smooth_kernel(sky_count, line, sky_ref, across_ref, *refs):
    pieces, out_ref = refs[:-1], refs[-1]
    part_rows, chunk_rows = pieces[0].shape[0], out_ref.shape[1]

    def store(half, row, values):
        out_ref[half, pl.ds(pl.multiple_of(row, part_rows), part_rows), :] = values

    smooth_pieces(sky_count, line, across_ref[...], pieces, chunk_rows, store)


def smooth(pieces, across_band, sky_columns, pair, chunk_rows, sky_count):
    line = len(pieces) // pair
    operands = [across_band, *pieces]
    return pl.pallas_call(
        functools.partial(smooth_kernel, sky_count, line),
        out_shape=jax.ShapeDtypeStruct((pair, chunk_rows, TILE), BF16),
        grid_spec=pltpu.PrefetchScalarGridSpec(
            num_scalar_prefetch=0,
            grid=(1,),
            in_specs=[SCALARS] + [pl.BlockSpec(array.shape, lambda i: (0, 0)) for array in operands],
            out_specs=pl.BlockSpec((pair, chunk_rows, TILE), lambda i: (0, 0, 0)),
        ),
        cost_estimate=pl.CostEstimate(
            flops=pair * chunk_rows * TILE * 512, bytes_accessed=pair * chunk_rows * sky_count * TILE * 2, transcendentals=0
        ),
        compiler_params=pltpu.CompilerParams(vmem_limit_bytes=LATE_GRANT),
        name="smooth",
    )(in_hbm(sky_columns), *operands)


def power_kernel(sky_count, line, band_count, sky_ref, across_ref, down_ref, *refs):
    sources = refs[: CHUNKS - 1]
    pieces = refs[CHUNKS - 1 : -band_count - 1]
    powers, smoothed = refs[-band_count - 1 : -1], refs[-1]
    part_rows = pieces[0].shape[0]
    pair = len(pieces) // line
    chunk_rows = part_rows * line
    side = pair * CHUNKS * chunk_rows
    rows = side // band_count
    smoothed[0:EDGE, :] = jnp.zeros((EDGE, TILE), BF16)
    smoothed[EDGE + side :, :] = jnp.zeros((EDGE, TILE), BF16)
    for half in range(pair):
        for chunk in range(CHUNKS - 1):
            first = EDGE + (half * CHUNKS + chunk) * chunk_rows
            smoothed[first : first + chunk_rows, :] = sources[chunk][half]

    def store(half, row, values):
        first = EDGE + (half * CHUNKS + CHUNKS - 1) * chunk_rows + row
        smoothed[pl.ds(pl.multiple_of(first, EDGE), part_rows), :] = values

    smooth_pieces(sky_count, line, across_ref[...], pieces, chunk_rows, store)
    for step in range(band_count):
        first = lax.rem(lax.axis_index("band") + step, band_count) * rows
        for inner in range(rows // TILE):
            source = pl.multiple_of(first + inner * TILE, TILE)
            filtered = jnp.dot(down_ref[...], smoothed[pl.ds(source, WINDOW), :], preferred_element_type=F32)
            powers[step][inner * TILE : (inner + 1) * TILE, :] = (filtered * filtered).astype(powers[step].dtype)


def power(sources, pieces, across_band, down_band, sky_columns, pair, sky_count, band_count):
    line = len(pieces) // pair
    side = CHUNKS * pair * line * pieces[0].shape[0]
    operands = [across_band, down_band, *sources, *pieces]
    return pl.pallas_call(
        functools.partial(power_kernel, sky_count, line, band_count),
        out_shape=[
            jax.ShapeDtypeStruct((side // band_count, TILE), BF16 if step else F32) for step in range(band_count)
        ],
        grid_spec=pltpu.PrefetchScalarGridSpec(
            num_scalar_prefetch=0,
            grid=(1,),
            in_specs=[SCALARS]
            + [pl.BlockSpec(array.shape, lambda i, n=array.ndim: (0,) * n) for array in operands],
            out_specs=[pl.BlockSpec((side // band_count, TILE), lambda i: (0, 0))] * band_count,
            scratch_shapes=[pltpu.VMEM((side + 2 * EDGE, TILE), BF16)],
        ),
        cost_estimate=pl.CostEstimate(flops=side * TILE * 600, bytes_accessed=side * TILE * 12, transcendentals=0),
        compiler_params=pltpu.CompilerParams(vmem_limit_bytes=LATE_GRANT),
        name="power",
    )(in_hbm(sky_columns), *operands)


def body(exposures, inv_variance, mask_planes, sky_columns, basis_rows, basis_cols, match_coeffs, detect_taps):
    picture = exposures[0, 0]
    side = picture.shape[0]
    sky_count = lax.axis_size("sky")
    band_count = lax.axis_size("band")
    own_sky = lax.axis_index("sky")
    pair = 2
    line = sky_count // pair
    half_rows = side // pair
    chunk_rows = half_rows // CHUNKS

    def exchange(block, bit):
        return lax.ppermute(block, "sky", [(i, i ^ (1 << bit)) for i in range(sky_count)])

    def reduce_line(terms):
        rows = chunk_rows
        bit = 1
        while 1 << bit < sky_count:
            rows = rows // 2
            mine = lax.rem(own_sky >> bit, 2)
            leaving = sum(lax.dynamic_slice_in_dim(t, (1 - mine) * rows, rows, -2).astype(F32) for t in terms)
            arrived = exchange(leaving.astype(BF16), bit)
            terms = [lax.dynamic_slice_in_dim(t, mine * rows, rows, -2) for t in terms] + [arrived]
            bit += 1
        return terms

    def total(terms):
        return sum(t.astype(F32) for t in terms)

    words = mask_planes[0, 0]
    variance = inv_variance[0, 0]

    def weighing(halves, chunk):
        return weigh(variance, words, sky_columns, halves, chunk, chunk_rows, sky_count)

    def matching(weight, which, half_slot, chunk):
        return match(
            picture, column_band, row_band, weight, which, sky_columns, half_slot, chunk, half_rows, sky_count
        )

    weight_other = weighing((OTHER,), 0)
    weight_in = exchange(weight_other[0], 0)
    weight_both = weighing((OTHER, OWN), 1)
    both_terms = reduce_line([weight_both])
    column_band, row_band, across_band, down_band = prepare(
        match_coeffs[0, 0], basis_cols, basis_rows, detect_taps
    )
    weight_own = weighing((OWN,), 0)

    away, product_in, home, product_own = ([None] * CHUNKS for _ in range(4))
    for c in range(CHUNKS):
        away[c], product = matching(weight_both if c else weight_other, 0, OTHER, c)
        product_in[c] = exchange(product, 0)
    for c in range(CHUNKS):
        home[c], product_own[c] = matching(weight_both if c else weight_own, c, OWN, c)
    both_in = exchange(total([t[0] for t in both_terms]).astype(BF16), 0)
    denoms = [
        total(reduce_line([weight_own[0], weight_in])),
        total([t[1] for t in both_terms] + [both_in]),
    ]

    smoothed = [None] * CHUNKS
    difference = None
    for c in range(CHUNKS):
        terms = reduce_line([product_own[c], product_in[c]])
        if c:
            terms[-1], _ = lax.optimization_barrier((terms[-1], block))
        numer = total(terms)
        block = (numer / jnp.maximum(denoms[c], 1.0)).astype(BF16)
        near, far = {0: block}, {}
        far[0] = exchange(block, 0)
        for bit in reversed(range(line.bit_length() - 1)):
            for held in list(near):
                step = held | 1 << bit
                near[step] = exchange(near[held], bit + 1)
        for step in range(1, line):
            far[step] = exchange(near[step], 0)
        pieces = [near[step] for step in range(line)] + [far[step] for step in range(line)]
        if c < CHUNKS - 1:
            smoothed[c] = smooth(pieces, across_band, sky_columns, pair, chunk_rows, sky_count)
        else:
            powers = power(
                smoothed[:-1], pieces, across_band, down_band, sky_columns, pair, sky_count, band_count
            )
        difference = subtract([home[c], away[c]], pieces, sky_columns, c, difference, sky_count)

    detection = powers[0]
    for step in range(1, band_count):
        ring = [(i, (i + step) % band_count) for i in range(band_count)]
        detection = detection + lax.ppermute(powers[step], "band", ring).astype(F32)
    return (difference.reshape(1, 1, side, side), detection)


def solution(mesh):
    in_specs = (
        P("sky", "band", None, None),
        P("sky", "band", None, None),
        P("sky", "band", None, None),
        P(),
        P(),
        P(),
        P("sky", "band", None),
        P("band", None),
    )
    out_specs = (P("sky", "band", None, None), P("band", "sky"))

    return jax.shard_map(body, mesh=mesh, in_specs=in_specs, out_specs=out_specs, check_vma=False)
```

```python
import functools

import jax
import jax.numpy as jnp
from jax import lax
from jax.experimental import pallas as pl
from jax.experimental.pallas import tpu as pltpu
from jax.sharding import PartitionSpec as P


TILE = 128
NB = 9
TAPS = 25
DTAPS = 31
BITS = 30
EDGE = 16
WINDOW = TILE + 2 * EDGE
SHIFT = TILE // 2
CHUNKS = 2
OWN, OTHER = 0, 1
EARLY_GRANT = 20 << 20
LATE_GRANT = 24 << 20
SCALARS = pl.BlockSpec(memory_space=pltpu.SMEM)
F32 = jnp.float32
BF16 = jnp.bfloat16


def in_hbm(array):
    return pltpu.with_memory_space_constraint(array, pltpu.HBM)


def start_column(sky_ref):
    return sky_ref[lax.axis_index("sky"), lax.axis_index("band"), 0]


def half_of(which):
    low = lax.rem(lax.axis_index("sky"), 2)
    return low if which == OWN else 1 - low


def toeplitz(base_row, rows):
    wide = jnp.broadcast_to(base_row, (rows, base_row.shape[1]))
    return pltpu.roll(wide, 0, 1, stride=1, stride_axis=0)


def prepare_kernel(base_ref, column_ref, row_ref, across_ref, down_ref):
    for k in range(NB):
        column_ref[:, k * TILE : (k + 1) * TILE] = toeplitz(base_ref[k : k + 1, :], TILE).T.astype(BF16)
        row_ref[:, k * WINDOW : (k + 1) * WINDOW] = toeplitz(base_ref[NB + k : NB + k + 1, :], TILE)[
            :, :WINDOW
        ].astype(BF16)
    across_ref[...] = toeplitz(base_ref[2 * NB : 2 * NB + 1, :], TILE).T.astype(BF16)
    down_ref[...] = toeplitz(base_ref[2 * NB + 1 : 2 * NB + 2, :], TILE)[:, :WINDOW].astype(BF16)


def place_left(taps, offset):
    return jnp.pad(taps, ((0, 0), (offset, 2 * TILE - offset - taps.shape[1])))


def prepare(match_coeffs, basis_cols, basis_rows, detect_taps):
    column_taps = (match_coeffs[:, None] * basis_cols).astype(BF16).astype(F32)
    row_taps = basis_rows.astype(BF16).astype(F32)
    taps = detect_taps.astype(BF16).astype(F32)
    base = jnp.concatenate(
        [
            place_left(column_taps, SHIFT - TAPS // 2),
            place_left(row_taps, EDGE - TAPS // 2),
            place_left(taps, SHIFT - DTAPS // 2),
            place_left(taps, EDGE - DTAPS // 2),
        ],
        0,
    )
    return pl.pallas_call(
        prepare_kernel,
        out_shape=(
            jax.ShapeDtypeStruct((2 * TILE, NB * TILE), BF16),
            jax.ShapeDtypeStruct((TILE, NB * WINDOW), BF16),
            jax.ShapeDtypeStruct((2 * TILE, TILE), BF16),
            jax.ShapeDtypeStruct((TILE, WINDOW), BF16),
        ),
        compiler_params=pltpu.CompilerParams(vmem_limit_bytes=16 << 20),
        name="prepare",
    )(base)


def bad_bits(words_ref, plane, first_word, count, places):
    last = words_ref.shape[1] - 1
    word = jnp.full(places.shape, words_ref[plane, jnp.minimum(first_word, last)])
    begin = jnp.full(places.shape, first_word * BITS)
    for step in range(1, count):
        index = first_word + step
        reached = places >= index * BITS
        word = jnp.where(reached, words_ref[plane, jnp.minimum(index, last)], word)
        begin = jnp.where(reached, index * BITS, begin)
    return jnp.bitwise_and(jnp.right_shift(word, places - begin), 1)


def pick_block(index, halves, chunk, blocks):
    half = half_of(halves[0])
    for place in range(1, len(halves)):
        half = jnp.where(index >= place * blocks, half_of(halves[place]), half)
    return (half * CHUNKS + chunk) * blocks + lax.rem(index, blocks)


def weight_kernel(sky_count, halves, chunk, blocks, sky_ref, words_ref, variance_ref, weight_ref):
    rows, side = variance_ref.shape
    start = start_column(sky_ref)
    first_row = pick_block(pl.program_id(0), halves, chunk, blocks) * rows
    lanes = lax.broadcasted_iota(jnp.int32, (8, side), 1)
    column_bad = bad_bits(words_ref, 0, 0, words_ref.shape[1], lanes)[0:1, :]
    places = first_row + lax.broadcasted_iota(jnp.int32, (rows, TILE), 0)
    row_bad = bad_bits(words_ref, 1, first_row // BITS, rows // BITS + 2, places)
    if sky_count * TILE != side:
        weight_ref[...] = jnp.zeros_like(weight_ref)
    for tile in range(side // TILE):
        window = slice(tile * TILE, (tile + 1) * TILE)
        bad = row_bad + column_bad[:, window]
        kept = jnp.where(bad == 0, variance_ref[:, window].astype(F32), 0.0)
        target = lax.rem(start + tile, sky_count) * TILE
        weight_ref[0, :, pl.ds(pl.multiple_of(target, TILE), TILE)] = kept.astype(BF16)


def weigh(inv_variance, words, sky_columns, halves, chunk, chunk_rows, sky_count):
    side = inv_variance.shape[0]
    stripe = sky_count * TILE
    rows = min(TILE, chunk_rows)
    blocks = chunk_rows // rows
    return pl.pallas_call(
        functools.partial(weight_kernel, sky_count, halves, chunk, blocks),
        out_shape=jax.ShapeDtypeStruct((len(halves), chunk_rows, stripe), BF16),
        grid_spec=pltpu.PrefetchScalarGridSpec(
            num_scalar_prefetch=0,
            grid=(len(halves) * blocks,),
            in_specs=[SCALARS, SCALARS, pl.BlockSpec((rows, side), lambda i: (pick_block(i, halves, chunk, blocks), 0))],
            out_specs=pl.BlockSpec((1, rows, stripe), lambda i: (i // blocks, lax.rem(i, blocks), 0)),
        ),
        cost_estimate=pl.CostEstimate(
            flops=len(halves) * chunk_rows * side * 8,
            bytes_accessed=len(halves) * chunk_rows * side * 4,
            transcendentals=0,
        ),
        compiler_params=pltpu.CompilerParams(vmem_limit_bytes=EARLY_GRANT),
        name="weigh",
    )(in_hbm(sky_columns), in_hbm(words), in_hbm(inv_variance))


def match_kernel(
    sky_count,
    which,
    offset,
    half_blocks,
    sky_ref,
    above_ref,
    main_ref,
    below_ref,
    column_ref,
    row_ref,
    weight_ref,
    matched_ref,
    product_ref,
    windows,
    stacked,
):
    side = main_ref.shape[1]
    start = start_column(sky_ref)
    block = half_of(which) * half_blocks + offset + pl.program_id(0)
    last_block = side // TILE - 1
    nothing = jnp.zeros((TILE, SHIFT), BF16)

    def spread(values):
        edge = nothing[: values.shape[0]]
        return jnp.concatenate([edge, values, edge], axis=1)

    above, below = above_ref[...], below_ref[...]
    tiles = side // TILE
    parts = (
        (0, spread(jnp.where(block > 0, above, jnp.zeros_like(above)))),
        (EDGE, spread(main_ref[...])),
        (EDGE + TILE, spread(jnp.where(block < last_block, below, jnp.zeros_like(below)))),
    )
    for tile in range(tiles):
        for row, part in parts:
            row = tile * WINDOW + row
            windows[row : row + part.shape[0], :] = part[:, tile * TILE : (tile + 2) * TILE]
    for group in range(0, NB, 2):
        bands = range(group, min(group + 2, NB))
        passed = jnp.dot(
            windows[...], column_ref[:, group * TILE : (bands[-1] + 1) * TILE], preferred_element_type=F32
        ).astype(BF16)
        for k in bands:
            for tile in range(tiles):
                stacked[k * WINDOW : (k + 1) * WINDOW, tile * TILE : (tile + 1) * TILE] = passed[
                    tile * WINDOW : (tile + 1) * WINDOW, (k - group) * TILE : (k - group + 1) * TILE
                ]
    if sky_count != tiles:
        product_ref[...] = jnp.zeros_like(product_ref)
    for pair in range(tiles // 2):
        both = slice(pair * 2 * TILE, (pair + 1) * 2 * TILE)
        summed = jnp.dot(row_ref[...], stacked[:, both], preferred_element_type=F32).astype(BF16)
        matched_ref[:, both] = summed
        for part in range(2):
            target = pl.multiple_of(lax.rem(start + 2 * pair + part, sky_count) * TILE, TILE)
            weight = weight_ref[:, pl.ds(target, TILE)].astype(F32)
            product = weight * summed[:, part * TILE : (part + 1) * TILE].astype(F32)
            product_ref[:, pl.ds(target, TILE)] = product.astype(BF16)


def match(picture, column_band, row_band, weight, which_weight, sky_columns, which, chunk, half_rows, sky_count):
    side = picture.shape[0]
    chunk_rows = half_rows // CHUNKS
    steps = chunk_rows // TILE
    stripe = sky_count * TILE
    edges = TILE // EDGE

    def block(i):
        return (half_of(which) * CHUNKS + chunk) * steps + i

    return pl.pallas_call(
        functools.partial(match_kernel, sky_count, which, chunk * steps, CHUNKS * steps),
        out_shape=(
            pltpu.HBM((chunk_rows, side), BF16),
            pltpu.HBM((chunk_rows, stripe), BF16)
            if which == OTHER
            else jax.ShapeDtypeStruct((chunk_rows, stripe), BF16),
        ),
        grid_spec=pltpu.PrefetchScalarGridSpec(
            num_scalar_prefetch=0,
            grid=(steps,),
            in_specs=[
                SCALARS,
                pl.BlockSpec((EDGE, side), lambda i: (jnp.maximum(block(i) * edges - 1, 0), 0)),
                pl.BlockSpec((TILE, side), lambda i: (block(i), 0)),
                pl.BlockSpec((EDGE, side), lambda i: (jnp.minimum((block(i) + 1) * edges, side // EDGE - 1), 0)),
                pl.BlockSpec(column_band.shape, lambda i: (0, 0), pipeline_mode=pl.Buffered(1)),
                pl.BlockSpec(row_band.shape, lambda i: (0, 0), pipeline_mode=pl.Buffered(1)),
                pl.BlockSpec((None, TILE, stripe), lambda i: (which_weight, i, 0)),
            ],
            out_specs=(
                pl.BlockSpec((TILE, side), lambda i: (i, 0)),
                pl.BlockSpec((TILE, stripe), lambda i: (i, 0)),
            ),
            scratch_shapes=[
                pltpu.VMEM((side // TILE * WINDOW, 2 * TILE), BF16),
                pltpu.VMEM((NB * WINDOW, side), BF16),
            ],
        ),
        cost_estimate=pl.CostEstimate(
            flops=2 * chunk_rows * side * NB * (2 * TILE + WINDOW), bytes_accessed=chunk_rows * side * 8, transcendentals=0
        ),
        compiler_params=pltpu.CompilerParams(vmem_limit_bytes=EARLY_GRANT),
        name="match",
    )(in_hbm(sky_columns), *[in_hbm(picture)] * 3, column_band, row_band, weight)


def row_of(place, line, chunk_rows):
    row = 0
    for bit in range(line.bit_length() - 1):
        row = row + lax.rem(place >> bit, 2) * (chunk_rows >> (bit + 1))
    return row


def smooth_pieces(sky_count, line, across, pieces, chunk_rows, store):
    def column(piece, away):
        source = lax.rem(lax.axis_index("sky") + away, sky_count) * TILE
        return piece[:, pl.ds(pl.multiple_of(source, TILE), TILE)]

    for group in range(len(pieces) // line):
        for step in range(line):
            piece = pieces[group * line + step]
            window = jnp.concatenate(
                [column(piece, sky_count - 1)[:, SHIFT:], column(piece, 0), column(piece, 1)[:, :SHIFT]], axis=1
            )
            row = row_of(lax.axis_index("sky") // 2 ^ step, line, chunk_rows)
            store(half_of((OWN, OTHER)[group]), row, jnp.dot(window, across, preferred_element_type=F32).astype(BF16))


def finish_kernel(sky_count, line, jobs, with_smooth, sky_ref, *refs):
    count = len(jobs)
    if with_smooth:
        across_ref, refs = refs[0], refs[1:]
    matched, refs = refs[:count], refs[count:]
    pieces, refs = refs[: count * line], refs[count * line :]
    if not with_smooth:
        refs = refs[1:]
    out_ref, refs = refs[0], refs[1:]
    if with_smooth:
        smooth_ref, refs = refs[0], refs[1:]
    taken, ready, taken_sem, ready_sem = refs if with_smooth else (None, *refs[:1], None, *refs[1:])
    chunk_rows, side = matched[0].shape
    part_rows = pieces[0].shape[0]
    start = start_column(sky_ref)
    arriving = []
    if with_smooth:
        arriving = [
            pltpu.make_async_copy(matched[index], taken.at[index], taken_sem.at[index]) for index in range(count)
        ]
    for copy in arriving:
        copy.start()
    if with_smooth:

        def store(half, row, values):
            smooth_ref[half, pl.ds(pl.multiple_of(row, part_rows), part_rows), :] = values

        smooth_pieces(sky_count, line, across_ref[...], pieces[: 2 * line], chunk_rows, store)
    leaving = []
    for index, (which, chunk) in enumerate(jobs):
        source_ref = matched[index]
        if with_smooth:
            arriving[index].wait()
            source_ref = taken.at[index]
        for step in range(line):
            row = row_of(lax.axis_index("sky") // 2 ^ step, line, chunk_rows)
            rows = pl.ds(pl.multiple_of(row, part_rows), part_rows)
            piece = pieces[index * line + step]
            for tile in range(side // TILE):
                window = slice(tile * TILE, (tile + 1) * TILE)
                source = pl.multiple_of(lax.rem(start + tile, sky_count) * TILE, TILE)
                picked = piece[:, pl.ds(source, TILE)].astype(F32)
                ready[index, rows, window] = (source_ref[rows, window].astype(F32) - picked).astype(BF16)
        copy = pltpu.make_async_copy(ready.at[index], out_ref.at[half_of(which), chunk], ready_sem.at[index])
        copy.start()
        leaving.append(copy)
    for copy in leaving:
        copy.wait()


def finish(jobs, matched, pieces, across_band, sky_columns, before, sky_count):
    chunk_rows, side = matched[0].shape
    count = len(jobs)
    line = len(pieces) // count
    with_smooth = before is None
    place = pl.BlockSpec(memory_space=pl.ANY)
    operands = [*map(in_hbm, matched), *pieces]
    specs = [pl.BlockSpec(array.shape, lambda i: (0, 0)) for array in operands]
    scratch = [pltpu.VMEM((count, chunk_rows, side), BF16), pltpu.SemaphoreType.DMA((count,))]
    if with_smooth:
        operands = [across_band, *operands]
        specs = [pl.BlockSpec(across_band.shape, lambda i: (0, 0))] + [place] * count + specs[count:]
        scratch = [scratch[0], scratch[0], scratch[1], scratch[1]]
    specs = [SCALARS] + specs
    shapes = [pltpu.HBM((2, CHUNKS, chunk_rows, side), BF16)]
    outs = [place]
    aliases = {}
    if with_smooth:
        shapes.append(jax.ShapeDtypeStruct((2, chunk_rows, TILE), BF16))
        outs.append(pl.BlockSpec((2, chunk_rows, TILE), lambda i: (0, 0, 0)))
    else:
        operands.append(before)
        specs.append(place)
        aliases = {len(operands): 0}
    return pl.pallas_call(
        functools.partial(finish_kernel, sky_count, line, jobs, with_smooth),
        out_shape=shapes,
        grid_spec=pltpu.PrefetchScalarGridSpec(
            num_scalar_prefetch=0,
            grid=(1,),
            in_specs=specs,
            out_specs=outs,
            scratch_shapes=scratch,
        ),
        input_output_aliases=aliases,
        cost_estimate=pl.CostEstimate(
            flops=count * chunk_rows * side, bytes_accessed=count * chunk_rows * side * 6, transcendentals=0
        ),
        compiler_params=pltpu.CompilerParams(vmem_limit_bytes=LATE_GRANT),
        name="finish",
    )(in_hbm(sky_columns), *operands)


def power_kernel(sky_count, line, band_count, sky_ref, across_ref, down_ref, *refs):
    sources = refs[: CHUNKS - 1]
    pieces = refs[CHUNKS - 1 : -band_count - 1]
    powers, smoothed = refs[-band_count - 1 : -1], refs[-1]
    part_rows = pieces[0].shape[0]
    pair = len(pieces) // line
    chunk_rows = part_rows * line
    side = pair * CHUNKS * chunk_rows
    rows = side // band_count
    smoothed[0:EDGE, :] = jnp.zeros((EDGE, TILE), BF16)
    smoothed[EDGE + side :, :] = jnp.zeros((EDGE, TILE), BF16)
    for half in range(pair):
        for chunk in range(CHUNKS - 1):
            first = EDGE + (half * CHUNKS + chunk) * chunk_rows
            smoothed[first : first + chunk_rows, :] = sources[chunk][half]

    def store(half, row, values):
        first = EDGE + (half * CHUNKS + CHUNKS - 1) * chunk_rows + row
        smoothed[pl.ds(pl.multiple_of(first, EDGE), part_rows), :] = values

    smooth_pieces(sky_count, line, across_ref[...], pieces, chunk_rows, store)
    for step in range(band_count):
        first = lax.rem(lax.axis_index("band") + step, band_count) * rows
        for inner in range(rows // TILE):
            source = pl.multiple_of(first + inner * TILE, TILE)
            filtered = jnp.dot(down_ref[...], smoothed[pl.ds(source, WINDOW), :], preferred_element_type=F32)
            powers[step][inner * TILE : (inner + 1) * TILE, :] = (filtered * filtered).astype(powers[step].dtype)


def power(sources, pieces, across_band, down_band, sky_columns, pair, sky_count, band_count):
    line = len(pieces) // pair
    side = CHUNKS * pair * line * pieces[0].shape[0]
    operands = [across_band, down_band, *sources, *pieces]
    return pl.pallas_call(
        functools.partial(power_kernel, sky_count, line, band_count),
        out_shape=[
            jax.ShapeDtypeStruct((side // band_count, TILE), BF16 if step else F32) for step in range(band_count)
        ],
        grid_spec=pltpu.PrefetchScalarGridSpec(
            num_scalar_prefetch=0,
            grid=(1,),
            in_specs=[SCALARS]
            + [pl.BlockSpec(array.shape, lambda i, n=array.ndim: (0,) * n) for array in operands],
            out_specs=[pl.BlockSpec((side // band_count, TILE), lambda i: (0, 0))] * band_count,
            scratch_shapes=[pltpu.VMEM((side + 2 * EDGE, TILE), BF16)],
        ),
        cost_estimate=pl.CostEstimate(flops=side * TILE * 600, bytes_accessed=side * TILE * 12, transcendentals=0),
        compiler_params=pltpu.CompilerParams(vmem_limit_bytes=LATE_GRANT),
        name="power",
    )(in_hbm(sky_columns), *operands)


def body(exposures, inv_variance, mask_planes, sky_columns, basis_rows, basis_cols, match_coeffs, detect_taps):
    picture = exposures[0, 0]
    side = picture.shape[0]
    sky_count = lax.axis_size("sky")
    band_count = lax.axis_size("band")
    own_sky = lax.axis_index("sky")
    pair = 2
    line = sky_count // pair
    half_rows = side // pair
    chunk_rows = half_rows // CHUNKS

    def exchange(block, bit):
        return lax.ppermute(block, "sky", [(i, i ^ (1 << bit)) for i in range(sky_count)])

    def reduce_line(terms):
        rows = chunk_rows
        bit = 1
        while 1 << bit < sky_count:
            rows = rows // 2
            mine = lax.rem(own_sky >> bit, 2)
            leaving = sum(lax.dynamic_slice_in_dim(t, (1 - mine) * rows, rows, -2).astype(F32) for t in terms)
            arrived = exchange(leaving.astype(BF16), bit)
            terms = [lax.dynamic_slice_in_dim(t, mine * rows, rows, -2) for t in terms] + [arrived]
            bit += 1
        return terms

    def total(terms):
        return sum(t.astype(F32) for t in terms)

    words = mask_planes[0, 0]
    variance = inv_variance[0, 0]

    def weighing(halves, chunk):
        return weigh(variance, words, sky_columns, halves, chunk, chunk_rows, sky_count)

    def matching(weight, which, half_slot, chunk):
        return match(
            picture, column_band, row_band, weight, which, sky_columns, half_slot, chunk, half_rows, sky_count
        )

    weight_other = weighing((OTHER,), 0)
    weight_in = exchange(weight_other[0], 0)
    weight_both = weighing((OTHER, OWN), 1)
    both_terms = reduce_line([weight_both])
    column_band, row_band, across_band, down_band = prepare(
        match_coeffs[0, 0], basis_cols, basis_rows, detect_taps
    )
    weight_own = weighing((OWN,), 0)

    away, product_in, home, product_own = ([None] * CHUNKS for _ in range(4))
    for c in range(CHUNKS):
        away[c], product = matching(weight_both if c else weight_other, 0, OTHER, c)
        product_in[c] = exchange(product, 0)
    for c in range(CHUNKS):
        home[c], product_own[c] = matching(weight_both if c else weight_own, c, OWN, c)
    both_in = exchange(total([t[0] for t in both_terms]).astype(BF16), 0)
    denoms = [
        total(reduce_line([weight_own[0], weight_in])),
        total([t[1] for t in both_terms] + [both_in]),
    ]

    gathered = []
    for c in range(CHUNKS):
        terms = reduce_line([product_own[c], product_in[c]])
        if c:
            terms[-1], _ = lax.optimization_barrier((terms[-1], block))
        numer = total(terms)
        block = (numer / jnp.maximum(denoms[c], 1.0)).astype(BF16)
        near, far = {0: block}, {}
        far[0] = exchange(block, 0)
        for bit in reversed(range(line.bit_length() - 1)):
            for held in list(near):
                step = held | 1 << bit
                near[step] = exchange(near[held], bit + 1)
        for step in range(1, line):
            far[step] = exchange(near[step], 0)
        gathered.append([[group[step] for step in range(line)] for group in (near, far)])

    (near_first, far_first), (near_last, far_last) = gathered
    early = ((OWN, 0), (OTHER, 0), (OWN, 1))
    difference, smoothed = finish(
        early, [home[0], away[0], home[1]], near_first + far_first + near_last, across_band, sky_columns, None, sky_count
    )
    powers = power(
        [smoothed], near_last + far_last, across_band, down_band, sky_columns, pair, sky_count, band_count
    )
    (difference,) = finish(((OTHER, 1),), [away[1]], far_last, across_band, sky_columns, difference, sky_count)
    detection = powers[0]
    for step in range(1, band_count):
        ring = [(i, (i + step) % band_count) for i in range(band_count)]
        detection = detection + lax.ppermute(powers[step], "band", ring).astype(F32)
    return (difference.reshape(1, 1, side, side), detection)


def solution(mesh):
    in_specs = (
        P("sky", "band", None, None),
        P("sky", "band", None, None),
        P("sky", "band", None, None),
        P(),
        P(),
        P(),
        P("sky", "band", None),
        P("band", None),
    )
    out_specs = (P("sky", "band", None, None), P("band", "sky"))

    return jax.shard_map(body, mesh=mesh, in_specs=in_specs, out_specs=out_specs, check_vma=False)
```

```python
import functools

import jax
import jax.numpy as jnp
from jax import lax
from jax.experimental import pallas as pl
from jax.experimental.pallas import tpu as pltpu
from jax.sharding import PartitionSpec as P


TILE = 128
NB = 9
TAPS = 25
DTAPS = 31
BITS = 30
EDGE = 16
WINDOW = TILE + 2 * EDGE
SHIFT = TILE // 2
CHUNKS = 2
OWN, OTHER = 0, 1
EARLY_GRANT = 20 << 20
LATE_GRANT = 24 << 20
SCALARS = pl.BlockSpec(memory_space=pltpu.SMEM)
F32 = jnp.float32
BF16 = jnp.bfloat16


def in_hbm(array):
    return pltpu.with_memory_space_constraint(array, pltpu.HBM)


def start_column(sky_ref):
    return sky_ref[lax.axis_index("sky"), lax.axis_index("band"), 0]


def half_of(which):
    low = lax.rem(lax.axis_index("sky"), 2)
    return low if which == OWN else 1 - low


def toeplitz(base_row, rows):
    wide = jnp.broadcast_to(base_row, (rows, base_row.shape[1]))
    return pltpu.roll(wide, 0, 1, stride=1, stride_axis=0)


def prepare_kernel(base_ref, column_ref, row_ref, across_ref, down_ref):
    for k in range(NB):
        column_ref[:, k * TILE : (k + 1) * TILE] = toeplitz(base_ref[k : k + 1, :], TILE).T.astype(BF16)
        row_ref[:, k * WINDOW : (k + 1) * WINDOW] = toeplitz(base_ref[NB + k : NB + k + 1, :], TILE)[
            :, :WINDOW
        ].astype(BF16)
    across_ref[...] = toeplitz(base_ref[2 * NB : 2 * NB + 1, :], TILE).T.astype(BF16)
    down_ref[...] = toeplitz(base_ref[2 * NB + 1 : 2 * NB + 2, :], TILE)[:, :WINDOW].astype(BF16)


def place_left(taps, offset):
    return jnp.pad(taps, ((0, 0), (offset, 2 * TILE - offset - taps.shape[1])))


def prepare(match_coeffs, basis_cols, basis_rows, detect_taps):
    column_taps = (match_coeffs[:, None] * basis_cols).astype(BF16).astype(F32)
    row_taps = basis_rows.astype(BF16).astype(F32)
    taps = detect_taps.astype(BF16).astype(F32)
    base = jnp.concatenate(
        [
            place_left(column_taps, SHIFT - TAPS // 2),
            place_left(row_taps, EDGE - TAPS // 2),
            place_left(taps, SHIFT - DTAPS // 2),
            place_left(taps, EDGE - DTAPS // 2),
        ],
        0,
    )
    return pl.pallas_call(
        prepare_kernel,
        out_shape=(
            jax.ShapeDtypeStruct((2 * TILE, NB * TILE), BF16),
            jax.ShapeDtypeStruct((TILE, NB * WINDOW), BF16),
            jax.ShapeDtypeStruct((2 * TILE, TILE), BF16),
            jax.ShapeDtypeStruct((TILE, WINDOW), BF16),
        ),
        compiler_params=pltpu.CompilerParams(vmem_limit_bytes=16 << 20),
        name="prepare",
    )(base)


def bad_bits(words_ref, plane, first_word, count, places):
    last = words_ref.shape[1] - 1
    word = jnp.full(places.shape, words_ref[plane, jnp.minimum(first_word, last)])
    begin = jnp.full(places.shape, first_word * BITS)
    for step in range(1, count):
        index = first_word + step
        reached = places >= index * BITS
        word = jnp.where(reached, words_ref[plane, jnp.minimum(index, last)], word)
        begin = jnp.where(reached, index * BITS, begin)
    return jnp.bitwise_and(jnp.right_shift(word, places - begin), 1)


def pick_block(index, halves, chunk, blocks):
    half = half_of(halves[0])
    for place in range(1, len(halves)):
        half = jnp.where(index >= place * blocks, half_of(halves[place]), half)
    return (half * CHUNKS + chunk) * blocks + lax.rem(index, blocks)


def weight_kernel(sky_count, halves, chunk, blocks, sky_ref, words_ref, variance_ref, weight_ref):
    rows, side = variance_ref.shape
    start = start_column(sky_ref)
    first_row = pick_block(pl.program_id(0), halves, chunk, blocks) * rows
    lanes = lax.broadcasted_iota(jnp.int32, (8, side), 1)
    column_bad = bad_bits(words_ref, 0, 0, words_ref.shape[1], lanes)[0:1, :]
    places = first_row + lax.broadcasted_iota(jnp.int32, (rows, TILE), 0)
    row_bad = bad_bits(words_ref, 1, first_row // BITS, rows // BITS + 2, places)
    if sky_count * TILE != side:
        weight_ref[...] = jnp.zeros_like(weight_ref)
    for tile in range(side // TILE):
        window = slice(tile * TILE, (tile + 1) * TILE)
        bad = row_bad + column_bad[:, window]
        kept = jnp.where(bad == 0, variance_ref[:, window].astype(F32), 0.0)
        target = lax.rem(start + tile, sky_count) * TILE
        weight_ref[0, :, pl.ds(pl.multiple_of(target, TILE), TILE)] = kept.astype(BF16)


def weigh(inv_variance, words, sky_columns, halves, chunk, chunk_rows, sky_count):
    side = inv_variance.shape[0]
    stripe = sky_count * TILE
    rows = min(TILE, chunk_rows)
    blocks = chunk_rows // rows
    return pl.pallas_call(
        functools.partial(weight_kernel, sky_count, halves, chunk, blocks),
        out_shape=jax.ShapeDtypeStruct((len(halves), chunk_rows, stripe), BF16),
        grid_spec=pltpu.PrefetchScalarGridSpec(
            num_scalar_prefetch=0,
            grid=(len(halves) * blocks,),
            in_specs=[SCALARS, SCALARS, pl.BlockSpec((rows, side), lambda i: (pick_block(i, halves, chunk, blocks), 0))],
            out_specs=pl.BlockSpec((1, rows, stripe), lambda i: (i // blocks, lax.rem(i, blocks), 0)),
        ),
        cost_estimate=pl.CostEstimate(
            flops=len(halves) * chunk_rows * side * 8,
            bytes_accessed=len(halves) * chunk_rows * side * 4,
            transcendentals=0,
        ),
        compiler_params=pltpu.CompilerParams(vmem_limit_bytes=EARLY_GRANT),
        name="weigh",
    )(in_hbm(sky_columns), in_hbm(words), in_hbm(inv_variance))


def match_kernel(
    sky_count,
    which,
    offset,
    half_blocks,
    sky_ref,
    above_ref,
    main_ref,
    below_ref,
    column_ref,
    row_ref,
    weight_ref,
    matched_ref,
    product_ref,
    windows,
    stacked,
):
    side = main_ref.shape[1]
    start = start_column(sky_ref)
    block = half_of(which) * half_blocks + offset + pl.program_id(0)
    last_block = side // TILE - 1
    nothing = jnp.zeros((TILE, SHIFT), BF16)

    def spread(values):
        edge = nothing[: values.shape[0]]
        return jnp.concatenate([edge, values, edge], axis=1)

    above, below = above_ref[...], below_ref[...]
    tiles = side // TILE
    parts = (
        (0, spread(jnp.where(block > 0, above, jnp.zeros_like(above)))),
        (EDGE, spread(main_ref[...])),
        (EDGE + TILE, spread(jnp.where(block < last_block, below, jnp.zeros_like(below)))),
    )
    for tile in range(tiles):
        for row, part in parts:
            row = tile * WINDOW + row
            windows[row : row + part.shape[0], :] = part[:, tile * TILE : (tile + 2) * TILE]
    for group in range(0, NB, 2):
        bands = range(group, min(group + 2, NB))
        passed = jnp.dot(
            windows[...], column_ref[:, group * TILE : (bands[-1] + 1) * TILE], preferred_element_type=F32
        ).astype(BF16)
        for k in bands:
            for tile in range(tiles):
                stacked[k * WINDOW : (k + 1) * WINDOW, tile * TILE : (tile + 1) * TILE] = passed[
                    tile * WINDOW : (tile + 1) * WINDOW, (k - group) * TILE : (k - group + 1) * TILE
                ]
    if sky_count != tiles:
        product_ref[...] = jnp.zeros_like(product_ref)
    for pair in range(tiles // 2):
        both = slice(pair * 2 * TILE, (pair + 1) * 2 * TILE)
        summed = jnp.dot(row_ref[...], stacked[:, both], preferred_element_type=F32).astype(BF16)
        matched_ref[:, both] = summed
        for part in range(2):
            target = pl.multiple_of(lax.rem(start + 2 * pair + part, sky_count) * TILE, TILE)
            weight = weight_ref[:, pl.ds(target, TILE)].astype(F32)
            product = weight * summed[:, part * TILE : (part + 1) * TILE].astype(F32)
            product_ref[:, pl.ds(target, TILE)] = product.astype(BF16)


def match(picture, column_band, row_band, weight, which_weight, sky_columns, which, chunk, half_rows, sky_count):
    side = picture.shape[0]
    chunk_rows = half_rows // CHUNKS
    steps = chunk_rows // TILE
    stripe = sky_count * TILE
    edges = TILE // EDGE

    def block(i):
        return (half_of(which) * CHUNKS + chunk) * steps + i

    return pl.pallas_call(
        functools.partial(match_kernel, sky_count, which, chunk * steps, CHUNKS * steps),
        out_shape=(
            pltpu.HBM((chunk_rows, side), BF16),
            pltpu.HBM((chunk_rows, stripe), BF16)
            if which == OTHER
            else jax.ShapeDtypeStruct((chunk_rows, stripe), BF16),
        ),
        grid_spec=pltpu.PrefetchScalarGridSpec(
            num_scalar_prefetch=0,
            grid=(steps,),
            in_specs=[
                SCALARS,
                pl.BlockSpec((EDGE, side), lambda i: (jnp.maximum(block(i) * edges - 1, 0), 0)),
                pl.BlockSpec((TILE, side), lambda i: (block(i), 0)),
                pl.BlockSpec((EDGE, side), lambda i: (jnp.minimum((block(i) + 1) * edges, side // EDGE - 1), 0)),
                pl.BlockSpec(column_band.shape, lambda i: (0, 0), pipeline_mode=pl.Buffered(1)),
                pl.BlockSpec(row_band.shape, lambda i: (0, 0), pipeline_mode=pl.Buffered(1)),
                pl.BlockSpec((None, TILE, stripe), lambda i: (which_weight, i, 0)),
            ],
            out_specs=(
                pl.BlockSpec((TILE, side), lambda i: (i, 0)),
                pl.BlockSpec((TILE, stripe), lambda i: (i, 0)),
            ),
            scratch_shapes=[
                pltpu.VMEM((side // TILE * WINDOW, 2 * TILE), BF16),
                pltpu.VMEM((NB * WINDOW, side), BF16),
            ],
        ),
        cost_estimate=pl.CostEstimate(
            flops=2 * chunk_rows * side * NB * (2 * TILE + WINDOW), bytes_accessed=chunk_rows * side * 8, transcendentals=0
        ),
        compiler_params=pltpu.CompilerParams(vmem_limit_bytes=EARLY_GRANT),
        name="match",
    )(in_hbm(sky_columns), *[in_hbm(picture)] * 3, column_band, row_band, weight)


def row_of(place, line, chunk_rows):
    row = 0
    for bit in range(line.bit_length() - 1):
        row = row + lax.rem(place >> bit, 2) * (chunk_rows >> (bit + 1))
    return row


def smooth_pieces(sky_count, line, across, pieces, chunk_rows, store):
    def column(piece, away):
        source = lax.rem(lax.axis_index("sky") + away, sky_count) * TILE
        return piece[:, pl.ds(pl.multiple_of(source, TILE), TILE)]

    for group in range(len(pieces) // line):
        for step in range(line):
            piece = pieces[group * line + step]
            window = jnp.concatenate(
                [column(piece, sky_count - 1)[:, SHIFT:], column(piece, 0), column(piece, 1)[:, :SHIFT]], axis=1
            )
            row = row_of(lax.axis_index("sky") // 2 ^ step, line, chunk_rows)
            store(half_of((OWN, OTHER)[group]), row, jnp.dot(window, across, preferred_element_type=F32).astype(BF16))


def finish_kernel(sky_count, line, jobs, with_smooth, sky_ref, *refs):
    count = len(jobs)
    if with_smooth:
        across_ref, refs = refs[0], refs[1:]
    matched, refs = refs[:count], refs[count:]
    pieces, refs = refs[: count * line], refs[count * line :]
    if not with_smooth:
        refs = refs[1:]
    out_ref, refs = refs[0], refs[1:]
    if with_smooth:
        smooth_ref, refs = refs[0], refs[1:]
    taken, ready, taken_sem, ready_sem = refs if with_smooth else (None, *refs[:1], None, *refs[1:])
    chunk_rows, side = matched[0].shape
    part_rows = pieces[0].shape[0]
    start = start_column(sky_ref)
    arriving = []
    if with_smooth:
        arriving = [
            pltpu.make_async_copy(matched[index], taken.at[index], taken_sem.at[index]) for index in range(count)
        ]
    for copy in arriving:
        copy.start()
    if with_smooth:

        def store(half, row, values):
            smooth_ref[half, pl.ds(pl.multiple_of(row, part_rows), part_rows), :] = values

        smooth_pieces(sky_count, line, across_ref[...], pieces[: 2 * line], chunk_rows, store)
    leaving = []
    for index, (which, chunk) in enumerate(jobs):
        source_ref = matched[index]
        if with_smooth:
            arriving[index].wait()
            source_ref = taken.at[index]
        for step in range(line):
            row = row_of(lax.axis_index("sky") // 2 ^ step, line, chunk_rows)
            rows = pl.ds(pl.multiple_of(row, part_rows), part_rows)
            piece = pieces[index * line + step]
            for tile in range(side // TILE):
                window = slice(tile * TILE, (tile + 1) * TILE)
                source = pl.multiple_of(lax.rem(start + tile, sky_count) * TILE, TILE)
                picked = piece[:, pl.ds(source, TILE)].astype(F32)
                ready[index, rows, window] = (source_ref[rows, window].astype(F32) - picked).astype(BF16)
        copy = pltpu.make_async_copy(ready.at[index], out_ref.at[half_of(which), chunk], ready_sem.at[index])
        copy.start()
        leaving.append(copy)
    for copy in leaving:
        copy.wait()


def finish(jobs, matched, pieces, across_band, sky_columns, before, sky_count):
    chunk_rows, side = matched[0].shape
    count = len(jobs)
    line = len(pieces) // count
    with_smooth = before is None
    place = pl.BlockSpec(memory_space=pl.ANY)
    operands = [*map(in_hbm, matched), *pieces]
    specs = [pl.BlockSpec(array.shape, lambda i: (0, 0)) for array in operands]
    scratch = [pltpu.VMEM((count, chunk_rows, side), BF16), pltpu.SemaphoreType.DMA((count,))]
    if with_smooth:
        operands = [across_band, *operands]
        specs = [pl.BlockSpec(across_band.shape, lambda i: (0, 0))] + [place] * count + specs[count:]
        scratch = [scratch[0], scratch[0], scratch[1], scratch[1]]
    specs = [SCALARS] + specs
    shapes = [pltpu.HBM((2, CHUNKS, chunk_rows, side), BF16)]
    outs = [place]
    aliases = {}
    if with_smooth:
        shapes.append(jax.ShapeDtypeStruct((2, chunk_rows, TILE), BF16))
        outs.append(pl.BlockSpec((2, chunk_rows, TILE), lambda i: (0, 0, 0)))
    else:
        operands.append(before)
        specs.append(place)
        aliases = {len(operands): 0}
    return pl.pallas_call(
        functools.partial(finish_kernel, sky_count, line, jobs, with_smooth),
        out_shape=shapes,
        grid_spec=pltpu.PrefetchScalarGridSpec(
            num_scalar_prefetch=0,
            grid=(1,),
            in_specs=specs,
            out_specs=outs,
            scratch_shapes=scratch,
        ),
        input_output_aliases=aliases,
        cost_estimate=pl.CostEstimate(
            flops=count * chunk_rows * side, bytes_accessed=count * chunk_rows * side * 6, transcendentals=0
        ),
        compiler_params=pltpu.CompilerParams(vmem_limit_bytes=LATE_GRANT),
        name="finish",
    )(in_hbm(sky_columns), *operands)


def power_kernel(sky_count, line, band_count, across_ref, down_ref, *refs):
    sources = refs[: CHUNKS - 1]
    pieces = refs[CHUNKS - 1 : -band_count - 1]
    powers, smoothed = refs[-band_count - 1 : -1], refs[-1]
    part_rows = pieces[0].shape[0]
    pair = len(pieces) // line
    chunk_rows = part_rows * line
    side = pair * CHUNKS * chunk_rows
    rows = side // band_count
    smoothed[0:EDGE, :] = jnp.zeros((EDGE, TILE), BF16)
    smoothed[EDGE + side :, :] = jnp.zeros((EDGE, TILE), BF16)
    for half in range(pair):
        for chunk in range(CHUNKS - 1):
            first = EDGE + (half * CHUNKS + chunk) * chunk_rows
            smoothed[first : first + chunk_rows, :] = sources[chunk][half]

    def store(half, row, values):
        first = EDGE + (half * CHUNKS + CHUNKS - 1) * chunk_rows + row
        smoothed[pl.ds(pl.multiple_of(first, EDGE), part_rows), :] = values

    smooth_pieces(sky_count, line, across_ref[...], pieces, chunk_rows, store)
    for step in range(band_count):
        first = lax.rem(lax.axis_index("band") + step, band_count) * rows
        for inner in range(rows // TILE):
            source = pl.multiple_of(first + inner * TILE, TILE)
            filtered = jnp.dot(down_ref[...], smoothed[pl.ds(source, WINDOW), :], preferred_element_type=F32)
            powers[step][inner * TILE : (inner + 1) * TILE, :] = (filtered * filtered).astype(powers[step].dtype)


def power(sources, pieces, across_band, down_band, pair, sky_count, band_count):
    line = len(pieces) // pair
    side = CHUNKS * pair * line * pieces[0].shape[0]
    operands = [across_band, down_band, *sources, *pieces]
    return pl.pallas_call(
        functools.partial(power_kernel, sky_count, line, band_count),
        out_shape=[
            jax.ShapeDtypeStruct((side // band_count, TILE), BF16 if step else F32) for step in range(band_count)
        ],
        grid_spec=pltpu.PrefetchScalarGridSpec(
            num_scalar_prefetch=0,
            grid=(1,),
            in_specs=[pl.BlockSpec(array.shape, lambda i, n=array.ndim: (0,) * n) for array in operands],
            out_specs=[pl.BlockSpec((side // band_count, TILE), lambda i: (0, 0))] * band_count,
            scratch_shapes=[pltpu.VMEM((side + 2 * EDGE, TILE), BF16)],
        ),
        cost_estimate=pl.CostEstimate(flops=side * TILE * 600, bytes_accessed=side * TILE * 12, transcendentals=0),
        compiler_params=pltpu.CompilerParams(vmem_limit_bytes=LATE_GRANT),
        name="power",
    )(*operands)


def body(exposures, inv_variance, mask_planes, sky_columns, basis_rows, basis_cols, match_coeffs, detect_taps):
    picture = exposures[0, 0]
    side = picture.shape[0]
    sky_count = lax.axis_size("sky")
    band_count = lax.axis_size("band")
    own_sky = lax.axis_index("sky")
    pair = 2
    line = sky_count // pair
    half_rows = side // pair
    chunk_rows = half_rows // CHUNKS

    def exchange(block, bit):
        return lax.ppermute(block, "sky", [(i, i ^ (1 << bit)) for i in range(sky_count)])

    def reduce_line(terms):
        rows = chunk_rows
        bit = 1
        while 1 << bit < sky_count:
            rows = rows // 2
            mine = lax.rem(own_sky >> bit, 2)
            leaving = sum(lax.dynamic_slice_in_dim(t, (1 - mine) * rows, rows, -2).astype(F32) for t in terms)
            arrived = exchange(leaving.astype(BF16), bit)
            terms = [lax.dynamic_slice_in_dim(t, mine * rows, rows, -2) for t in terms] + [arrived]
            bit += 1
        return terms

    def total(terms):
        return sum(t.astype(F32) for t in terms)

    words = mask_planes[0, 0]
    variance = inv_variance[0, 0]

    def weighing(halves, chunk):
        return weigh(variance, words, sky_columns, halves, chunk, chunk_rows, sky_count)

    def matching(weight, which, half_slot, chunk):
        return match(
            picture, column_band, row_band, weight, which, sky_columns, half_slot, chunk, half_rows, sky_count
        )

    weight_other = weighing((OTHER,), 0)
    weight_in = exchange(weight_other[0], 0)
    weight_both = weighing((OTHER, OWN), 1)
    both_terms = reduce_line([weight_both])
    column_band, row_band, across_band, down_band = prepare(
        match_coeffs[0, 0], basis_cols, basis_rows, detect_taps
    )
    weight_own = weighing((OWN,), 0)

    away, product_in, home, product_own = ([None] * CHUNKS for _ in range(4))
    for c in range(CHUNKS):
        away[c], product = matching(weight_both if c else weight_other, 0, OTHER, c)
        product_in[c] = exchange(product, 0)
    for c in range(CHUNKS):
        home[c], product_own[c] = matching(weight_both if c else weight_own, c, OWN, c)
    both_in = exchange(total([t[0] for t in both_terms]).astype(BF16), 0)
    denoms = [
        total(reduce_line([weight_own[0], weight_in])),
        total([t[1] for t in both_terms] + [both_in]),
    ]

    gathered = []
    for c in range(CHUNKS):
        terms = reduce_line([product_own[c], product_in[c]])
        if c:
            terms[-1], _ = lax.optimization_barrier((terms[-1], block))
        numer = total(terms)
        block = (numer / jnp.maximum(denoms[c], 1.0)).astype(BF16)
        near, far = {0: block}, {}
        far[0] = exchange(block, 0)
        for bit in reversed(range(line.bit_length() - 1)):
            for held in list(near):
                step = held | 1 << bit
                near[step] = exchange(near[held], bit + 1)
        for step in range(1, line):
            far[step] = exchange(near[step], 0)
        gathered.append([[group[step] for step in range(line)] for group in (near, far)])

    (near_first, far_first), (near_last, far_last) = gathered
    early = ((OWN, 0), (OTHER, 0), (OWN, 1))
    difference, smoothed = finish(
        early, [home[0], away[0], home[1]], near_first + far_first + near_last, across_band, sky_columns, None, sky_count
    )
    powers = power(
        [smoothed], near_last + far_last, across_band, down_band, pair, sky_count, band_count
    )
    (difference,) = finish(((OTHER, 1),), [away[1]], far_last, across_band, sky_columns, difference, sky_count)
    detection = powers[0]
    for step in range(1, band_count):
        ring = [(i, (i + step) % band_count) for i in range(band_count)]
        detection = detection + lax.ppermute(powers[step], "band", ring).astype(F32)
    return (difference.reshape(1, 1, side, side), detection)


def solution(mesh):
    in_specs = (
        P("sky", "band", None, None),
        P("sky", "band", None, None),
        P("sky", "band", None, None),
        P(),
        P(),
        P(),
        P("sky", "band", None),
        P("band", None),
    )
    out_specs = (P("sky", "band", None, None), P("band", "sky"))

    return jax.shard_map(body, mesh=mesh, in_specs=in_specs, out_specs=out_specs, check_vma=False)
```

```python
import functools

import jax
import jax.numpy as jnp
from jax import lax
from jax.experimental import pallas as pl
from jax.experimental.pallas import tpu as pltpu
from jax.sharding import PartitionSpec as P


TILE = 128
NB = 9
TAPS = 25
DTAPS = 31
BITS = 30
EDGE = 16
WINDOW = TILE + 2 * EDGE
SHIFT = TILE // 2
CHUNKS = 2
OWN, OTHER = 0, 1
EARLY_GRANT = 20 << 20
LATE_GRANT = 24 << 20
SCALARS = pl.BlockSpec(memory_space=pltpu.SMEM)
F32 = jnp.float32
BF16 = jnp.bfloat16


def in_hbm(array):
    if array.ndim == 1:
        return array
    return pltpu.with_memory_space_constraint(array, pltpu.HBM)


def start_column(sky_ref):
    if len(sky_ref.shape) == 1:
        return sky_ref[0]
    return sky_ref[lax.axis_index("sky"), lax.axis_index("band"), 0]


def half_of(which):
    low = lax.rem(lax.axis_index("sky"), 2)
    return low if which == OWN else 1 - low


def toeplitz(base_row, rows):
    wide = jnp.broadcast_to(base_row, (rows, base_row.shape[1]))
    return pltpu.roll(wide, 0, 1, stride=1, stride_axis=0)


def prepare_kernel(base_ref, column_ref, row_ref, across_ref, down_ref):
    for k in range(NB):
        column_ref[:, k * TILE : (k + 1) * TILE] = toeplitz(base_ref[k : k + 1, :], TILE).T.astype(BF16)
        row_ref[:, k * WINDOW : (k + 1) * WINDOW] = toeplitz(base_ref[NB + k : NB + k + 1, :], TILE)[
            :, :WINDOW
        ].astype(BF16)
    across_ref[...] = toeplitz(base_ref[2 * NB : 2 * NB + 1, :], TILE).T.astype(BF16)
    down_ref[...] = toeplitz(base_ref[2 * NB + 1 : 2 * NB + 2, :], TILE)[:, :WINDOW].astype(BF16)


def place_left(taps, offset):
    return jnp.pad(taps, ((0, 0), (offset, 2 * TILE - offset - taps.shape[1])))


def prepare(match_coeffs, basis_cols, basis_rows, detect_taps):
    column_taps = (match_coeffs[:, None] * basis_cols).astype(BF16).astype(F32)
    row_taps = basis_rows.astype(BF16).astype(F32)
    taps = detect_taps.astype(BF16).astype(F32)
    base = jnp.concatenate(
        [
            place_left(column_taps, SHIFT - TAPS // 2),
            place_left(row_taps, EDGE - TAPS // 2),
            place_left(taps, SHIFT - DTAPS // 2),
            place_left(taps, EDGE - DTAPS // 2),
        ],
        0,
    )
    return pl.pallas_call(
        prepare_kernel,
        out_shape=(
            jax.ShapeDtypeStruct((2 * TILE, NB * TILE), BF16),
            jax.ShapeDtypeStruct((TILE, NB * WINDOW), BF16),
            jax.ShapeDtypeStruct((2 * TILE, TILE), BF16),
            jax.ShapeDtypeStruct((TILE, WINDOW), BF16),
        ),
        compiler_params=pltpu.CompilerParams(vmem_limit_bytes=16 << 20),
        name="prepare",
    )(base)


def bad_bits(words_ref, plane, first_word, count, places):
    last = words_ref.shape[1] - 1
    word = jnp.full(places.shape, words_ref[plane, jnp.minimum(first_word, last)])
    begin = jnp.full(places.shape, first_word * BITS)
    for step in range(1, count):
        index = first_word + step
        reached = places >= index * BITS
        word = jnp.where(reached, words_ref[plane, jnp.minimum(index, last)], word)
        begin = jnp.where(reached, index * BITS, begin)
    return jnp.bitwise_and(jnp.right_shift(word, places - begin), 1)


def pick_block(index, halves, chunk, blocks):
    half = half_of(halves[0])
    for place in range(1, len(halves)):
        half = jnp.where(index >= place * blocks, half_of(halves[place]), half)
    return (half * CHUNKS + chunk) * blocks + lax.rem(index, blocks)


def weight_kernel(sky_count, halves, chunk, blocks, sky_ref, words_ref, variance_ref, weight_ref):
    rows, side = variance_ref.shape
    start = start_column(sky_ref)
    first_row = pick_block(pl.program_id(0), halves, chunk, blocks) * rows
    lanes = lax.broadcasted_iota(jnp.int32, (8, side), 1)
    column_bad = bad_bits(words_ref, 0, 0, words_ref.shape[1], lanes)[0:1, :]
    places = first_row + lax.broadcasted_iota(jnp.int32, (rows, TILE), 0)
    row_bad = bad_bits(words_ref, 1, first_row // BITS, rows // BITS + 2, places)
    if sky_count * TILE != side:
        weight_ref[...] = jnp.zeros_like(weight_ref)
    for tile in range(side // TILE):
        window = slice(tile * TILE, (tile + 1) * TILE)
        bad = row_bad + column_bad[:, window]
        kept = jnp.where(bad == 0, variance_ref[:, window].astype(F32), 0.0)
        target = lax.rem(start + tile, sky_count) * TILE
        weight_ref[0, :, pl.ds(pl.multiple_of(target, TILE), TILE)] = kept.astype(BF16)


def weigh(inv_variance, words, sky_columns, halves, chunk, chunk_rows, sky_count):
    side = inv_variance.shape[0]
    stripe = sky_count * TILE
    rows = min(TILE, chunk_rows)
    blocks = chunk_rows // rows
    return pl.pallas_call(
        functools.partial(weight_kernel, sky_count, halves, chunk, blocks),
        out_shape=jax.ShapeDtypeStruct((len(halves), chunk_rows, stripe), BF16),
        grid_spec=pltpu.PrefetchScalarGridSpec(
            num_scalar_prefetch=0,
            grid=(len(halves) * blocks,),
            in_specs=[SCALARS, SCALARS, pl.BlockSpec((rows, side), lambda i: (pick_block(i, halves, chunk, blocks), 0))],
            out_specs=pl.BlockSpec((1, rows, stripe), lambda i: (i // blocks, lax.rem(i, blocks), 0)),
        ),
        cost_estimate=pl.CostEstimate(
            flops=len(halves) * chunk_rows * side * 8,
            bytes_accessed=len(halves) * chunk_rows * side * 4,
            transcendentals=0,
        ),
        compiler_params=pltpu.CompilerParams(vmem_limit_bytes=EARLY_GRANT),
        name="weigh",
    )(in_hbm(sky_columns), in_hbm(words), in_hbm(inv_variance))


def match_kernel(
    sky_count,
    which,
    offset,
    half_blocks,
    sky_ref,
    above_ref,
    main_ref,
    below_ref,
    column_ref,
    row_ref,
    weight_ref,
    matched_ref,
    product_ref,
    windows,
    stacked,
):
    side = main_ref.shape[1]
    start = start_column(sky_ref)
    block = half_of(which) * half_blocks + offset + pl.program_id(0)
    last_block = side // TILE - 1
    nothing = jnp.zeros((TILE, SHIFT), BF16)

    def spread(values):
        edge = nothing[: values.shape[0]]
        return jnp.concatenate([edge, values, edge], axis=1)

    above, below = above_ref[...], below_ref[...]
    tiles = side // TILE
    parts = (
        (0, spread(jnp.where(block > 0, above, jnp.zeros_like(above)))),
        (EDGE, spread(main_ref[...])),
        (EDGE + TILE, spread(jnp.where(block < last_block, below, jnp.zeros_like(below)))),
    )
    for tile in range(tiles):
        for row, part in parts:
            row = tile * WINDOW + row
            windows[row : row + part.shape[0], :] = part[:, tile * TILE : (tile + 2) * TILE]
    for group in range(0, NB, 2):
        bands = range(group, min(group + 2, NB))
        passed = jnp.dot(
            windows[...], column_ref[:, group * TILE : (bands[-1] + 1) * TILE], preferred_element_type=F32
        ).astype(BF16)
        for k in bands:
            for tile in range(tiles):
                stacked[k * WINDOW : (k + 1) * WINDOW, tile * TILE : (tile + 1) * TILE] = passed[
                    tile * WINDOW : (tile + 1) * WINDOW, (k - group) * TILE : (k - group + 1) * TILE
                ]
    if sky_count != tiles:
        product_ref[...] = jnp.zeros_like(product_ref)
    for pair in range(tiles // 2):
        both = slice(pair * 2 * TILE, (pair + 1) * 2 * TILE)
        summed = jnp.dot(row_ref[...], stacked[:, both], preferred_element_type=F32).astype(BF16)
        matched_ref[:, both] = summed
        for part in range(2):
            target = pl.multiple_of(lax.rem(start + 2 * pair + part, sky_count) * TILE, TILE)
            weight = weight_ref[:, pl.ds(target, TILE)].astype(F32)
            product = weight * summed[:, part * TILE : (part + 1) * TILE].astype(F32)
            product_ref[:, pl.ds(target, TILE)] = product.astype(BF16)


def match(picture, column_band, row_band, weight, which_weight, sky_columns, which, chunk, half_rows, sky_count):
    side = picture.shape[0]
    chunk_rows = half_rows // CHUNKS
    steps = chunk_rows // TILE
    stripe = sky_count * TILE
    edges = TILE // EDGE

    def block(i):
        return (half_of(which) * CHUNKS + chunk) * steps + i

    return pl.pallas_call(
        functools.partial(match_kernel, sky_count, which, chunk * steps, CHUNKS * steps),
        out_shape=(
            pltpu.HBM((chunk_rows, side), BF16),
            pltpu.HBM((chunk_rows, stripe), BF16)
            if which == OTHER
            else jax.ShapeDtypeStruct((chunk_rows, stripe), BF16),
        ),
        grid_spec=pltpu.PrefetchScalarGridSpec(
            num_scalar_prefetch=0,
            grid=(steps,),
            in_specs=[
                SCALARS,
                pl.BlockSpec((EDGE, side), lambda i: (jnp.maximum(block(i) * edges - 1, 0), 0)),
                pl.BlockSpec((TILE, side), lambda i: (block(i), 0)),
                pl.BlockSpec((EDGE, side), lambda i: (jnp.minimum((block(i) + 1) * edges, side // EDGE - 1), 0)),
                pl.BlockSpec(column_band.shape, lambda i: (0, 0), pipeline_mode=pl.Buffered(1)),
                pl.BlockSpec(row_band.shape, lambda i: (0, 0), pipeline_mode=pl.Buffered(1)),
                pl.BlockSpec((None, TILE, stripe), lambda i: (which_weight, i, 0)),
            ],
            out_specs=(
                pl.BlockSpec((TILE, side), lambda i: (i, 0)),
                pl.BlockSpec((TILE, stripe), lambda i: (i, 0)),
            ),
            scratch_shapes=[
                pltpu.VMEM((side // TILE * WINDOW, 2 * TILE), BF16),
                pltpu.VMEM((NB * WINDOW, side), BF16),
            ],
        ),
        cost_estimate=pl.CostEstimate(
            flops=2 * chunk_rows * side * NB * (2 * TILE + WINDOW), bytes_accessed=chunk_rows * side * 8, transcendentals=0
        ),
        compiler_params=pltpu.CompilerParams(vmem_limit_bytes=EARLY_GRANT),
        name="match",
    )(in_hbm(sky_columns), *[in_hbm(picture)] * 3, column_band, row_band, weight)


def row_of(place, line, chunk_rows):
    row = 0
    for bit in range(line.bit_length() - 1):
        row = row + lax.rem(place >> bit, 2) * (chunk_rows >> (bit + 1))
    return row


def smooth_pieces(sky_count, line, across, pieces, chunk_rows, store):
    def column(piece, away):
        source = lax.rem(lax.axis_index("sky") + away, sky_count) * TILE
        return piece[:, pl.ds(pl.multiple_of(source, TILE), TILE)]

    for group in range(len(pieces) // line):
        for step in range(line):
            piece = pieces[group * line + step]
            window = jnp.concatenate(
                [column(piece, sky_count - 1)[:, SHIFT:], column(piece, 0), column(piece, 1)[:, :SHIFT]], axis=1
            )
            row = row_of(lax.axis_index("sky") // 2 ^ step, line, chunk_rows)
            store(half_of((OWN, OTHER)[group]), row, jnp.dot(window, across, preferred_element_type=F32).astype(BF16))


def finish_kernel(sky_count, line, jobs, with_smooth, sky_ref, *refs):
    count = len(jobs)
    if with_smooth:
        across_ref, refs = refs[0], refs[1:]
    matched, refs = refs[:count], refs[count:]
    pieces, refs = refs[: count * line], refs[count * line :]
    if not with_smooth:
        refs = refs[1:]
    out_ref, refs = refs[0], refs[1:]
    if with_smooth:
        smooth_ref, refs = refs[0], refs[1:]
    taken, ready, taken_sem, ready_sem = refs if with_smooth else (None, *refs[:1], None, *refs[1:])
    chunk_rows, side = matched[0].shape
    part_rows = pieces[0].shape[0]
    start = start_column(sky_ref)
    arriving = []
    if with_smooth:
        arriving = [
            pltpu.make_async_copy(matched[index], taken.at[index], taken_sem.at[index]) for index in range(count)
        ]
    for copy in arriving:
        copy.start()
    if with_smooth:

        def store(half, row, values):
            smooth_ref[half, pl.ds(pl.multiple_of(row, part_rows), part_rows), :] = values

        smooth_pieces(sky_count, line, across_ref[...], pieces[: 2 * line], chunk_rows, store)
    leaving = []
    for index, (which, chunk) in enumerate(jobs):
        source_ref = matched[index]
        if with_smooth:
            arriving[index].wait()
            source_ref = taken.at[index]
        for step in range(line):
            row = row_of(lax.axis_index("sky") // 2 ^ step, line, chunk_rows)
            rows = pl.ds(pl.multiple_of(row, part_rows), part_rows)
            piece = pieces[index * line + step]
            for tile in range(side // TILE):
                window = slice(tile * TILE, (tile + 1) * TILE)
                source = pl.multiple_of(lax.rem(start + tile, sky_count) * TILE, TILE)
                picked = piece[:, pl.ds(source, TILE)].astype(F32)
                ready[index, rows, window] = (source_ref[rows, window].astype(F32) - picked).astype(BF16)
        copy = pltpu.make_async_copy(ready.at[index], out_ref.at[half_of(which), chunk], ready_sem.at[index])
        copy.start()
        leaving.append(copy)
    for copy in leaving:
        copy.wait()


def finish(jobs, matched, pieces, across_band, sky_columns, before, sky_count):
    chunk_rows, side = matched[0].shape
    count = len(jobs)
    line = len(pieces) // count
    with_smooth = before is None
    place = pl.BlockSpec(memory_space=pl.ANY)
    operands = [*map(in_hbm, matched), *pieces]
    specs = [pl.BlockSpec(array.shape, lambda i: (0, 0)) for array in operands]
    scratch = [pltpu.VMEM((count, chunk_rows, side), BF16), pltpu.SemaphoreType.DMA((count,))]
    if with_smooth:
        operands = [across_band, *operands]
        specs = [pl.BlockSpec(across_band.shape, lambda i: (0, 0))] + [place] * count + specs[count:]
        scratch = [scratch[0], scratch[0], scratch[1], scratch[1]]
    specs = [SCALARS] + specs
    shapes = [pltpu.HBM((2, CHUNKS, chunk_rows, side), BF16)]
    outs = [place]
    aliases = {}
    if with_smooth:
        shapes.append(jax.ShapeDtypeStruct((2, chunk_rows, TILE), BF16))
        outs.append(pl.BlockSpec((2, chunk_rows, TILE), lambda i: (0, 0, 0)))
    else:
        operands.append(before)
        specs.append(place)
        aliases = {len(operands): 0}
    return pl.pallas_call(
        functools.partial(finish_kernel, sky_count, line, jobs, with_smooth),
        out_shape=shapes,
        grid_spec=pltpu.PrefetchScalarGridSpec(
            num_scalar_prefetch=0,
            grid=(1,),
            in_specs=specs,
            out_specs=outs,
            scratch_shapes=scratch,
        ),
        input_output_aliases=aliases,
        cost_estimate=pl.CostEstimate(
            flops=count * chunk_rows * side, bytes_accessed=count * chunk_rows * side * 6, transcendentals=0
        ),
        compiler_params=pltpu.CompilerParams(vmem_limit_bytes=LATE_GRANT),
        name="finish",
    )(in_hbm(sky_columns), *operands)


def power_kernel(sky_count, line, band_count, across_ref, down_ref, *refs):
    sources = refs[: CHUNKS - 1]
    pieces = refs[CHUNKS - 1 : -band_count - 1]
    powers, smoothed = refs[-band_count - 1 : -1], refs[-1]
    part_rows = pieces[0].shape[0]
    pair = len(pieces) // line
    chunk_rows = part_rows * line
    side = pair * CHUNKS * chunk_rows
    rows = side // band_count
    smoothed[0:EDGE, :] = jnp.zeros((EDGE, TILE), BF16)
    smoothed[EDGE + side :, :] = jnp.zeros((EDGE, TILE), BF16)
    for half in range(pair):
        for chunk in range(CHUNKS - 1):
            first = EDGE + (half * CHUNKS + chunk) * chunk_rows
            smoothed[first : first + chunk_rows, :] = sources[chunk][half]

    def store(half, row, values):
        first = EDGE + (half * CHUNKS + CHUNKS - 1) * chunk_rows + row
        smoothed[pl.ds(pl.multiple_of(first, EDGE), part_rows), :] = values

    smooth_pieces(sky_count, line, across_ref[...], pieces, chunk_rows, store)
    for step in range(band_count):
        first = lax.rem(lax.axis_index("band") + step, band_count) * rows
        for inner in range(rows // TILE):
            source = pl.multiple_of(first + inner * TILE, TILE)
            filtered = jnp.dot(down_ref[...], smoothed[pl.ds(source, WINDOW), :], preferred_element_type=F32)
            powers[step][inner * TILE : (inner + 1) * TILE, :] = (filtered * filtered).astype(powers[step].dtype)


def power(sources, pieces, across_band, down_band, pair, sky_count, band_count):
    line = len(pieces) // pair
    side = CHUNKS * pair * line * pieces[0].shape[0]
    operands = [across_band, down_band, *sources, *pieces]
    return pl.pallas_call(
        functools.partial(power_kernel, sky_count, line, band_count),
        out_shape=[
            jax.ShapeDtypeStruct((side // band_count, TILE), BF16 if step else F32) for step in range(band_count)
        ],
        grid_spec=pltpu.PrefetchScalarGridSpec(
            num_scalar_prefetch=0,
            grid=(1,),
            in_specs=[pl.BlockSpec(array.shape, lambda i, n=array.ndim: (0,) * n) for array in operands],
            out_specs=[pl.BlockSpec((side // band_count, TILE), lambda i: (0, 0))] * band_count,
            scratch_shapes=[pltpu.VMEM((side + 2 * EDGE, TILE), BF16)],
        ),
        cost_estimate=pl.CostEstimate(flops=side * TILE * 600, bytes_accessed=side * TILE * 12, transcendentals=0),
        compiler_params=pltpu.CompilerParams(vmem_limit_bytes=LATE_GRANT),
        name="power",
    )(*operands)


def body(exposures, inv_variance, mask_planes, sky_columns, basis_rows, basis_cols, match_coeffs, detect_taps):
    picture = exposures[0, 0]
    side = picture.shape[0]
    sky_count = lax.axis_size("sky")
    band_count = lax.axis_size("band")
    own_sky = lax.axis_index("sky")
    pair = 2
    line = sky_count // pair
    half_rows = side // pair
    chunk_rows = half_rows // CHUNKS

    def exchange(block, bit):
        return lax.ppermute(block, "sky", [(i, i ^ (1 << bit)) for i in range(sky_count)])

    def reduce_line(terms):
        rows = chunk_rows
        bit = 1
        while 1 << bit < sky_count:
            rows = rows // 2
            mine = lax.rem(own_sky >> bit, 2)
            leaving = sum(lax.dynamic_slice_in_dim(t, (1 - mine) * rows, rows, -2).astype(F32) for t in terms)
            arrived = exchange(leaving.astype(BF16), bit)
            terms = [lax.dynamic_slice_in_dim(t, mine * rows, rows, -2) for t in terms] + [arrived]
            bit += 1
        return terms

    def total(terms):
        return sum(t.astype(F32) for t in terms)

    words = mask_planes[0, 0]
    variance = inv_variance[0, 0]

    own_row = sky_columns[own_sky, lax.axis_index("band")]

    def weighing(halves, chunk, places=own_row):
        return weigh(variance, words, places, halves, chunk, chunk_rows, sky_count)

    def matching(weight, which, half_slot, chunk):
        return match(
            picture, column_band, row_band, weight, which, own_row, half_slot, chunk, half_rows, sky_count
        )

    weight_other = weighing((OTHER,), 0, sky_columns)
    weight_in = exchange(weight_other[0], 0)
    weight_both = weighing((OTHER, OWN), 1)
    both_terms = reduce_line([weight_both])
    column_band, row_band, across_band, down_band = prepare(
        match_coeffs[0, 0], basis_cols, basis_rows, detect_taps
    )
    weight_own = weighing((OWN,), 0)

    away, product_in, home, product_own = ([None] * CHUNKS for _ in range(4))
    for c in range(CHUNKS):
        away[c], product = matching(weight_both if c else weight_other, 0, OTHER, c)
        product_in[c] = exchange(product, 0)
    for c in range(CHUNKS):
        home[c], product_own[c] = matching(weight_both if c else weight_own, c, OWN, c)
    both_in = exchange(total([t[0] for t in both_terms]).astype(BF16), 0)
    denoms = [
        total(reduce_line([weight_own[0], weight_in])),
        total([t[1] for t in both_terms] + [both_in]),
    ]

    gathered = []
    for c in range(CHUNKS):
        terms = reduce_line([product_own[c], product_in[c]])
        if c:
            terms[-1], _ = lax.optimization_barrier((terms[-1], block))
        numer = total(terms)
        block = (numer / jnp.maximum(denoms[c], 1.0)).astype(BF16)
        near, far = {0: block}, {}
        far[0] = exchange(block, 0)
        for bit in reversed(range(line.bit_length() - 1)):
            for held in list(near):
                step = held | 1 << bit
                near[step] = exchange(near[held], bit + 1)
        for step in range(1, line):
            far[step] = exchange(near[step], 0)
        gathered.append([[group[step] for step in range(line)] for group in (near, far)])

    (near_first, far_first), (near_last, far_last) = gathered
    early = ((OWN, 0), (OTHER, 0), (OWN, 1))
    difference, smoothed = finish(
        early, [home[0], away[0], home[1]], near_first + far_first + near_last, across_band, own_row, None, sky_count
    )
    powers = power(
        [smoothed], near_last + far_last, across_band, down_band, pair, sky_count, band_count
    )
    (difference,) = finish(((OTHER, 1),), [away[1]], far_last, across_band, own_row, difference, sky_count)
    detection = powers[0]
    for step in range(1, band_count):
        ring = [(i, (i + step) % band_count) for i in range(band_count)]
        detection = detection + lax.ppermute(powers[step], "band", ring).astype(F32)
    return (difference.reshape(1, 1, side, side), detection)


def solution(mesh):
    in_specs = (
        P("sky", "band", None, None),
        P("sky", "band", None, None),
        P("sky", "band", None, None),
        P(),
        P(),
        P(),
        P("sky", "band", None),
        P("band", None),
    )
    out_specs = (P("sky", "band", None, None), P("band", "sky"))

    return jax.shard_map(body, mesh=mesh, in_specs=in_specs, out_specs=out_specs, check_vma=False)
```
